32 devices in a mesh: seq: 8 (over z, core), head: 4 (over y, x).
Axes of the slice: x: 2, y: 2, z: 4, core: 2. Of those that a mesh axis runs over, the one named last changes fastest.
Arguments:
- tokens: bfloat16 [4096, 2304], P(('seq', 'head')), may hold values from -6 to 6
- in_gain: float32 [2304], replicated, may hold values from 0.5 to 1.5
- out_gain: float32 [2304], replicated, may hold values from 0.5 to 1.5
- query_weight: bfloat16 [2304, 2048], P(None, 'head'), may hold values from -1.25 to 1.25
- keyval_weight: bfloat16 [2304, 2048], replicated, may hold values from -0.125 to 0.125
- out_weight: bfloat16 [2048, 2304], P('head'), may hold values from -0.125 to 0.125
- cache_entries: bfloat16 [4, 2048, 512], P(None, 'seq'), may hold values from -6 to 6
- segment_ids: int32 [4096], P('seq'), may hold values from -1 to 63, as said below
- cache_lengths: int32 [64], replicated, may hold values from 0 to 512, as said below
- block_owners: int32 [128], P('seq'), may hold values from -1 to 63, as said below
Outputs:
- layer_out: bfloat16 [4096, 2304], P(('seq', 'head'))
The draws below stay inside these ranges and needn't reach their ends.
Inputs may be any that keep to these rules, and one draw needn't show every extreme that they name: `segment_ids`: valid slots come first and their ids never fall; every id from 0 to 63 has at least one slot; padding slots, marked -1, fill the end of the stream; exactly one segment has 2048 slots and none has more. `block_owners`: the segment that owns each cache block, or -1 for a free block; a segment's cache fills its blocks in the order of their indices; no segment owns more than 32 blocks. `cache_lengths`: zero for a segment without blocks, and some segment has none; otherwise more than 16 times one less than its number of blocks and at most 16 times that number; exactly one segment holds 512 rows.
All inputs are finite; a program needn't handle non-finite values.
Results may differ from the reference program's by a relative error of at most 0.012.
Values may be sent and summed in bfloat16 or wider, within the bound.
A program may use at most 128 MiB of HBM per device.

```python
import math
import jax
import jax.numpy as jnp
from jax import lax

D = 2304
QH = 8
KVH = 4
HD = 256
NSEG = 64
BLK = 16
TOKENS = 4096
CACHE_ROWS = 2048
CBLK = 128
MAXSEG = 2048


def segment_plan(key):
    pad_key, long_key, weight_key = jax.random.split(key, 3)
    padding = jax.random.randint(pad_key, (), 0, TOKENS // 16 + 1)
    longest = jax.random.randint(long_key, (), 0, NSEG)
    seg_range = jnp.arange(NSEG, dtype=jnp.int32)
    weights = jax.random.randint(weight_key, (NSEG,), 1, 100)
    weights = jnp.where(seg_range == longest, 0, weights)
    remainder = TOKENS - padding - MAXSEG - (NSEG - 1)
    surplus = remainder * weights // jnp.sum(weights)
    leftover = remainder - jnp.sum(surplus)
    receiver = (longest + 1) % NSEG
    lengths = jnp.where(seg_range == longest, MAXSEG, 1 + surplus + jnp.where(seg_range == receiver, leftover, 0))
    return (lengths.astype(jnp.int32), padding)


def draw_segment_ids(key, part):
    lengths, padding = segment_plan(jax.random.fold_in(key, 11))
    boundaries = jnp.cumsum(lengths)
    slot_index = jnp.arange(TOKENS, dtype=jnp.int32)
    labels = jnp.sum((slot_index[:, None] >= boundaries[None, :]).astype(jnp.int32), axis=1)
    return jnp.where(slot_index < TOKENS - padding, labels, -1).astype(jnp.int32)


def cache_plan(key):
    perm_key, heavy_key, empty_key, free_key, fill_key = jax.random.split(jax.random.fold_in(key, 23), 5)
    without = jax.random.randint(empty_key, (), 0, NSEG)
    heavy = (without + 1 + jax.random.randint(heavy_key, (), 0, NSEG - 1)) % NSEG
    block_index = jnp.arange(CBLK, dtype=jnp.int32)
    group = block_index // 4
    within = block_index % 4
    cycle = (3 * group + within - 1) % NSEG
    order = jax.random.permutation(perm_key, NSEG).astype(jnp.int32)
    owners = jnp.take(order, cycle)
    freed = jax.random.randint(free_key, (CBLK,), 0, 4) == 0
    owners = jnp.where(freed | (owners == heavy) | (owners == without), -1, owners)
    owners = jnp.where(within == 0, heavy, owners)
    seg_range = jnp.arange(NSEG, dtype=jnp.int32)
    owned_count = jnp.sum((owners[:, None] == seg_range[None, :]).astype(jnp.int32), axis=0)
    partial_value = jax.random.randint(fill_key, (NSEG,), 1, BLK + 1)
    partial_value = jnp.where(seg_range == heavy, BLK, partial_value)
    lengths = jnp.where(owned_count > 0, BLK * (owned_count - 1) + partial_value, 0)
    return (owners.astype(jnp.int32), lengths.astype(jnp.int32))


def draw_block_owners(key, part):
    owners, lengths = cache_plan(key)
    return owners


def draw_cache_lengths(key, part):
    owners, lengths = cache_plan(key)
    return lengths


def levels(rng, shape, cuts, least, largest):
    gain = 1.0
    for dim, shards_of in cuts:
        draws = jax.random.uniform(jax.random.fold_in(jax.random.fold_in(rng, 6), dim), (shards_of,), jnp.float32, least / len(cuts), largest / len(cuts))
        gain = gain * jnp.repeat(jnp.exp(draws), shape[dim] // shards_of).reshape((-1,) + (1,) * (len(shape) - 1 - dim))
    return gain


def noise(own_key, shape, scale, bound, shards=(), kind=jnp.bfloat16):
    array = jax.random.normal(own_key, shape, jnp.float32) * scale
    if len(shards) > 0:
        array = levels(own_key, shape, shards, -0.22, 0.18) * array
    return jnp.clip(array, min=-bound, max=bound).astype(kind)


def setup_inputs(seed: int = 0) -> dict:
    seeds = jax.random.split(jax.random.key(seed), 11)
    tokens = noise(seeds[0], (TOKENS, D), 1.0, 6.0, ((0, 32),))
    in_gain = jnp.clip(1.0 + 0.1 * jax.random.normal(seeds[1], (D,), jnp.float32), 0.5, 1.5)
    out_gain = jnp.clip(1.0 + 0.1 * jax.random.normal(seeds[2], (D,), jnp.float32), 0.5, 1.5)
    query_weight = noise(seeds[3], (D, QH * HD), (max(D // 100, 1)) ** -0.5, 1.25, ((1, 4),))
    keyval_weight = noise(seeds[4], (D, KVH * 2 * HD), D ** -0.5, 0.125)
    out_weight = noise(seeds[5], (QH * HD, D), (QH * HD) ** -0.5, 0.125, ((0, 4),))
    cache_entries = noise(seeds[6], (KVH, CACHE_ROWS, 2 * HD), 1.0, 6.0, ((1, 8),))
    segment_ids = draw_segment_ids(jax.random.fold_in(seeds[10], 71), 0)
    cache_lengths = draw_cache_lengths(jax.random.fold_in(seeds[10], 71), 0)
    block_owners = draw_block_owners(jax.random.fold_in(seeds[10], 71), 0)
    return dict(tokens=tokens, in_gain=in_gain, out_gain=out_gain, query_weight=query_weight, keyval_weight=keyval_weight, out_weight=out_weight, cache_entries=cache_entries, segment_ids=segment_ids, cache_lengths=cache_lengths, block_owners=block_owners)


EPSILON = 1e-06
SOFT_CAP = 50.0
far_away = 1073741824

def rms_scale(matrix, scaling):
    matrix = matrix.astype(jnp.float32)
    mean_square = lax.optimization_barrier(jnp.mean(matrix * matrix, axis=-1, keepdims=True))
    return matrix * lax.rsqrt(mean_square + EPSILON) * scaling.astype(jnp.float32)

def frequencies(extent):
    return 10000.0 ** (-(jnp.arange(extent // 2, dtype=jnp.float32) * 2.0 / extent))

def rotate(vectors, angles):
    half_width = vectors.shape[-1] // 2
    leading = vectors[..., :half_width]
    trailing = vectors[..., half_width:]
    cosine = jnp.cos(angles)
    sine_part = jnp.sin(angles)
    return jnp.concatenate([leading * cosine - trailing * sine_part, trailing * cosine + leading * sine_part], axis=-1)

def attend(queries, q_seg, q_slot, key_table, value_table, k_seg, k_slot):
    q_total, head_count, extent = queries.shape
    q_rows = math.gcd(q_total, 1024)
    k_rows = math.gcd(key_table.shape[0], 1024)
    key_blocks = (key_table.reshape(-1, k_rows, extent), value_table.reshape(-1, k_rows, extent), k_seg.reshape(-1, k_rows), k_slot.reshape(-1, k_rows))

    def one_block(query_block):
        query_rows, query_seg, query_slot = query_block
        present = query_seg >= 0
        lowest = jnp.min(jnp.where(present, query_seg, far_away))
        highest = jnp.max(query_seg)
        latest = jnp.max(query_slot)

        def advance(totals, key_block):
            key_rows, value_rows, key_seg, key_slot = key_block

            def accumulate(partial_value):
                numerator, denominator = partial_value
                scores = jnp.einsum('qhd,kd->qhk', query_rows.astype(jnp.float32), key_rows.astype(jnp.float32))
                scores = SOFT_CAP * jnp.tanh(scores / SOFT_CAP)
                allowed = (key_seg[None, :] == query_seg[:, None]) & (key_slot[None, :] <= query_slot[:, None]) & present[:, None]
                weights = jnp.where(allowed[:, None, :], jnp.exp(scores), 0.0)
                rounded = lax.optimization_barrier(weights.astype(jnp.bfloat16))
                numerator = numerator + jnp.einsum('qhk,kd->qhd', rounded.astype(jnp.float32), value_rows.astype(jnp.float32))
                denominator = denominator + lax.optimization_barrier(jnp.sum(weights, axis=-1))
                return (numerator, denominator)
            key_present = key_seg >= 0
            touches = (lowest <= jnp.max(key_seg)) & (jnp.min(jnp.where(key_present, key_seg, far_away)) <= highest) & (jnp.min(key_slot) <= latest)
            return (lax.cond(touches, accumulate, lambda unchanged: unchanged, totals), None)
        start_totals = (jnp.zeros((q_rows, head_count, extent), jnp.float32), jnp.zeros((q_rows, head_count), jnp.float32))
        (numerator, denominator), _ = lax.scan(advance, start_totals, key_blocks)
        safe = jnp.where(present[:, None], denominator, 1.0)
        return jnp.where(present[:, None, None], numerator / safe[:, :, None], 0.0)
    results = lax.map(one_block, (queries.reshape(-1, q_rows, head_count, extent), q_seg.reshape(-1, q_rows), q_slot.reshape(-1, q_rows)))
    return results.reshape(q_total, head_count, extent)

def reference(tokens, in_gain, out_gain, query_weight, keyval_weight, out_weight, cache_entries, segment_ids, cache_lengths, block_owners):
    seg_range = jnp.arange(NSEG, dtype=jnp.int32)
    matches = (segment_ids[:, None] == seg_range[None, :]).astype(jnp.int32)
    counts = lax.optimization_barrier(jnp.sum(matches, axis=0))
    firsts = jnp.cumsum(counts) - counts
    slot_index = jnp.arange(TOKENS, dtype=jnp.int32)
    positions = lax.optimization_barrier(jnp.sum(matches * (cache_lengths - firsts)[None, :], axis=1)) + slot_index
    angles = positions.astype(jnp.float32)[:, None] * frequencies(HD)[None, :]
    normed = rms_scale(tokens, in_gain).astype(jnp.bfloat16)
    projected = jnp.dot(normed, query_weight, preferred_element_type=jnp.float32).reshape(TOKENS, QH, HD)
    queries = lax.optimization_barrier((rotate(projected, angles[:, None, :]) * HD ** (-0.5)).astype(jnp.bfloat16))
    keyvals = jnp.dot(normed, keyval_weight, preferred_element_type=jnp.float32).reshape(TOKENS, KVH, 2 * HD)
    new_keys = lax.optimization_barrier(rotate(keyvals[:, :, :HD], angles[:, None, :]).astype(jnp.bfloat16))
    new_values = lax.optimization_barrier(keyvals[:, :, HD:].astype(jnp.bfloat16))
    owner_match = (block_owners[:, None] == seg_range[None, :]).astype(jnp.int32)
    block_rank = lax.optimization_barrier(jnp.sum(owner_match * (jnp.cumsum(owner_match, axis=0) - owner_match), axis=1))
    limits = lax.optimization_barrier(jnp.sum(owner_match * cache_lengths[None, :], axis=1))
    offsets = jnp.arange(BLK, dtype=jnp.int32)
    usable = (block_owners[:, None] >= 0) & (block_rank[:, None] * BLK + offsets[None, :] < limits[:, None])
    cache_seg = jnp.where(usable, block_owners[:, None], -1).reshape(CACHE_ROWS).astype(jnp.int32)
    key_seg = jnp.concatenate([segment_ids, cache_seg])
    key_slot = jnp.concatenate([slot_index, jnp.full((CACHE_ROWS,), -1, jnp.int32)])
    group_size = QH // KVH
    outputs = []
    for shared in range(KVH):
        key_table = jnp.concatenate([new_keys[:, shared], cache_entries[shared, :, :HD]], axis=0)
        value_table = jnp.concatenate([new_values[:, shared], cache_entries[shared, :, HD:]], axis=0)
        outputs.append(attend(queries[:, shared * group_size:(shared + 1) * group_size], segment_ids, slot_index, key_table, value_table, key_seg, key_slot))
    attended = jnp.stack(outputs, axis=1).astype(jnp.bfloat16).reshape(TOKENS, QH * HD)
    branch = jnp.dot(attended, out_weight, preferred_element_type=jnp.float32)
    return (tokens.astype(jnp.float32) + rms_scale(branch, out_gain)).astype(jnp.bfloat16)
```

```python
import functools
import math

import jax
import jax.numpy as jnp
from jax import lax
from jax.experimental import pallas as pl
from jax.experimental.pallas import tpu as pltpu
from jax.sharding import PartitionSpec as P

QH = 8
KVH = 4
HD = 256
NSEG = 64
BLK = 16
LANES = 128
EPSILON = 1e-06
SOFT_CAP = 50.0
FAR = 1073741824
VMEM_BYTES = 40 << 20


def rms_scale(matrix, scaling):
    matrix = matrix.astype(jnp.float32)
    mean_square = jnp.mean(matrix * matrix, axis=-1, keepdims=True)
    return matrix * lax.rsqrt(mean_square + EPSILON) * scaling


def frequencies(extent):
    return 10000.0 ** (-(jnp.arange(extent // 2, dtype=jnp.float32) * 2.0 / extent))


def turn(y, cosine, sine, scale):
    half = y.shape[1] // 2
    a, b = y[:, :half], y[:, half:]
    return (a * cosine - b * sine) * scale, (b * cosine + a * sine) * scale


def query_kernel(count, which_ref, cos_ref, sin_ref, w_ref, *rest):
    parts, out_ref = rest[:count], rest[count]
    half = HD // 2
    x = jnp.concatenate([part[...] for part in parts], axis=0)
    for h in range(w_ref.shape[1] // HD):
        y = jnp.dot(x, w_ref[:, h * HD : (h + 1) * HD], preferred_element_type=jnp.float32)
        a, b = turn(y, cos_ref[...], sin_ref[...], HD**-0.5)
        out_ref[h, :, :half] = a.astype(out_ref.dtype)
        out_ref[h, :, half:] = b.astype(out_ref.dtype)


def keyval_kernel(count, which_ref, cos_ref, sin_ref, w_ref, *rest):
    parts, out_ref = rest[:count], rest[count]
    half = HD // 2
    x = jnp.concatenate([part[...] for part in parts], axis=0)
    y = jnp.dot(x, w_ref[...], preferred_element_type=jnp.float32)
    a, b = turn(y[:, :HD], cos_ref[...], sin_ref[...], 1.0)
    out_ref[:, :half] = a.astype(out_ref.dtype)
    out_ref[:, half:HD] = b.astype(out_ref.dtype)
    out_ref[:, HD:] = y[:, HD:].astype(out_ref.dtype)


def project(body, parts, weight, columns, which, cosine, sine, out_shape):
    rows = cosine.shape[0]
    width = weight.shape[0]
    whole = [pl.BlockSpec(x.shape, lambda i, s: (0, 0)) for x in (cosine, sine)]
    return pl.pallas_call(
        functools.partial(body, len(parts)),
        grid_spec=pltpu.PrefetchScalarGridSpec(
            num_scalar_prefetch=1,
            grid=(1,),
            in_specs=whole
            + [pl.BlockSpec((width, columns), lambda i, s: (0, s[0]))]
            + [pl.BlockSpec(x.shape, lambda i, s: (0, 0)) for x in parts],
            out_specs=pl.BlockSpec(out_shape, lambda i, s: (0,) * len(out_shape)),
        ),
        out_shape=jax.ShapeDtypeStruct(out_shape, jnp.bfloat16),
        compiler_params=pltpu.CompilerParams(vmem_limit_bytes=VMEM_BYTES),
        cost_estimate=pl.CostEstimate(
            flops=2 * rows * width * columns,
            bytes_accessed=2 * width * (columns + rows),
            transcendentals=0,
        ),
        name="project",
    )(which.reshape(1), cosine, sine, weight, *parts)


def fold_blocks(
    heads, q_tile, k_tile, touch_ref, q_ref, qseg_ref, qslot_ref, kseg_ref, kslot_ref, parts, acc, den
):
    q_tiles = q_ref.shape[1] // q_tile
    blocks = kseg_ref.shape[0]
    first = 0
    for part in parts:
        here = part.shape[0] // k_tile

        def step(index, carry, part=part, here=here, first=first):
            qi = index // here
            kj = index % here

            @pl.when(touch_ref[qi * blocks + first + kj] > 0)
            def _():
                rows = pl.ds(pl.multiple_of(qi * q_tile, q_tile), q_tile)
                keys = pl.ds(pl.multiple_of(kj * k_tile, k_tile), k_tile)
                allowed = (kseg_ref[first + kj] == qseg_ref[rows, :]) & (
                    kslot_ref[first + kj] <= qslot_ref[rows, :]
                )
                for h in range(heads):
                    scores = lax.dot_general(
                        q_ref[h, rows, :],
                        part[keys, :HD],
                        (((1,), (1,)), ((), ())),
                        preferred_element_type=jnp.float32,
                    )
                    scores = jnp.tanh(scores * (1.0 / SOFT_CAP))
                    weights = jnp.where(
                        allowed, jnp.exp2(scores * (SOFT_CAP * math.log2(math.e))), 0.0
                    )
                    total = weights[:, :LANES]
                    for c in range(1, k_tile // LANES):
                        total += weights[:, c * LANES : (c + 1) * LANES]
                    den[h, rows, :] += total
                    acc[h, rows, :] += jnp.dot(
                        weights.astype(jnp.bfloat16),
                        part[keys, HD:],
                        preferred_element_type=jnp.float32,
                    )

            return carry

        lax.fori_loop(0, q_tiles * here, step, 0)
        first += here


def middle_kernel(heads, q_tile, k_tile, count, touch_ref, q_ref, qseg_ref, qslot_ref, kseg_ref, kslot_ref, *rest):
    parts, (acc_in, den_in, acc, den) = rest[:count], rest[count:]
    acc[...] = acc_in[...]
    den[...] = den_in[...]
    fold_blocks(
        heads, q_tile, k_tile, touch_ref, q_ref, qseg_ref, qslot_ref, kseg_ref, kslot_ref, parts, acc, den
    )


def first_kernel(heads, q_tile, k_tile, count, touch_ref, q_ref, qseg_ref, qslot_ref, kseg_ref, kslot_ref, *rest):
    parts, (acc, den) = rest[:count], rest[count:]
    acc[...] = jnp.zeros_like(acc)
    den[...] = jnp.zeros_like(den)
    fold_blocks(
        heads, q_tile, k_tile, touch_ref, q_ref, qseg_ref, qslot_ref, kseg_ref, kslot_ref, parts, acc, den
    )


def last_kernel(heads, q_tile, k_tile, count, touch_ref, q_ref, qseg_ref, qslot_ref, kseg_ref, kslot_ref, *rest):
    parts, (acc_in, den_in, out_ref, acc, den) = rest[:count], rest[count:]
    acc[...] = acc_in[...]
    den[...] = den_in[...]
    fold_blocks(
        heads, q_tile, k_tile, touch_ref, q_ref, qseg_ref, qslot_ref, kseg_ref, kslot_ref, parts, acc, den
    )
    present = qseg_ref[...] >= 0
    for h in range(heads):
        total = jnp.sum(den[h], axis=-1, keepdims=True)
        safe = jnp.where(present, total, 1.0)
        out_ref[:, h * HD : (h + 1) * HD] = jnp.where(present, acc[h] / safe, 0.0).astype(
            out_ref.dtype
        )


def attend(queries, q_seg, q_slot, parts, ints, totals=None, last=False):
    heads, rows, _ = queries.shape
    k_seg = jnp.concatenate([pair[0] for pair in ints])
    k_slot = jnp.concatenate([pair[1] for pair in ints])
    q_tile = math.gcd(rows, 256)
    k_tile = math.gcd(*[part.shape[0] for part in parts], 512)
    blocks = k_seg.shape[0] // k_tile
    seg_tiles = q_seg.reshape(-1, q_tile)
    lowest = jnp.min(jnp.where(seg_tiles >= 0, seg_tiles, FAR), axis=1)[:, None]
    highest = jnp.max(seg_tiles, axis=1)[:, None]
    latest = jnp.max(q_slot.reshape(-1, q_tile), axis=1)[:, None]
    near = (k_seg[None] >= lowest) & (k_seg[None] <= highest) & (k_slot[None] <= latest)
    touch = jnp.max(near.astype(jnp.int32).reshape(-1, blocks, k_tile), axis=2).reshape(-1)
    operands = [
        touch,
        queries,
        q_seg[:, None],
        q_slot[:, None],
        k_seg.reshape(blocks, 1, k_tile),
        k_slot.reshape(blocks, 1, k_tile),
        *parts,
    ]
    vmem = pl.BlockSpec(memory_space=pltpu.VMEM)
    sums = [
        jax.ShapeDtypeStruct((heads, rows, HD), jnp.float32),
        jax.ShapeDtypeStruct((heads, rows, LANES), jnp.float32),
    ]
    body, out_shape, out_specs, scratch = first_kernel, sums, [vmem, vmem], []
    if totals is not None:
        operands += list(totals)
        body = middle_kernel
    if last:
        body = last_kernel
        out_shape = jax.ShapeDtypeStruct((rows, heads * HD), jnp.bfloat16)
        out_specs = vmem
        scratch = [pltpu.VMEM(s.shape, s.dtype) for s in sums]
    pairs = heads * rows * k_seg.shape[0]
    return pl.pallas_call(
        functools.partial(body, heads, q_tile, k_tile, len(parts)),
        in_specs=[pl.BlockSpec(memory_space=pltpu.SMEM)] + [vmem] * (len(operands) - 1),
        out_specs=out_specs,
        out_shape=out_shape,
        scratch_shapes=scratch,
        compiler_params=pltpu.CompilerParams(vmem_limit_bytes=VMEM_BYTES),
        cost_estimate=pl.CostEstimate(
            flops=4 * pairs * HD, bytes_accessed=4 * HD * k_seg.shape[0], transcendentals=2 * pairs
        ),
        name="attend",
    )(*operands)


MESH = pl.DeviceIdType.MESH
LOG2E = math.log2(math.e)


def block_kernel(
    table_ref, freq_ref, tok_ref, ig_ref, og_ref, wq_hbm, wkv_hbm, wo_hbm, cache_hbm,
    out_ref,
    tabs, xbuf, wq, wkv, wo, keys, kseg, qseg, cosine, sine, q2, acc, den, sbuf, rbuf, hold,
    load_sem, int_s, int_r, ag_s, ag_r, cu_s, cu_r, cd_s, cd_r, cs_s, cs_r, ku_s, ku_r, ks_s, ks_r,
    rs_s, rs_r,
):
    s, h = lax.axis_index("seq"), lax.axis_index("head")
    n_seq = tabs.shape[0]
    chips = n_seq // 2
    z, core = s // 2, s % 2
    mate = s + 1 - 2 * core
    hx, hy, hd = h + 1 - 2 * (h % 2), (h + 2) % 4, 3 - h
    rel = (h, hx, hy, hd)
    rows = tok_ref.shape[0]
    shard = 4 * rows
    half = rows // 2
    wide = out_ref.shape[1] // 2
    crow = cache_hbm.shape[1]
    cbase = 6 * shard
    f32, bf16 = jnp.float32, jnp.bfloat16

    def remote(src, dst, send, recv, seq=None, head=None):
        device = {"seq": s if seq is None else seq, "head": h if head is None else head}
        return pltpu.make_async_remote_copy(
            src_ref=src, dst_ref=dst, send_sem=send, recv_sem=recv, device_id=device, device_id_type=MESH
        )

    barrier = pltpu.get_barrier_semaphore()
    peers = [lax.rem(s + d, n_seq) for d in range(1, n_seq)]
    for peer in peers:
        pl.semaphore_signal(barrier, inc=1, device_id={"seq": peer, "head": h}, device_id_type=MESH)
    for head in (hx, hy):
        pl.semaphore_signal(barrier, inc=1, device_id={"seq": s, "head": head}, device_id_type=MESH)

    kv_cols = pl.ds(pl.multiple_of(h * 2 * HD, 2 * HD), 2 * HD)
    own_cache = keys.at[pl.ds(pl.multiple_of(cbase + s * crow, crow), crow)]
    loads = [
        pltpu.make_async_copy(wkv_hbm.at[:, kv_cols], wkv, load_sem.at[0]),
        pltpu.make_async_copy(wq_hbm, wq, load_sem.at[1]),
        pltpu.make_async_copy(wo_hbm, wo, load_sem.at[2]),
        pltpu.make_async_copy(cache_hbm.at[h], own_cache, load_sem.at[3]),
    ]
    for load in loads:
        load.start()

    x = tok_ref[...].astype(f32)
    scale = lax.rsqrt(jnp.mean(x * x, axis=-1, keepdims=True) + EPSILON)
    xbuf[h] = (x * scale * ig_ref[...]).astype(bf16)

    pl.semaphore_wait(barrier, n_seq + 1)

    ints = [
        remote(table_ref, tabs.at[s], int_s.at[d], int_r.at[d], seq=peers[d]) for d in range(n_seq - 1)
    ]
    top, bottom = pl.ds(0, half), pl.ds(half, half)

    def token_copy(m, block, part, head):
        ref = xbuf.at[block, part]
        return remote(ref, ref, ag_s.at[m], ag_r.at[m], head=head)

    gather = [
        token_copy(0, h, top, hx), token_copy(1, h, bottom, hx), token_copy(2, h, bottom, hy),
        token_copy(3, h, top, hy), token_copy(4, hx, top, hy), token_copy(5, hy, bottom, hx),
    ]
    gather_in = [
        token_copy(0, hx, top, hx), token_copy(1, hx, bottom, hx), token_copy(2, hy, bottom, hy),
        token_copy(3, hy, top, hy), token_copy(4, hd, top, hy), token_copy(5, hd, bottom, hx),
    ]

    def cache_ref(owner):
        return keys.at[pl.ds(pl.multiple_of(cbase + owner * crow, crow), crow)]

    def cache_up(k, owner):
        src = cache_hbm.at[h] if k == 0 else cache_ref(owner)
        return remote(src, cache_ref(owner), cu_s.at[k], cu_r.at[k], seq=s + 2)

    def cache_down(k, owner):
        src = cache_hbm.at[h] if k == 0 else cache_ref(owner)
        return remote(src, cache_ref(owner), cd_s.at[k], cd_r.at[k], seq=s - 2)

    def cache_side(i, owner):
        src = cache_hbm.at[h] if i == 0 else cache_ref(owner)
        return remote(src, cache_ref(owner), cs_s.at[i], cs_r.at[i], seq=mate)

    last = chips - 1
    for i in range(n_seq - 1):
        ints[i].start()
    for m in (0, 2, 1, 3):
        gather[m].start()

    @pl.when(z < last)
    def _():
        cache_up(0, s).start()

    @pl.when(z > 0)
    def _():
        cache_down(0, s).start()

    cache_side(0, s).start()

    tabs[s] = table_ref[...]
    acc[...] = jnp.zeros_like(acc)
    den[...] = jnp.zeros_like(den)
    for d in range(n_seq - 1):
        source = lax.rem(s + n_seq - 1 - d, n_seq)
        remote(table_ref, tabs.at[source], int_s.at[d], int_r.at[d], seq=source).wait_recv()

    def column(row):
        return jnp.broadcast_to(row, (LANES, LANES)).T

    lane = lax.broadcasted_iota(jnp.int32, (1, LANES), 1)
    segs = lax.broadcasted_iota(jnp.int32, (NSEG, LANES), 0)
    blocks = shard // LANES
    count = jnp.zeros((NSEG, LANES), jnp.int32)
    owners = jnp.zeros((1, LANES), jnp.int32)
    for p in range(n_seq):
        for i in range(blocks):
            row = tabs[p, i : i + 1, :]
            count += jnp.where((row >= 0) & (row < segs), 1, 0)
        owners += tabs[p, blocks : blocks + 1, :]
    firsts = jnp.sum(count.astype(f32), axis=1, keepdims=True)
    lengths = column(table_ref[blocks + 1 : blocks + 2, :].astype(f32))[:NSEG, :1]
    base = lengths - firsts
    for i in range(blocks):
        row = table_ref[i : i + 1, :]
        start = jnp.sum(jnp.where(segs == row, base, 0.0), axis=0, keepdims=True)
        place = start + (s * shard + i * LANES + lane).astype(f32)
        angle = column(place) * freq_ref[...]
        cosine[i] = jnp.cos(angle)
        sine[i] = jnp.sin(angle)
        qseg[i] = column(row)
    for dz in range(3):
        for c in range(2):
            source = jnp.maximum(z - dz, 0) * 2 + c
            for i in range(blocks):
                row = tabs[source, i : i + 1, :]
                at = (dz * 2 + c) * blocks + i
                kseg[at : at + 1, :] = jnp.where(row < 0, -2, row)
    same = (column(owners) == owners) & (
        lax.broadcasted_iota(jnp.int32, (LANES, LANES), 0)
        < lax.broadcasted_iota(jnp.int32, (LANES, LANES), 1)
    )
    rank = jnp.sum(jnp.where(same, 1, 0), axis=0, keepdims=True)
    limit = jnp.sum(jnp.where(segs == owners, lengths, 0.0), axis=0, keepdims=True).astype(jnp.int32)
    filled = jnp.where(owners >= 0, jnp.clip(limit - BLK * rank, 0, BLK), 0)
    owner_col, filled_col = column(owners), column(filled)
    per = LANES // BLK
    pick = lax.broadcasted_iota(jnp.int32, (per, LANES), 0) == lane // BLK
    for i in range(n_seq * crow // LANES):
        part = slice(i * per, (i + 1) * per)
        who = jnp.sum(jnp.where(pick, owner_col[part], 0), axis=0, keepdims=True)
        many = jnp.sum(jnp.where(pick, filled_col[part], 0), axis=0, keepdims=True)
        at = 6 * blocks + i
        kseg[at : at + 1, :] = jnp.where(lane % BLK < many, who, -2)

    def kv_ref(dz, c, block):
        return keys.at[pl.ds(pl.multiple_of((dz * 2 + c) * shard + block * rows, rows), rows)]

    def kv_up(dz, r):
        return remote(
            kv_ref(dz, core, rel[r]), kv_ref(dz + 1, core, rel[r]), ku_s.at[dz, r], ku_r.at[dz, r], seq=s + 2
        )

    def kv_side(dz, r, c=None):
        ref = kv_ref(dz, core if c is None else c, rel[r])
        return remote(ref, ref, ks_s.at[dz, r], ks_r.at[dz, r], seq=mate)

    def project_kv(r):
        block = rel[r]
        y = jnp.dot(xbuf[block], wkv[...], preferred_element_type=f32)
        a, b = turn(y[:, :HD], cosine[block], sine[block], 1.0)
        at = pl.ds(pl.multiple_of(core * shard + block * rows, rows), rows)
        keys[at, : HD // 2] = a.astype(bf16)
        keys[at, HD // 2 : HD] = b.astype(bf16)
        keys[at, HD:] = y[:, HD:].astype(bf16)

        @pl.when(z < last)
        def _():
            kv_up(0, r).start()

        @pl.when(core == 0)
        def _():
            kv_side(0, r).start()

    def project_q(r):
        block = rel[r]
        y = jnp.dot(xbuf[block], wq[...], preferred_element_type=f32)
        for g in range(2):
            a, b = turn(y[:, g * HD : (g + 1) * HD], cosine[block], sine[block], HD**-0.5)
            q2[block, g * rows : (g + 1) * rows, : HD // 2] = a.astype(bf16)
            q2[block, g * rows : (g + 1) * rows, HD // 2 :] = b.astype(bf16)

    def pass_cache(k):
        @pl.when(z >= k)
        def _():
            owner = s - 2 * k
            cache_up(k - 1, owner).wait_recv()

            if k < last:
                pl.when(z < last)(lambda: cache_up(k, owner).start())

            cache_side(k, owner).start()

        @pl.when(z + k <= last)
        def _():
            owner = s + 2 * k
            cache_down(k - 1, owner).wait_recv()

            if k < last:
                pl.when(z > 0)(lambda: cache_down(k, owner).start())

            cache_side(last + k, owner).start()

    def pass_kv(r):
        @pl.when(z >= 1)
        def _():
            kv_up(0, r).wait_recv()

            @pl.when(z < last)
            def _():
                kv_up(1, r).start()

            kv_side(1, r).start()

    def pass_far(r):
        @pl.when(z >= 2)
        def _():
            kv_up(1, r).wait_recv()

            @pl.when(core == 1)
            def _():
                kv_side(2, r).start()

    tile = shard

    def attend(j, at, causal=False):
        span = pl.ds(pl.multiple_of(at * tile, tile), tile)
        scores = lax.dot_general(
            q2[j], keys[span, :HD], (((1,), (1,)), ((), ())), preferred_element_type=f32
        )
        columns = []
        total = [den[j, g * rows : (g + 1) * rows, :] for g in range(2)]
        for c in range(tile // LANES):
            allowed = qseg[j] == kseg[pl.ds(at * (tile // LANES) + c, 1), :]
            if causal:
                query = j * rows + lax.broadcasted_iota(jnp.int32, (rows, LANES), 0)
                allowed &= c * LANES + lax.broadcasted_iota(jnp.int32, (rows, LANES), 1) <= query
            pair = []
            for g in range(2):
                part = scores[g * rows : (g + 1) * rows, c * LANES : (c + 1) * LANES]
                part = jnp.exp2(jnp.tanh(part * (1.0 / SOFT_CAP)) * (SOFT_CAP * LOG2E))
                part = jnp.where(allowed, part, 0.0)
                total[g] += part
                pair.append(part.astype(bf16))
            columns.append(jnp.concatenate(pair, axis=0))
        for g in range(2):
            den[j, g * rows : (g + 1) * rows, :] = total[g]
        weights = jnp.concatenate(columns, axis=1)
        acc[j] += jnp.dot(weights, keys[span, HD:], preferred_element_type=f32)

    def attend_all(at, causal=False):
        def body(j, carry):
            attend(j, at, causal)
            return carry

        lax.fori_loop(0, 4, body, 0)

    def attend_cache(other):
        attend_all(6 + other)

    loads[0].wait()
    project_kv(0)
    loads[1].wait()
    project_q(0)
    gather_in[0].wait_recv()
    gather[4].start()
    gather_in[2].wait_recv()
    gather[5].start()
    pass_cache(1)
    gather_in[1].wait_recv()
    project_kv(1)
    gather_in[3].wait_recv()
    project_kv(2)
    pass_kv(0)
    project_q(1)
    project_q(2)
    pass_cache(2)
    gather_in[4].wait_recv()
    gather_in[5].wait_recv()
    project_kv(3)
    pass_kv(1)
    pass_kv(2)
    project_q(3)
    loads[3].wait()
    cache_side(0, mate).wait_recv()
    attend_all(core, True)
    pass_cache(3)
    pass_kv(3)
    attend_cache(z)

    @pl.when(core == 1)
    def _():
        for r in range(4):
            kv_side(0, r, 0).wait_recv()
        attend_all(0)

    for k in range(1, chips):
        @pl.when(z >= k)
        def _():
            cache_side(k, mate - 2 * k).wait_recv()
            attend_cache(z - k)

        @pl.when(z + k <= last)
        def _():
            cache_side(last + k, mate + 2 * k).wait_recv()
            attend_cache(z + k)

    @pl.when(z >= 1)
    def _():
        for r in range(4):
            kv_side(1, r, 1 - core).wait_recv()
        attend_all(2)
        attend_all(3)

    for r in range(4):
        pass_far(r)

    @pl.when(z >= 2)
    def _():
        @pl.when(core == 0)
        def _():
            attend_all(4)
            for r in range(4):
                kv_side(2, r, 1).wait_recv()

        attend_all(5)

    loads[2].wait()

    def attended(j):
        present = qseg[j] >= 0
        present = present[:, :1]
        parts = []
        for g in range(2):
            total = jnp.sum(den[j, g * rows : (g + 1) * rows, :], axis=-1, keepdims=True)
            safe = jnp.where(present, total, 1.0)
            value = acc[j, g * rows : (g + 1) * rows, :] / safe
            parts.append(jnp.where(present, value, 0.0).astype(bf16))
        return jnp.concatenate(parts, axis=1)

    def out_copy(m):
        return remote(sbuf.at[m], rbuf.at[m], rs_s.at[m], rs_r.at[m], head=hx if m in (0, 2, 3) else hy)

    def left(a):
        return jnp.dot(a, wo[:, :wide], preferred_element_type=f32)

    def right(a):
        return jnp.dot(a, wo[:, wide:], preferred_element_type=f32)

    a = attended(hd)
    sbuf[0] = left(a).astype(bf16)
    out_copy(0).start()
    sbuf[1] = right(a).astype(bf16)
    out_copy(1).start()
    a = attended(hx)
    sbuf[2] = left(a).astype(bf16)
    out_copy(2).start()
    b = attended(hy)
    sbuf[4] = right(b).astype(bf16)
    out_copy(4).start()
    hold[0] = right(a)
    hold[1] = left(b)
    out_copy(1).wait_recv()
    sbuf[3] = (hold[0] + rbuf[1].astype(f32)).astype(bf16)
    out_copy(3).start()
    out_copy(0).wait_recv()
    sbuf[5] = (hold[1] + rbuf[0].astype(f32)).astype(bf16)
    out_copy(5).start()
    a = attended(h)
    hold[0] = left(a)
    hold[1] = right(a)
    out_copy(2).wait_recv()
    hold[0] += rbuf[2].astype(f32)
    out_copy(4).wait_recv()
    hold[1] += rbuf[4].astype(f32)
    out_copy(5).wait_recv()
    out_copy(3).wait_recv()
    branch_l = hold[0] + rbuf[5].astype(f32)
    branch_r = hold[1] + rbuf[3].astype(f32)
    square = jnp.sum(branch_l * branch_l, axis=-1, keepdims=True) + jnp.sum(
        branch_r * branch_r, axis=-1, keepdims=True
    )
    scale = lax.rsqrt(square / (2 * wide) + EPSILON)
    out_ref[:, :wide] = (
        tok_ref[:, :wide].astype(f32) + branch_l * scale * og_ref[:, :wide]
    ).astype(bf16)
    out_ref[:, wide:] = (
        tok_ref[:, wide:].astype(f32) + branch_r * scale * og_ref[:, wide:]
    ).astype(bf16)

    for i in range(n_seq - 1):
        ints[i].wait_send()
    for copy in gather:
        copy.wait_send()
    for m in range(6):
        out_copy(m).wait_send()
    cache_side(0, s).wait_send()
    for k in range(chips - 1):
        @pl.when((z < last) & (z >= k))
        def _():
            cache_up(k, s - 2 * k).wait_send()

        @pl.when((z > 0) & (z + k <= last))
        def _():
            cache_down(k, s + 2 * k).wait_send()

    for k in range(1, chips):
        @pl.when(z >= k)
        def _():
            cache_side(k, s - 2 * k).wait_send()

        @pl.when(z + k <= last)
        def _():
            cache_side(last + k, s + 2 * k).wait_send()

    for r in range(4):
        @pl.when(z < last)
        def _():
            kv_up(0, r).wait_send()

        @pl.when(core == 0)
        def _():
            kv_side(0, r).wait_send()

        @pl.when(z >= 1)
        def _():
            kv_side(1, r).wait_send()

        @pl.when((z >= 1) & (z < last))
        def _():
            kv_up(1, r).wait_send()

        @pl.when((z >= 2) & (core == 1))
        def _():
            kv_side(2, r).wait_send()


def whole_block(
    tokens, in_gain, out_gain, query_weight, keyval_weight, out_weight, cache_entries, segment_ids,
    cache_lengths, block_owners,
):
    n_seq = lax.axis_size("seq")
    s = lax.axis_index("seq")
    rows, width = tokens.shape
    shard = segment_ids.shape[0]
    blocks = shard // LANES
    lane = jnp.arange(LANES, dtype=jnp.int32)
    here = block_owners.shape[0]
    owners = jnp.where(lane // here == s, jnp.tile(block_owners, LANES // here), 0)
    lengths = jnp.pad(cache_lengths, (0, LANES - NSEG))
    table = jnp.concatenate([segment_ids.reshape(blocks, LANES), owners[None], lengths[None]])
    table = jnp.pad(table, ((0, -table.shape[0] % 8), (0, 0)))
    crow = cache_entries.shape[1]
    n_keys = 6 * shard + n_seq * crow
    vmem, hbm = pl.BlockSpec(memory_space=pltpu.VMEM), pl.BlockSpec(memory_space=pl.ANY)
    f32, bf16, i32 = jnp.float32, jnp.bfloat16, jnp.int32
    dma = pltpu.SemaphoreType.DMA
    hops = n_seq // 2 - 1
    pairs = [dma((n,)) for n in (n_seq - 1, 6, hops, hops, 2 * hops + 1) for _ in range(2)]
    return pl.pallas_call(
        block_kernel,
        out_shape=jax.ShapeDtypeStruct((rows, width), bf16),
        in_specs=[vmem] * 5 + [hbm] * 4,
        out_specs=vmem,
        scratch_shapes=[
            pltpu.VMEM((n_seq,) + table.shape, i32),
            pltpu.VMEM((4, rows, width), bf16),
            pltpu.VMEM((width, 2 * HD), bf16),
            pltpu.VMEM((width, 2 * HD), bf16),
            pltpu.VMEM((2 * HD, width), bf16),
            pltpu.VMEM((n_keys, 2 * HD), bf16),
            pltpu.VMEM((n_keys // LANES, LANES), i32),
            pltpu.VMEM((4, rows, LANES), i32),
            pltpu.VMEM((4, rows, LANES), f32),
            pltpu.VMEM((4, rows, LANES), f32),
            pltpu.VMEM((4, 2 * rows, HD), bf16),
            pltpu.VMEM((4, 2 * rows, HD), f32),
            pltpu.VMEM((4, 2 * rows, LANES), f32),
            pltpu.VMEM((6, rows, width // 2), bf16),
            pltpu.VMEM((6, rows, width // 2), bf16),
            pltpu.VMEM((2, rows, width // 2), f32),
            dma((4,)),
            *pairs,
            dma((2, 4)), dma((2, 4)), dma((3, 4)), dma((3, 4)),
            dma((6,)), dma((6,)),
        ],
        compiler_params=pltpu.CompilerParams(
            collective_id=0, has_side_effects=True, vmem_limit_bytes=56 << 20
        ),
        cost_estimate=pl.CostEstimate(
            flops=2 * shard * (6 * HD * width + 8 * n_keys * HD // 4),
            bytes_accessed=6 * HD * 2 * width,
            transcendentals=4 * shard * n_keys,
        ),
        name="block",
    )(
        table, frequencies(HD)[None], tokens, in_gain[None], out_gain[None], query_weight, keyval_weight,
        out_weight, cache_entries,
    )


def local(
    tokens,
    in_gain,
    out_gain,
    query_weight,
    keyval_weight,
    out_weight,
    cache_entries,
    segment_ids,
    cache_lengths,
    block_owners,
):
    heads_here = query_weight.shape[1] // HD
    group_size = QH // KVH
    seq_size, head_size = lax.axis_size("seq"), lax.axis_size("head")
    seq_index = lax.axis_index("seq")
    head_index = lax.axis_index("head")
    shared_head = head_index * heads_here // group_size
    stream_rows = segment_ids.shape[0]
    normed_own = rms_scale(tokens, in_gain).astype(jnp.bfloat16)
    chunks = [[lax.all_gather(normed_own, "head", axis=0, tiled=True)]]

    cache_own = lax.dynamic_index_in_dim(cache_entries, shared_head, 0, keepdims=False)
    cache_pairs = lax.all_gather(cache_own, "seq", axis=0, tiled=True)

    table = jnp.concatenate([segment_ids, block_owners])[None]
    bits = 0
    while 1 << bits < seq_size:
        step = 1 << bits
        other = lax.ppermute(table, "seq", [(s, s ^ step) for s in range(seq_size)])
        table = jnp.concatenate([table, other], axis=0)
        bits += 1
    for bit in range(bits):
        pieces = table.reshape(-1, 2, 1 << bit, table.shape[-1])
        pieces = jnp.where((seq_index >> bit) % 2 == 1, pieces[:, ::-1], pieces)
        table = pieces.reshape(seq_size, -1)
    seg_all = table[:, :stream_rows].reshape(-1)
    owners = table[:, stream_rows:].reshape(-1)

    seg_range = jnp.arange(NSEG, dtype=jnp.int32)
    earlier = (seg_all[None, :] >= 0) & (seg_all[None, :] < seg_range[:, None])
    firsts = jnp.sum(earlier.astype(jnp.int32), axis=1)
    slots_all = jnp.arange(seg_all.shape[0], dtype=jnp.int32)
    begin = seq_index * stream_rows
    q_seg = lax.dynamic_slice_in_dim(seg_all, begin, stream_rows)
    q_slot = lax.dynamic_slice_in_dim(slots_all, begin, stream_rows)
    matches = (q_seg[:, None] == seg_range[None, :]).astype(jnp.int32)
    positions = jnp.sum(matches * (cache_lengths - firsts)[None, :], axis=1) + q_slot
    angles = positions.astype(jnp.float32)[:, None] * frequencies(HD)[None, :]
    cosine, sine = jnp.cos(angles), jnp.sin(angles)

    block_index = jnp.arange(owners.shape[0], dtype=jnp.int32)
    same = (owners[:, None] == owners[None, :]) & (block_index[None, :] < block_index[:, None])
    block_rank = jnp.sum(same.astype(jnp.int32), axis=1)
    owner_match = (owners[:, None] == seg_range[None, :]).astype(jnp.int32)
    limits = jnp.sum(owner_match * cache_lengths[None, :], axis=1)
    offsets = jnp.arange(BLK, dtype=jnp.int32)
    usable = (owners[:, None] >= 0) & (
        block_rank[:, None] * BLK + offsets[None, :] < limits[:, None]
    )
    cache_seg = jnp.where(usable, owners[:, None], -2).reshape(-1)
    cache_slot = jnp.full((cache_seg.shape[0],), -1, jnp.int32)

    chunk_rows = stream_rows // len(chunks)
    pairs = []
    for at, parts in enumerate(chunks):
        rows = slice(at * chunk_rows, (at + 1) * chunk_rows)
        pairs.append(
            project(
                keyval_kernel, parts, keyval_weight, 2 * HD, shared_head,
                cosine[rows], sine[rows], (chunk_rows, 2 * HD),
            )
        )
    queries = project(
        query_kernel, sum(chunks, []), query_weight, heads_here * HD, jnp.int32(0),
        cosine, sine, (heads_here, stream_rows, HD),
    )

    hops = seq_size // 4

    def onward(array):
        return lax.ppermute(array, "seq", [(s, s + 2) for s in range(seq_size - 2)])

    def sibling(array):
        return lax.ppermute(array, "seq", [(s, s ^ 1) for s in range(seq_size)])

    key_seg = jnp.where(seg_all >= 0, seg_all, -2)

    def shard_ints(shard):
        inside = (shard >= 0) & (shard < seq_size)
        at = jnp.clip(shard, 0, seq_size - 1) * stream_rows
        seg = lax.dynamic_slice_in_dim(key_seg, at, stream_rows)
        return jnp.where(inside, seg, -2), lax.dynamic_slice_in_dim(slots_all, at, stream_rows)

    mate = seq_index + 1 - 2 * (seq_index % 2)
    travelling = [onward(pair) for pair in pairs]
    waiting, waiting_ints = [sibling(pair) for pair in pairs], [shard_ints(mate)]
    totals = attend(
        queries, q_seg, q_slot, pairs + [cache_pairs], [shard_ints(seq_index), (cache_seg, cache_slot)]
    )
    for hop in range(1, hops + 1):
        travelling, totals = lax.optimization_barrier((travelling, totals))
        following = [onward(pair) for pair in travelling] if hop < hops else []
        beside = [sibling(pair) for pair in travelling]
        parts = waiting + travelling
        ints = waiting_ints + [shard_ints(seq_index - 2 * hop)]
        waiting, waiting_ints = beside, [shard_ints(mate - 2 * hop)]
        if hop < hops:
            totals = attend(queries, q_seg, q_slot, parts, ints, totals)
        else:
            attended = attend(
                queries, q_seg, q_slot, parts + waiting, ints + waiting_ints, totals, last=True
            )
        travelling = following

    branch = lax.psum_scatter(
        jnp.dot(attended, out_weight, preferred_element_type=jnp.float32),
        "head",
        scatter_dimension=0,
        tiled=True,
    )
    return (tokens.astype(jnp.float32) + rms_scale(branch, out_gain)).astype(jnp.bfloat16)


def solution(mesh):
    in_specs = (
        P(("seq", "head"), None),
        P(),
        P(),
        P(None, "head"),
        P(),
        P("head", None),
        P(None, "seq", None),
        P("seq"),
        P(),
        P("seq"),
    )
    out_specs = P(("seq", "head"), None)
    fits = mesh.shape["seq"] == 8 and mesh.shape["head"] == 4
    body = whole_block if fits else local
    return jax.shard_map(body, mesh=mesh, in_specs=in_specs, out_specs=out_specs, check_vma=False)
```

```python
import functools
import math

import jax
import jax.numpy as jnp
import numpy as np
from jax import lax
from jax.experimental import pallas as pl
from jax.experimental.pallas import tpu as pltpu
from jax.sharding import PartitionSpec as P

QH = 8
KVH = 4
HD = 256
NSEG = 64
BLK = 16
LANES = 128
EPSILON = 1e-06
SOFT_CAP = 50.0
FAR = 1073741824
VMEM_BYTES = 40 << 20


def rms_scale(matrix, scaling):
    matrix = matrix.astype(jnp.float32)
    mean_square = jnp.mean(matrix * matrix, axis=-1, keepdims=True)
    return matrix * lax.rsqrt(mean_square + EPSILON) * scaling


def frequencies(extent):
    return 10000.0 ** (-(jnp.arange(extent // 2, dtype=jnp.float32) * 2.0 / extent))


def turn(y, cosine, sine, scale):
    half = y.shape[1] // 2
    a, b = y[:, :half], y[:, half:]
    return (a * cosine - b * sine) * scale, (b * cosine + a * sine) * scale


def query_kernel(count, which_ref, cos_ref, sin_ref, w_ref, *rest):
    parts, out_ref = rest[:count], rest[count]
    half = HD // 2
    x = jnp.concatenate([part[...] for part in parts], axis=0)
    for h in range(w_ref.shape[1] // HD):
        y = jnp.dot(x, w_ref[:, h * HD : (h + 1) * HD], preferred_element_type=jnp.float32)
        a, b = turn(y, cos_ref[...], sin_ref[...], HD**-0.5)
        out_ref[h, :, :half] = a.astype(out_ref.dtype)
        out_ref[h, :, half:] = b.astype(out_ref.dtype)


def keyval_kernel(count, which_ref, cos_ref, sin_ref, w_ref, *rest):
    parts, out_ref = rest[:count], rest[count]
    half = HD // 2
    x = jnp.concatenate([part[...] for part in parts], axis=0)
    y = jnp.dot(x, w_ref[...], preferred_element_type=jnp.float32)
    a, b = turn(y[:, :HD], cos_ref[...], sin_ref[...], 1.0)
    out_ref[:, :half] = a.astype(out_ref.dtype)
    out_ref[:, half:HD] = b.astype(out_ref.dtype)
    out_ref[:, HD:] = y[:, HD:].astype(out_ref.dtype)


def project(body, parts, weight, columns, which, cosine, sine, out_shape):
    rows = cosine.shape[0]
    width = weight.shape[0]
    whole = [pl.BlockSpec(x.shape, lambda i, s: (0, 0)) for x in (cosine, sine)]
    return pl.pallas_call(
        functools.partial(body, len(parts)),
        grid_spec=pltpu.PrefetchScalarGridSpec(
            num_scalar_prefetch=1,
            grid=(1,),
            in_specs=whole
            + [pl.BlockSpec((width, columns), lambda i, s: (0, s[0]))]
            + [pl.BlockSpec(x.shape, lambda i, s: (0, 0)) for x in parts],
            out_specs=pl.BlockSpec(out_shape, lambda i, s: (0,) * len(out_shape)),
        ),
        out_shape=jax.ShapeDtypeStruct(out_shape, jnp.bfloat16),
        compiler_params=pltpu.CompilerParams(vmem_limit_bytes=VMEM_BYTES),
        cost_estimate=pl.CostEstimate(
            flops=2 * rows * width * columns,
            bytes_accessed=2 * width * (columns + rows),
            transcendentals=0,
        ),
        name="project",
    )(which.reshape(1), cosine, sine, weight, *parts)


def fold_blocks(
    heads, q_tile, k_tile, touch_ref, q_ref, qseg_ref, qslot_ref, kseg_ref, kslot_ref, parts, acc, den
):
    q_tiles = q_ref.shape[1] // q_tile
    blocks = kseg_ref.shape[0]
    first = 0
    for part in parts:
        here = part.shape[0] // k_tile

        def step(index, carry, part=part, here=here, first=first):
            qi = index // here
            kj = index % here

            @pl.when(touch_ref[qi * blocks + first + kj] > 0)
            def _():
                rows = pl.ds(pl.multiple_of(qi * q_tile, q_tile), q_tile)
                keys = pl.ds(pl.multiple_of(kj * k_tile, k_tile), k_tile)
                allowed = (kseg_ref[first + kj] == qseg_ref[rows, :]) & (
                    kslot_ref[first + kj] <= qslot_ref[rows, :]
                )
                for h in range(heads):
                    scores = lax.dot_general(
                        q_ref[h, rows, :],
                        part[keys, :HD],
                        (((1,), (1,)), ((), ())),
                        preferred_element_type=jnp.float32,
                    )
                    scores = jnp.tanh(scores * (1.0 / SOFT_CAP))
                    weights = jnp.where(
                        allowed, jnp.exp2(scores * (SOFT_CAP * math.log2(math.e))), 0.0
                    )
                    total = weights[:, :LANES]
                    for c in range(1, k_tile // LANES):
                        total += weights[:, c * LANES : (c + 1) * LANES]
                    den[h, rows, :] += total
                    acc[h, rows, :] += jnp.dot(
                        weights.astype(jnp.bfloat16),
                        part[keys, HD:],
                        preferred_element_type=jnp.float32,
                    )

            return carry

        lax.fori_loop(0, q_tiles * here, step, 0)
        first += here


def middle_kernel(heads, q_tile, k_tile, count, touch_ref, q_ref, qseg_ref, qslot_ref, kseg_ref, kslot_ref, *rest):
    parts, (acc_in, den_in, acc, den) = rest[:count], rest[count:]
    acc[...] = acc_in[...]
    den[...] = den_in[...]
    fold_blocks(
        heads, q_tile, k_tile, touch_ref, q_ref, qseg_ref, qslot_ref, kseg_ref, kslot_ref, parts, acc, den
    )


def first_kernel(heads, q_tile, k_tile, count, touch_ref, q_ref, qseg_ref, qslot_ref, kseg_ref, kslot_ref, *rest):
    parts, (acc, den) = rest[:count], rest[count:]
    acc[...] = jnp.zeros_like(acc)
    den[...] = jnp.zeros_like(den)
    fold_blocks(
        heads, q_tile, k_tile, touch_ref, q_ref, qseg_ref, qslot_ref, kseg_ref, kslot_ref, parts, acc, den
    )


def last_kernel(heads, q_tile, k_tile, count, touch_ref, q_ref, qseg_ref, qslot_ref, kseg_ref, kslot_ref, *rest):
    parts, (acc_in, den_in, out_ref, acc, den) = rest[:count], rest[count:]
    acc[...] = acc_in[...]
    den[...] = den_in[...]
    fold_blocks(
        heads, q_tile, k_tile, touch_ref, q_ref, qseg_ref, qslot_ref, kseg_ref, kslot_ref, parts, acc, den
    )
    present = qseg_ref[...] >= 0
    for h in range(heads):
        total = jnp.sum(den[h], axis=-1, keepdims=True)
        safe = jnp.where(present, total, 1.0)
        out_ref[:, h * HD : (h + 1) * HD] = jnp.where(present, acc[h] / safe, 0.0).astype(
            out_ref.dtype
        )


def attend(queries, q_seg, q_slot, parts, ints, totals=None, last=False):
    heads, rows, _ = queries.shape
    k_seg = jnp.concatenate([pair[0] for pair in ints])
    k_slot = jnp.concatenate([pair[1] for pair in ints])
    q_tile = math.gcd(rows, 256)
    k_tile = math.gcd(*[part.shape[0] for part in parts], 512)
    blocks = k_seg.shape[0] // k_tile
    seg_tiles = q_seg.reshape(-1, q_tile)
    lowest = jnp.min(jnp.where(seg_tiles >= 0, seg_tiles, FAR), axis=1)[:, None]
    highest = jnp.max(seg_tiles, axis=1)[:, None]
    latest = jnp.max(q_slot.reshape(-1, q_tile), axis=1)[:, None]
    near = (k_seg[None] >= lowest) & (k_seg[None] <= highest) & (k_slot[None] <= latest)
    touch = jnp.max(near.astype(jnp.int32).reshape(-1, blocks, k_tile), axis=2).reshape(-1)
    operands = [
        touch,
        queries,
        q_seg[:, None],
        q_slot[:, None],
        k_seg.reshape(blocks, 1, k_tile),
        k_slot.reshape(blocks, 1, k_tile),
        *parts,
    ]
    vmem = pl.BlockSpec(memory_space=pltpu.VMEM)
    sums = [
        jax.ShapeDtypeStruct((heads, rows, HD), jnp.float32),
        jax.ShapeDtypeStruct((heads, rows, LANES), jnp.float32),
    ]
    body, out_shape, out_specs, scratch = first_kernel, sums, [vmem, vmem], []
    if totals is not None:
        operands += list(totals)
        body = middle_kernel
    if last:
        body = last_kernel
        out_shape = jax.ShapeDtypeStruct((rows, heads * HD), jnp.bfloat16)
        out_specs = vmem
        scratch = [pltpu.VMEM(s.shape, s.dtype) for s in sums]
    pairs = heads * rows * k_seg.shape[0]
    return pl.pallas_call(
        functools.partial(body, heads, q_tile, k_tile, len(parts)),
        in_specs=[pl.BlockSpec(memory_space=pltpu.SMEM)] + [vmem] * (len(operands) - 1),
        out_specs=out_specs,
        out_shape=out_shape,
        scratch_shapes=scratch,
        compiler_params=pltpu.CompilerParams(vmem_limit_bytes=VMEM_BYTES),
        cost_estimate=pl.CostEstimate(
            flops=4 * pairs * HD, bytes_accessed=4 * HD * k_seg.shape[0], transcendentals=2 * pairs
        ),
        name="attend",
    )(*operands)


MESH = pl.DeviceIdType.MESH
LOG2E = math.log2(math.e)


def block_kernel(
    len_ref, own_ref, freq_ref, tok_ref, seg_hbm, ig_hbm, og_hbm, wq_hbm, wkv_hbm, wo_hbm, cache_hbm,
    out_ref,
    tabs, ig_ref, og_ref, xbuf, wq, wkv, wo, keys, kseg, qseg, cosine, sine, q2, acc, den, sbuf, rbuf, hold,
    load_sem, int_s, int_r, ag_s, ag_r, cu_s, cu_r, cd_s, cd_r, cs_s, cs_r, ku_s, ku_r, ks_s, ks_r,
    rs_s, rs_r,
):
    s, h = lax.axis_index("seq"), lax.axis_index("head")
    n_seq = tabs.shape[0]
    chips = n_seq // 2
    z, core = s // 2, s % 2
    mate = s + 1 - 2 * core
    hx, hy, hd = h + 1 - 2 * (h % 2), (h + 2) % 4, 3 - h
    rel = (h, hx, hy, hd)
    rows = tok_ref.shape[0]
    shard = 4 * rows
    half = rows // 2
    wide = out_ref.shape[1] // 2
    crow = cache_hbm.shape[1]
    cbase = 6 * shard
    f32, bf16 = jnp.float32, jnp.bfloat16

    def remote(src, dst, send, recv, seq=None, head=None):
        device = {"seq": s if seq is None else seq, "head": h if head is None else head}
        return pltpu.make_async_remote_copy(
            src_ref=src, dst_ref=dst, send_sem=send, recv_sem=recv, device_id=device, device_id_type=MESH
        )

    barrier = pltpu.get_barrier_semaphore()
    peers = [lax.rem(s + d, n_seq) for d in range(1, n_seq)]
    for peer in peers:
        pl.semaphore_signal(barrier, inc=1, device_id={"seq": peer, "head": h}, device_id_type=MESH)
    for head in (hx, hy):
        pl.semaphore_signal(barrier, inc=1, device_id={"seq": s, "head": head}, device_id_type=MESH)

    kv_cols = pl.ds(pl.multiple_of(h * 2 * HD, 2 * HD), 2 * HD)
    own_cache = keys.at[pl.ds(pl.multiple_of(cbase + s * crow, crow), crow)]
    blocks = shard // LANES
    loads = [
        pltpu.make_async_copy(wkv_hbm.at[:, kv_cols], wkv, load_sem.at[0]),
        pltpu.make_async_copy(wq_hbm, wq, load_sem.at[1]),
        pltpu.make_async_copy(wo_hbm, wo, load_sem.at[2]),
        pltpu.make_async_copy(cache_hbm.at[h], own_cache, load_sem.at[3]),
    ]
    early = [
        pltpu.make_async_copy(ig_hbm, ig_ref.at[0], load_sem.at[4]),
        pltpu.make_async_copy(og_hbm, og_ref.at[0], load_sem.at[5]),
    ] + [
        pltpu.make_async_copy(seg_hbm.at[pl.ds(i * LANES, LANES)], tabs.at[s, i], load_sem.at[6 + i])
        for i in range(blocks)
    ]
    for load in early + loads:
        load.start()

    lane = lax.broadcasted_iota(jnp.int32, (1, LANES), 1)
    owned = jnp.zeros((1, LANES), jnp.int32)
    for i in range(own_ref.shape[0]):
        owned = jnp.where(lane == s * own_ref.shape[0] + i, own_ref[i], owned)
    tabs[s, blocks : blocks + 1, :] = owned
    for load in early:
        load.wait()

    x = tok_ref[...].astype(f32)
    scale = lax.rsqrt(jnp.mean(x * x, axis=-1, keepdims=True) + EPSILON)
    xbuf[h] = (x * scale * ig_ref[...]).astype(bf16)

    pl.semaphore_wait(barrier, n_seq + 1)

    ints = [
        remote(tabs.at[s], tabs.at[s], int_s.at[d], int_r.at[d], seq=peers[d]) for d in range(n_seq - 1)
    ]
    top, bottom = pl.ds(0, half), pl.ds(half, half)

    def token_copy(m, block, part, head):
        ref = xbuf.at[block, part]
        return remote(ref, ref, ag_s.at[m], ag_r.at[m], head=head)

    gather = [
        token_copy(0, h, top, hx), token_copy(1, h, bottom, hx), token_copy(2, h, bottom, hy),
        token_copy(3, h, top, hy), token_copy(4, hx, top, hy), token_copy(5, hy, bottom, hx),
    ]
    gather_in = [
        token_copy(0, hx, top, hx), token_copy(1, hx, bottom, hx), token_copy(2, hy, bottom, hy),
        token_copy(3, hy, top, hy), token_copy(4, hd, top, hy), token_copy(5, hd, bottom, hx),
    ]

    def cache_ref(owner):
        return keys.at[pl.ds(pl.multiple_of(cbase + owner * crow, crow), crow)]

    def cache_up(k, owner):
        src = cache_hbm.at[h] if k == 0 else cache_ref(owner)
        return remote(src, cache_ref(owner), cu_s.at[k], cu_r.at[k], seq=s + 2)

    def cache_down(k, owner):
        src = cache_hbm.at[h] if k == 0 else cache_ref(owner)
        return remote(src, cache_ref(owner), cd_s.at[k], cd_r.at[k], seq=s - 2)

    def cache_side(i, owner):
        src = cache_hbm.at[h] if i == 0 else cache_ref(owner)
        return remote(src, cache_ref(owner), cs_s.at[i], cs_r.at[i], seq=mate)

    last = chips - 1
    for i in range(n_seq - 1):
        ints[i].start()
    for m in (0, 2, 1, 3):
        gather[m].start()

    @pl.when(z < last)
    def _():
        cache_up(0, s).start()

    @pl.when(z > 0)
    def _():
        cache_down(0, s).start()

    cache_side(0, s).start()

    acc[...] = jnp.zeros_like(acc)
    den[...] = jnp.zeros_like(den)
    for d in range(n_seq - 1):
        source = lax.rem(s + n_seq - 1 - d, n_seq)
        remote(tabs.at[source], tabs.at[source], int_s.at[d], int_r.at[d], seq=source).wait_recv()

    def column(row):
        return jnp.broadcast_to(row, (LANES, LANES)).T

    segs = lax.broadcasted_iota(jnp.int32, (NSEG, LANES), 0)
    count = jnp.zeros((NSEG, LANES), jnp.int32)
    owners = jnp.zeros((1, LANES), jnp.int32)
    for p in range(n_seq):
        for i in range(blocks):
            row = tabs[p, i : i + 1, :]
            count += jnp.where((row >= 0) & (row < segs), 1, 0)
        owners += tabs[p, blocks : blocks + 1, :]
    firsts = jnp.sum(count.astype(f32), axis=1, keepdims=True)
    lengths = jnp.zeros((1, LANES), jnp.int32)
    for g in range(NSEG):
        lengths = jnp.where(lane == g, len_ref[g], lengths)
    lengths = column(lengths.astype(f32))[:NSEG, :1]
    base = lengths - firsts
    for i in range(blocks):
        row = tabs[s, i : i + 1, :]
        start = jnp.sum(jnp.where(segs == row, base, 0.0), axis=0, keepdims=True)
        place = start + (s * shard + i * LANES + lane).astype(f32)
        angle = column(place) * freq_ref[...]
        cosine[i] = jnp.cos(angle)
        sine[i] = jnp.sin(angle)
        qseg[i] = column(row)
    for dz in range(3):
        for c in range(2):
            source = jnp.maximum(z - dz, 0) * 2 + c
            for i in range(blocks):
                row = tabs[source, i : i + 1, :]
                at = (dz * 2 + c) * blocks + i
                kseg[at : at + 1, :] = jnp.where(row < 0, -2, row)
    same = (column(owners) == owners) & (
        lax.broadcasted_iota(jnp.int32, (LANES, LANES), 0)
        < lax.broadcasted_iota(jnp.int32, (LANES, LANES), 1)
    )
    rank = jnp.sum(jnp.where(same, 1, 0), axis=0, keepdims=True)
    limit = jnp.sum(jnp.where(segs == owners, lengths, 0.0), axis=0, keepdims=True).astype(jnp.int32)
    filled = jnp.where(owners >= 0, jnp.clip(limit - BLK * rank, 0, BLK), 0)
    owner_col, filled_col = column(owners), column(filled)
    per = LANES // BLK
    pick = lax.broadcasted_iota(jnp.int32, (per, LANES), 0) == lane // BLK
    for i in range(n_seq * crow // LANES):
        part = slice(i * per, (i + 1) * per)
        who = jnp.sum(jnp.where(pick, owner_col[part], 0), axis=0, keepdims=True)
        many = jnp.sum(jnp.where(pick, filled_col[part], 0), axis=0, keepdims=True)
        at = 6 * blocks + i
        kseg[at : at + 1, :] = jnp.where(lane % BLK < many, who, -2)

    def kv_ref(dz, c, block):
        return keys.at[pl.ds(pl.multiple_of((dz * 2 + c) * shard + block * rows, rows), rows)]

    def kv_up(dz, r):
        return remote(
            kv_ref(dz, core, rel[r]), kv_ref(dz + 1, core, rel[r]), ku_s.at[dz, r], ku_r.at[dz, r], seq=s + 2
        )

    def kv_side(dz, r, c=None):
        ref = kv_ref(dz, core if c is None else c, rel[r])
        return remote(ref, ref, ks_s.at[dz, r], ks_r.at[dz, r], seq=mate)

    def project_kv(r):
        block = rel[r]
        y = jnp.dot(xbuf[block], wkv[...], preferred_element_type=f32)
        a, b = turn(y[:, :HD], cosine[block], sine[block], 1.0)
        at = pl.ds(pl.multiple_of(core * shard + block * rows, rows), rows)
        keys[at, : HD // 2] = a.astype(bf16)
        keys[at, HD // 2 : HD] = b.astype(bf16)
        keys[at, HD:] = y[:, HD:].astype(bf16)

        @pl.when(z < last)
        def _():
            kv_up(0, r).start()

        @pl.when(core == 0)
        def _():
            kv_side(0, r).start()

    def project_q(r):
        block = rel[r]
        y = jnp.dot(xbuf[block], wq[...], preferred_element_type=f32)
        for g in range(2):
            a, b = turn(y[:, g * HD : (g + 1) * HD], cosine[block], sine[block], HD**-0.5)
            q2[block, g * rows : (g + 1) * rows, : HD // 2] = a.astype(bf16)
            q2[block, g * rows : (g + 1) * rows, HD // 2 :] = b.astype(bf16)

    def pass_cache(k):
        @pl.when(z >= k)
        def _():
            owner = s - 2 * k
            cache_up(k - 1, owner).wait_recv()

            if k < last:
                pl.when(z < last)(lambda: cache_up(k, owner).start())

            cache_side(k, owner).start()

        @pl.when(z + k <= last)
        def _():
            owner = s + 2 * k
            cache_down(k - 1, owner).wait_recv()

            if k < last:
                pl.when(z > 0)(lambda: cache_down(k, owner).start())

            cache_side(last + k, owner).start()

    def pass_kv(r):
        @pl.when(z >= 1)
        def _():
            kv_up(0, r).wait_recv()

            @pl.when(z < last)
            def _():
                kv_up(1, r).start()

            kv_side(1, r).start()

    def pass_far(r):
        @pl.when(z >= 2)
        def _():
            kv_up(1, r).wait_recv()

            @pl.when(core == 1)
            def _():
                kv_side(2, r).start()

    tile = shard

    def attend(j, at, causal=False):
        span = pl.ds(pl.multiple_of(at * tile, tile), tile)
        scores = lax.dot_general(
            q2[j], keys[span, :HD], (((1,), (1,)), ((), ())), preferred_element_type=f32
        )
        columns = []
        total = [den[j, g * rows : (g + 1) * rows, :] for g in range(2)]
        for c in range(tile // LANES):
            allowed = qseg[j] == kseg[pl.ds(at * (tile // LANES) + c, 1), :]
            if causal:
                query = j * rows + lax.broadcasted_iota(jnp.int32, (rows, LANES), 0)
                allowed &= c * LANES + lax.broadcasted_iota(jnp.int32, (rows, LANES), 1) <= query
            pair = []
            for g in range(2):
                part = scores[g * rows : (g + 1) * rows, c * LANES : (c + 1) * LANES]
                part = jnp.exp2(jnp.tanh(part * (1.0 / SOFT_CAP)) * (SOFT_CAP * LOG2E))
                part = jnp.where(allowed, part, 0.0)
                total[g] += part
                pair.append(part.astype(bf16))
            columns.append(jnp.concatenate(pair, axis=0))
        for g in range(2):
            den[j, g * rows : (g + 1) * rows, :] = total[g]
        weights = jnp.concatenate(columns, axis=1)
        acc[j] += jnp.dot(weights, keys[span, HD:], preferred_element_type=f32)

    def attend_all(at, causal=False):
        def body(j, carry):
            attend(j, at, causal)
            return carry

        lax.fori_loop(0, 4, body, 0, unroll=4)

    def attend_cache(other):
        attend_all(6 + other)

    loads[0].wait()
    project_kv(0)
    loads[1].wait()
    project_q(0)
    gather_in[0].wait_recv()
    gather[4].start()
    gather_in[2].wait_recv()
    gather[5].start()
    pass_cache(1)
    gather_in[1].wait_recv()
    project_kv(1)
    gather_in[3].wait_recv()
    project_kv(2)
    pass_kv(0)
    project_q(1)
    project_q(2)
    pass_cache(2)
    gather_in[4].wait_recv()
    gather_in[5].wait_recv()
    project_kv(3)
    project_q(3)
    pass_kv(1)
    attend_all(core, True)
    pass_kv(2)
    loads[3].wait()
    cache_side(0, mate).wait_recv()
    attend_cache(z)

    def cache_tiles(k):
        @pl.when(z >= k)
        def _():
            cache_side(k, mate - 2 * k).wait_recv()
            attend_cache(z - k)

        @pl.when(z + k <= last)
        def _():
            cache_side(last + k, mate + 2 * k).wait_recv()
            attend_cache(z + k)

    cache_tiles(1)
    pass_kv(3)
    pass_cache(3)

    @pl.when(core == 1)
    def _():
        for r in range(4):
            kv_side(0, r, 0).wait_recv()
        attend_all(0)

    cache_tiles(2)
    pass_far(0)
    cache_tiles(3)
    pass_far(1)

    @pl.when(z >= 1)
    def _():
        for r in range(4):
            kv_side(1, r, 1 - core).wait_recv()
        attend_all(2)
        attend_all(3)

    pass_far(2)
    pass_far(3)

    @pl.when(z >= 2)
    def _():
        @pl.when(core == 0)
        def _():
            attend_all(4)
            for r in range(4):
                kv_side(2, r, 1).wait_recv()

        attend_all(5)

    loads[2].wait()

    def attended(j):
        present = qseg[j] >= 0
        present = present[:, :1]
        parts = []
        for g in range(2):
            total = jnp.sum(den[j, g * rows : (g + 1) * rows, :], axis=-1, keepdims=True)
            safe = jnp.where(present, total, 1.0)
            value = acc[j, g * rows : (g + 1) * rows, :] / safe
            parts.append(jnp.where(present, value, 0.0).astype(bf16))
        return jnp.concatenate(parts, axis=1)

    def out_copy(m):
        return remote(sbuf.at[m], rbuf.at[m], rs_s.at[m], rs_r.at[m], head=hx if m in (0, 2, 3) else hy)

    def left(a):
        return jnp.dot(a, wo[:, :wide], preferred_element_type=f32)

    def right(a):
        return jnp.dot(a, wo[:, wide:], preferred_element_type=f32)

    a = attended(hd)
    sbuf[0] = left(a).astype(bf16)
    out_copy(0).start()
    sbuf[1] = right(a).astype(bf16)
    out_copy(1).start()
    a = attended(hx)
    sbuf[2] = left(a).astype(bf16)
    out_copy(2).start()
    b = attended(hy)
    sbuf[4] = right(b).astype(bf16)
    out_copy(4).start()
    hold[0] = right(a)
    hold[1] = left(b)
    out_copy(1).wait_recv()
    sbuf[3] = (hold[0] + rbuf[1].astype(f32)).astype(bf16)
    out_copy(3).start()
    out_copy(0).wait_recv()
    sbuf[5] = (hold[1] + rbuf[0].astype(f32)).astype(bf16)
    out_copy(5).start()
    a = attended(h)
    hold[0] = left(a)
    hold[1] = right(a)
    out_copy(2).wait_recv()
    hold[0] += rbuf[2].astype(f32)
    out_copy(4).wait_recv()
    hold[1] += rbuf[4].astype(f32)
    out_copy(5).wait_recv()
    out_copy(3).wait_recv()
    branch_l = hold[0] + rbuf[5].astype(f32)
    branch_r = hold[1] + rbuf[3].astype(f32)
    square = jnp.sum(branch_l * branch_l, axis=-1, keepdims=True) + jnp.sum(
        branch_r * branch_r, axis=-1, keepdims=True
    )
    scale = lax.rsqrt(square / (2 * wide) + EPSILON)
    out_ref[:, :wide] = (
        tok_ref[:, :wide].astype(f32) + branch_l * scale * og_ref[:, :wide]
    ).astype(bf16)
    out_ref[:, wide:] = (
        tok_ref[:, wide:].astype(f32) + branch_r * scale * og_ref[:, wide:]
    ).astype(bf16)

    for i in range(n_seq - 1):
        ints[i].wait_send()
    for copy in gather:
        copy.wait_send()
    for m in range(6):
        out_copy(m).wait_send()
    cache_side(0, s).wait_send()
    for k in range(chips - 1):
        @pl.when((z < last) & (z >= k))
        def _():
            cache_up(k, s - 2 * k).wait_send()

        @pl.when((z > 0) & (z + k <= last))
        def _():
            cache_down(k, s + 2 * k).wait_send()

    for k in range(1, chips):
        @pl.when(z >= k)
        def _():
            cache_side(k, s - 2 * k).wait_send()

        @pl.when(z + k <= last)
        def _():
            cache_side(last + k, s + 2 * k).wait_send()

    for r in range(4):
        @pl.when(z < last)
        def _():
            kv_up(0, r).wait_send()

        @pl.when(core == 0)
        def _():
            kv_side(0, r).wait_send()

        @pl.when(z >= 1)
        def _():
            kv_side(1, r).wait_send()

        @pl.when((z >= 1) & (z < last))
        def _():
            kv_up(1, r).wait_send()

        @pl.when((z >= 2) & (core == 1))
        def _():
            kv_side(2, r).wait_send()


def whole_block(
    tokens, in_gain, out_gain, query_weight, keyval_weight, out_weight, cache_entries, segment_ids,
    cache_lengths, block_owners,
):
    n_seq = lax.axis_size("seq")
    rows, width = tokens.shape
    shard = segment_ids.shape[0]
    crow = cache_entries.shape[1]
    n_keys = 6 * shard + n_seq * crow
    angle = (10000.0 ** (-np.arange(HD // 2) * 2.0 / HD)).astype(np.float32)[None]
    smem = pl.BlockSpec(memory_space=pltpu.SMEM)
    vmem, hbm = pl.BlockSpec(memory_space=pltpu.VMEM), pl.BlockSpec(memory_space=pl.ANY)
    f32, bf16, i32 = jnp.float32, jnp.bfloat16, jnp.int32
    dma = pltpu.SemaphoreType.DMA
    hops = n_seq // 2 - 1
    pairs = [dma((n,)) for n in (n_seq - 1, 6, hops, hops, 2 * hops + 1) for _ in range(2)]
    return pl.pallas_call(
        block_kernel,
        out_shape=jax.ShapeDtypeStruct((rows, width), bf16),
        in_specs=[smem] * 2 + [vmem] * 2 + [hbm] * 7,
        out_specs=vmem,
        scratch_shapes=[
            pltpu.VMEM((n_seq, 8 * -(-(shard // LANES + 1) // 8), LANES), i32),
            pltpu.VMEM((1, width), f32),
            pltpu.VMEM((1, width), f32),
            pltpu.VMEM((4, rows, width), bf16),
            pltpu.VMEM((width, 2 * HD), bf16),
            pltpu.VMEM((width, 2 * HD), bf16),
            pltpu.VMEM((2 * HD, width), bf16),
            pltpu.VMEM((n_keys, 2 * HD), bf16),
            pltpu.VMEM((n_keys // LANES, LANES), i32),
            pltpu.VMEM((4, rows, LANES), i32),
            pltpu.VMEM((4, rows, LANES), f32),
            pltpu.VMEM((4, rows, LANES), f32),
            pltpu.VMEM((4, 2 * rows, HD), bf16),
            pltpu.VMEM((4, 2 * rows, HD), f32),
            pltpu.VMEM((4, 2 * rows, LANES), f32),
            pltpu.VMEM((6, rows, width // 2), bf16),
            pltpu.VMEM((6, rows, width // 2), bf16),
            pltpu.VMEM((2, rows, width // 2), f32),
            dma((6 + shard // LANES,)),
            *pairs,
            dma((2, 4)), dma((2, 4)), dma((3, 4)), dma((3, 4)),
            dma((6,)), dma((6,)),
        ],
        compiler_params=pltpu.CompilerParams(
            collective_id=0, has_side_effects=True, vmem_limit_bytes=56 << 20
        ),
        cost_estimate=pl.CostEstimate(
            flops=2 * shard * (6 * HD * width + 8 * n_keys * HD // 4),
            bytes_accessed=6 * HD * 2 * width,
            transcendentals=4 * shard * n_keys,
        ),
        name="block",
    )(
        cache_lengths, block_owners, jnp.asarray(angle), tokens, segment_ids, in_gain, out_gain,
        query_weight, keyval_weight, out_weight, cache_entries,
    )


def local(
    tokens,
    in_gain,
    out_gain,
    query_weight,
    keyval_weight,
    out_weight,
    cache_entries,
    segment_ids,
    cache_lengths,
    block_owners,
):
    heads_here = query_weight.shape[1] // HD
    group_size = QH // KVH
    seq_size, head_size = lax.axis_size("seq"), lax.axis_size("head")
    seq_index = lax.axis_index("seq")
    head_index = lax.axis_index("head")
    shared_head = head_index * heads_here // group_size
    stream_rows = segment_ids.shape[0]
    normed_own = rms_scale(tokens, in_gain).astype(jnp.bfloat16)
    chunks = [[lax.all_gather(normed_own, "head", axis=0, tiled=True)]]

    cache_own = lax.dynamic_index_in_dim(cache_entries, shared_head, 0, keepdims=False)
    cache_pairs = lax.all_gather(cache_own, "seq", axis=0, tiled=True)

    table = jnp.concatenate([segment_ids, block_owners])[None]
    bits = 0
    while 1 << bits < seq_size:
        step = 1 << bits
        other = lax.ppermute(table, "seq", [(s, s ^ step) for s in range(seq_size)])
        table = jnp.concatenate([table, other], axis=0)
        bits += 1
    for bit in range(bits):
        pieces = table.reshape(-1, 2, 1 << bit, table.shape[-1])
        pieces = jnp.where((seq_index >> bit) % 2 == 1, pieces[:, ::-1], pieces)
        table = pieces.reshape(seq_size, -1)
    seg_all = table[:, :stream_rows].reshape(-1)
    owners = table[:, stream_rows:].reshape(-1)

    seg_range = jnp.arange(NSEG, dtype=jnp.int32)
    earlier = (seg_all[None, :] >= 0) & (seg_all[None, :] < seg_range[:, None])
    firsts = jnp.sum(earlier.astype(jnp.int32), axis=1)
    slots_all = jnp.arange(seg_all.shape[0], dtype=jnp.int32)
    begin = seq_index * stream_rows
    q_seg = lax.dynamic_slice_in_dim(seg_all, begin, stream_rows)
    q_slot = lax.dynamic_slice_in_dim(slots_all, begin, stream_rows)
    matches = (q_seg[:, None] == seg_range[None, :]).astype(jnp.int32)
    positions = jnp.sum(matches * (cache_lengths - firsts)[None, :], axis=1) + q_slot
    angles = positions.astype(jnp.float32)[:, None] * frequencies(HD)[None, :]
    cosine, sine = jnp.cos(angles), jnp.sin(angles)

    block_index = jnp.arange(owners.shape[0], dtype=jnp.int32)
    same = (owners[:, None] == owners[None, :]) & (block_index[None, :] < block_index[:, None])
    block_rank = jnp.sum(same.astype(jnp.int32), axis=1)
    owner_match = (owners[:, None] == seg_range[None, :]).astype(jnp.int32)
    limits = jnp.sum(owner_match * cache_lengths[None, :], axis=1)
    offsets = jnp.arange(BLK, dtype=jnp.int32)
    usable = (owners[:, None] >= 0) & (
        block_rank[:, None] * BLK + offsets[None, :] < limits[:, None]
    )
    cache_seg = jnp.where(usable, owners[:, None], -2).reshape(-1)
    cache_slot = jnp.full((cache_seg.shape[0],), -1, jnp.int32)

    chunk_rows = stream_rows // len(chunks)
    pairs = []
    for at, parts in enumerate(chunks):
        rows = slice(at * chunk_rows, (at + 1) * chunk_rows)
        pairs.append(
            project(
                keyval_kernel, parts, keyval_weight, 2 * HD, shared_head,
                cosine[rows], sine[rows], (chunk_rows, 2 * HD),
            )
        )
    queries = project(
        query_kernel, sum(chunks, []), query_weight, heads_here * HD, jnp.int32(0),
        cosine, sine, (heads_here, stream_rows, HD),
    )

    hops = seq_size // 4

    def onward(array):
        return lax.ppermute(array, "seq", [(s, s + 2) for s in range(seq_size - 2)])

    def sibling(array):
        return lax.ppermute(array, "seq", [(s, s ^ 1) for s in range(seq_size)])

    key_seg = jnp.where(seg_all >= 0, seg_all, -2)

    def shard_ints(shard):
        inside = (shard >= 0) & (shard < seq_size)
        at = jnp.clip(shard, 0, seq_size - 1) * stream_rows
        seg = lax.dynamic_slice_in_dim(key_seg, at, stream_rows)
        return jnp.where(inside, seg, -2), lax.dynamic_slice_in_dim(slots_all, at, stream_rows)

    mate = seq_index + 1 - 2 * (seq_index % 2)
    travelling = [onward(pair) for pair in pairs]
    waiting, waiting_ints = [sibling(pair) for pair in pairs], [shard_ints(mate)]
    totals = attend(
        queries, q_seg, q_slot, pairs + [cache_pairs], [shard_ints(seq_index), (cache_seg, cache_slot)]
    )
    for hop in range(1, hops + 1):
        travelling, totals = lax.optimization_barrier((travelling, totals))
        following = [onward(pair) for pair in travelling] if hop < hops else []
        beside = [sibling(pair) for pair in travelling]
        parts = waiting + travelling
        ints = waiting_ints + [shard_ints(seq_index - 2 * hop)]
        waiting, waiting_ints = beside, [shard_ints(mate - 2 * hop)]
        if hop < hops:
            totals = attend(queries, q_seg, q_slot, parts, ints, totals)
        else:
            attended = attend(
                queries, q_seg, q_slot, parts + waiting, ints + waiting_ints, totals, last=True
            )
        travelling = following

    branch = lax.psum_scatter(
        jnp.dot(attended, out_weight, preferred_element_type=jnp.float32),
        "head",
        scatter_dimension=0,
        tiled=True,
    )
    return (tokens.astype(jnp.float32) + rms_scale(branch, out_gain)).astype(jnp.bfloat16)


def solution(mesh):
    in_specs = (
        P(("seq", "head"), None),
        P(),
        P(),
        P(None, "head"),
        P(),
        P("head", None),
        P(None, "seq", None),
        P("seq"),
        P(),
        P("seq"),
    )
    out_specs = P(("seq", "head"), None)
    fits = mesh.shape["seq"] == 8 and mesh.shape["head"] == 4
    body = whole_block if fits else local
    return jax.shard_map(body, mesh=mesh, in_specs=in_specs, out_specs=out_specs, check_vma=False)
```

```python
import functools
import math

import jax
import jax.numpy as jnp
import numpy as np
from jax import lax
from jax.experimental import pallas as pl
from jax.experimental.pallas import tpu as pltpu
from jax.sharding import PartitionSpec as P

QH = 8
KVH = 4
HD = 256
NSEG = 64
BLK = 16
LANES = 128
EPSILON = 1e-06
SOFT_CAP = 50.0
FAR = 1073741824
VMEM_BYTES = 40 << 20


def rms_scale(matrix, scaling):
    matrix = matrix.astype(jnp.float32)
    mean_square = jnp.mean(matrix * matrix, axis=-1, keepdims=True)
    return matrix * lax.rsqrt(mean_square + EPSILON) * scaling


def frequencies(extent):
    return 10000.0 ** (-(jnp.arange(extent // 2, dtype=jnp.float32) * 2.0 / extent))


def turn(y, cosine, sine, scale):
    half = y.shape[1] // 2
    a, b = y[:, :half], y[:, half:]
    return (a * cosine - b * sine) * scale, (b * cosine + a * sine) * scale


def query_kernel(count, which_ref, cos_ref, sin_ref, w_ref, *rest):
    parts, out_ref = rest[:count], rest[count]
    half = HD // 2
    x = jnp.concatenate([part[...] for part in parts], axis=0)
    for h in range(w_ref.shape[1] // HD):
        y = jnp.dot(x, w_ref[:, h * HD : (h + 1) * HD], preferred_element_type=jnp.float32)
        a, b = turn(y, cos_ref[...], sin_ref[...], HD**-0.5)
        out_ref[h, :, :half] = a.astype(out_ref.dtype)
        out_ref[h, :, half:] = b.astype(out_ref.dtype)


def keyval_kernel(count, which_ref, cos_ref, sin_ref, w_ref, *rest):
    parts, out_ref = rest[:count], rest[count]
    half = HD // 2
    x = jnp.concatenate([part[...] for part in parts], axis=0)
    y = jnp.dot(x, w_ref[...], preferred_element_type=jnp.float32)
    a, b = turn(y[:, :HD], cos_ref[...], sin_ref[...], 1.0)
    out_ref[:, :half] = a.astype(out_ref.dtype)
    out_ref[:, half:HD] = b.astype(out_ref.dtype)
    out_ref[:, HD:] = y[:, HD:].astype(out_ref.dtype)


def project(body, parts, weight, columns, which, cosine, sine, out_shape):
    rows = cosine.shape[0]
    width = weight.shape[0]
    whole = [pl.BlockSpec(x.shape, lambda i, s: (0, 0)) for x in (cosine, sine)]
    return pl.pallas_call(
        functools.partial(body, len(parts)),
        grid_spec=pltpu.PrefetchScalarGridSpec(
            num_scalar_prefetch=1,
            grid=(1,),
            in_specs=whole
            + [pl.BlockSpec((width, columns), lambda i, s: (0, s[0]))]
            + [pl.BlockSpec(x.shape, lambda i, s: (0, 0)) for x in parts],
            out_specs=pl.BlockSpec(out_shape, lambda i, s: (0,) * len(out_shape)),
        ),
        out_shape=jax.ShapeDtypeStruct(out_shape, jnp.bfloat16),
        compiler_params=pltpu.CompilerParams(vmem_limit_bytes=VMEM_BYTES),
        cost_estimate=pl.CostEstimate(
            flops=2 * rows * width * columns,
            bytes_accessed=2 * width * (columns + rows),
            transcendentals=0,
        ),
        name="project",
    )(which.reshape(1), cosine, sine, weight, *parts)


def fold_blocks(
    heads, q_tile, k_tile, touch_ref, q_ref, qseg_ref, qslot_ref, kseg_ref, kslot_ref, parts, acc, den
):
    q_tiles = q_ref.shape[1] // q_tile
    blocks = kseg_ref.shape[0]
    first = 0
    for part in parts:
        here = part.shape[0] // k_tile

        def step(index, carry, part=part, here=here, first=first):
            qi = index // here
            kj = index % here

            @pl.when(touch_ref[qi * blocks + first + kj] > 0)
            def _():
                rows = pl.ds(pl.multiple_of(qi * q_tile, q_tile), q_tile)
                keys = pl.ds(pl.multiple_of(kj * k_tile, k_tile), k_tile)
                allowed = (kseg_ref[first + kj] == qseg_ref[rows, :]) & (
                    kslot_ref[first + kj] <= qslot_ref[rows, :]
                )
                for h in range(heads):
                    scores = lax.dot_general(
                        q_ref[h, rows, :],
                        part[keys, :HD],
                        (((1,), (1,)), ((), ())),
                        preferred_element_type=jnp.float32,
                    )
                    scores = jnp.tanh(scores * (1.0 / SOFT_CAP))
                    weights = jnp.where(
                        allowed, jnp.exp2(scores * (SOFT_CAP * math.log2(math.e))), 0.0
                    )
                    total = weights[:, :LANES]
                    for c in range(1, k_tile // LANES):
                        total += weights[:, c * LANES : (c + 1) * LANES]
                    den[h, rows, :] += total
                    acc[h, rows, :] += jnp.dot(
                        weights.astype(jnp.bfloat16),
                        part[keys, HD:],
                        preferred_element_type=jnp.float32,
                    )

            return carry

        lax.fori_loop(0, q_tiles * here, step, 0)
        first += here


def middle_kernel(heads, q_tile, k_tile, count, touch_ref, q_ref, qseg_ref, qslot_ref, kseg_ref, kslot_ref, *rest):
    parts, (acc_in, den_in, acc, den) = rest[:count], rest[count:]
    acc[...] = acc_in[...]
    den[...] = den_in[...]
    fold_blocks(
        heads, q_tile, k_tile, touch_ref, q_ref, qseg_ref, qslot_ref, kseg_ref, kslot_ref, parts, acc, den
    )


def first_kernel(heads, q_tile, k_tile, count, touch_ref, q_ref, qseg_ref, qslot_ref, kseg_ref, kslot_ref, *rest):
    parts, (acc, den) = rest[:count], rest[count:]
    acc[...] = jnp.zeros_like(acc)
    den[...] = jnp.zeros_like(den)
    fold_blocks(
        heads, q_tile, k_tile, touch_ref, q_ref, qseg_ref, qslot_ref, kseg_ref, kslot_ref, parts, acc, den
    )


def last_kernel(heads, q_tile, k_tile, count, touch_ref, q_ref, qseg_ref, qslot_ref, kseg_ref, kslot_ref, *rest):
    parts, (acc_in, den_in, out_ref, acc, den) = rest[:count], rest[count:]
    acc[...] = acc_in[...]
    den[...] = den_in[...]
    fold_blocks(
        heads, q_tile, k_tile, touch_ref, q_ref, qseg_ref, qslot_ref, kseg_ref, kslot_ref, parts, acc, den
    )
    present = qseg_ref[...] >= 0
    for h in range(heads):
        total = jnp.sum(den[h], axis=-1, keepdims=True)
        safe = jnp.where(present, total, 1.0)
        out_ref[:, h * HD : (h + 1) * HD] = jnp.where(present, acc[h] / safe, 0.0).astype(
            out_ref.dtype
        )


def attend(queries, q_seg, q_slot, parts, ints, totals=None, last=False):
    heads, rows, _ = queries.shape
    k_seg = jnp.concatenate([pair[0] for pair in ints])
    k_slot = jnp.concatenate([pair[1] for pair in ints])
    q_tile = math.gcd(rows, 256)
    k_tile = math.gcd(*[part.shape[0] for part in parts], 512)
    blocks = k_seg.shape[0] // k_tile
    seg_tiles = q_seg.reshape(-1, q_tile)
    lowest = jnp.min(jnp.where(seg_tiles >= 0, seg_tiles, FAR), axis=1)[:, None]
    highest = jnp.max(seg_tiles, axis=1)[:, None]
    latest = jnp.max(q_slot.reshape(-1, q_tile), axis=1)[:, None]
    near = (k_seg[None] >= lowest) & (k_seg[None] <= highest) & (k_slot[None] <= latest)
    touch = jnp.max(near.astype(jnp.int32).reshape(-1, blocks, k_tile), axis=2).reshape(-1)
    operands = [
        touch,
        queries,
        q_seg[:, None],
        q_slot[:, None],
        k_seg.reshape(blocks, 1, k_tile),
        k_slot.reshape(blocks, 1, k_tile),
        *parts,
    ]
    vmem = pl.BlockSpec(memory_space=pltpu.VMEM)
    sums = [
        jax.ShapeDtypeStruct((heads, rows, HD), jnp.float32),
        jax.ShapeDtypeStruct((heads, rows, LANES), jnp.float32),
    ]
    body, out_shape, out_specs, scratch = first_kernel, sums, [vmem, vmem], []
    if totals is not None:
        operands += list(totals)
        body = middle_kernel
    if last:
        body = last_kernel
        out_shape = jax.ShapeDtypeStruct((rows, heads * HD), jnp.bfloat16)
        out_specs = vmem
        scratch = [pltpu.VMEM(s.shape, s.dtype) for s in sums]
    pairs = heads * rows * k_seg.shape[0]
    return pl.pallas_call(
        functools.partial(body, heads, q_tile, k_tile, len(parts)),
        in_specs=[pl.BlockSpec(memory_space=pltpu.SMEM)] + [vmem] * (len(operands) - 1),
        out_specs=out_specs,
        out_shape=out_shape,
        scratch_shapes=scratch,
        compiler_params=pltpu.CompilerParams(vmem_limit_bytes=VMEM_BYTES),
        cost_estimate=pl.CostEstimate(
            flops=4 * pairs * HD, bytes_accessed=4 * HD * k_seg.shape[0], transcendentals=2 * pairs
        ),
        name="attend",
    )(*operands)


MESH = pl.DeviceIdType.MESH
LOG2E = math.log2(math.e)


def block_kernel(
    len_ref, own_ref, freq_ref, tok_ref, seg_hbm, ig_hbm, og_hbm, wq_hbm, wkv_hbm, wo_hbm, cache_hbm,
    out_ref,
    tabs, ig_ref, og_ref, xbuf, wq, wkv, wo, keys, kseg, qseg, cosine, sine, q2, acc, den, abuf, ax, ay, wx, wy, sbuf, rbuf, hold,
    load_sem, int_s, int_r, ag_s, ag_r, cu_s, cu_r, cd_s, cd_r, cs_s, cs_r, ku_s, ku_r, ks_s, ks_r,
    w_s, w_r, at_s, at_r, rs_s, rs_r,
):
    s, h = lax.axis_index("seq"), lax.axis_index("head")
    n_seq = tabs.shape[0]
    chips = n_seq // 2
    z, core = s // 2, s % 2
    mate = s + 1 - 2 * core
    hx, hy, hd = h + 1 - 2 * (h % 2), (h + 2) % 4, 3 - h
    rel = (h, hx, hy, hd)
    rows = tok_ref.shape[0]
    shard = 4 * rows
    half = rows // 2
    wide = out_ref.shape[1] // 2
    crow = cache_hbm.shape[1]
    cbase = 6 * shard
    f32, bf16 = jnp.float32, jnp.bfloat16

    def remote(src, dst, send, recv, seq=None, head=None):
        device = {"seq": s if seq is None else seq, "head": h if head is None else head}
        return pltpu.make_async_remote_copy(
            src_ref=src, dst_ref=dst, send_sem=send, recv_sem=recv, device_id=device, device_id_type=MESH
        )

    barrier = pltpu.get_barrier_semaphore()
    peers = [lax.rem(s + d, n_seq) for d in range(1, n_seq)]
    for peer in peers:
        pl.semaphore_signal(barrier, inc=1, device_id={"seq": peer, "head": h}, device_id_type=MESH)
    for head in (hx, hy):
        pl.semaphore_signal(barrier, inc=1, device_id={"seq": s, "head": head}, device_id_type=MESH)

    kv_cols = pl.ds(pl.multiple_of(h * 2 * HD, 2 * HD), 2 * HD)
    own_cache = keys.at[pl.ds(pl.multiple_of(cbase + s * crow, crow), crow)]
    blocks = shard // LANES
    loads = [
        pltpu.make_async_copy(wkv_hbm.at[:, kv_cols], wkv, load_sem.at[0]),
        pltpu.make_async_copy(wq_hbm, wq, load_sem.at[1]),
        pltpu.make_async_copy(wo_hbm, wo, load_sem.at[2]),
        pltpu.make_async_copy(cache_hbm.at[h], own_cache, load_sem.at[3]),
    ]
    early = [
        pltpu.make_async_copy(ig_hbm, ig_ref.at[0], load_sem.at[4]),
        pltpu.make_async_copy(og_hbm, og_ref.at[0], load_sem.at[5]),
    ] + [
        pltpu.make_async_copy(seg_hbm.at[pl.ds(i * LANES, LANES)], tabs.at[s, i], load_sem.at[6 + i])
        for i in range(blocks)
    ]
    for load in early + loads:
        load.start()

    lane = lax.broadcasted_iota(jnp.int32, (1, LANES), 1)
    owned = jnp.zeros((1, LANES), jnp.int32)
    for i in range(own_ref.shape[0]):
        owned = jnp.where(lane == s * own_ref.shape[0] + i, own_ref[i], owned)
    tabs[s, blocks : blocks + 1, :] = owned
    for load in early:
        load.wait()

    x = tok_ref[...].astype(f32)
    scale = lax.rsqrt(jnp.mean(x * x, axis=-1, keepdims=True) + EPSILON)
    xbuf[h] = (x * scale * ig_ref[...]).astype(bf16)

    pl.semaphore_wait(barrier, n_seq + 1)

    ints = [
        remote(tabs.at[s], tabs.at[s], int_s.at[d], int_r.at[d], seq=peers[d]) for d in range(n_seq - 1)
    ]
    top, bottom = pl.ds(0, half), pl.ds(half, half)

    def token_copy(m, block, part, head):
        ref = xbuf.at[block, part]
        return remote(ref, ref, ag_s.at[m], ag_r.at[m], head=head)

    gather = [
        token_copy(0, h, top, hx), token_copy(1, h, bottom, hx), token_copy(2, h, bottom, hy),
        token_copy(3, h, top, hy), token_copy(4, hx, top, hy), token_copy(5, hy, bottom, hx),
    ]
    gather_in = [
        token_copy(0, hx, top, hx), token_copy(1, hx, bottom, hx), token_copy(2, hy, bottom, hy),
        token_copy(3, hy, top, hy), token_copy(4, hd, top, hy), token_copy(5, hd, bottom, hx),
    ]

    def cache_ref(owner):
        return keys.at[pl.ds(pl.multiple_of(cbase + owner * crow, crow), crow)]

    def cache_up(k, owner):
        src = cache_hbm.at[h] if k == 0 else cache_ref(owner)
        return remote(src, cache_ref(owner), cu_s.at[k], cu_r.at[k], seq=s + 2)

    def cache_down(k, owner):
        src = cache_hbm.at[h] if k == 0 else cache_ref(owner)
        return remote(src, cache_ref(owner), cd_s.at[k], cd_r.at[k], seq=s - 2)

    def cache_side(i, owner):
        src = cache_hbm.at[h] if i == 0 else cache_ref(owner)
        return remote(src, cache_ref(owner), cs_s.at[i], cs_r.at[i], seq=mate)

    part_rows = wx.shape[0] // 2

    def weight_copy(m, c):
        span = pl.ds(pl.multiple_of(c * part_rows, part_rows), part_rows)
        there = (wx, wy)[m % 2].at[span]
        if m < 2:
            columns = pl.ds(m * wide, wide)
            return remote(wo_hbm.at[span, columns], there, w_s.at[m], w_r.at[m], head=(hx, hy)[m])
        return remote(there, there, w_s.at[m], w_r.at[m], seq=mate)

    last = chips - 1
    for i in range(n_seq - 1):
        ints[i].start()
    for m in (0, 2, 1, 3):
        gather[m].start()

    @pl.when(z < last)
    def _():
        cache_up(0, s).start()

    @pl.when(z > 0)
    def _():
        cache_down(0, s).start()

    cache_side(0, s).start()

    acc[...] = jnp.zeros_like(acc)
    den[...] = jnp.zeros_like(den)
    for d in range(n_seq - 1):
        source = lax.rem(s + n_seq - 1 - d, n_seq)
        remote(tabs.at[source], tabs.at[source], int_s.at[d], int_r.at[d], seq=source).wait_recv()

    def column(row):
        return jnp.broadcast_to(row, (LANES, LANES)).T

    segs = lax.broadcasted_iota(jnp.int32, (NSEG, LANES), 0)
    count = jnp.zeros((NSEG, LANES), jnp.int32)
    owners = jnp.zeros((1, LANES), jnp.int32)
    for p in range(n_seq):
        for i in range(blocks):
            row = tabs[p, i : i + 1, :]
            count += jnp.where((row >= 0) & (row < segs), 1, 0)
        owners += tabs[p, blocks : blocks + 1, :]
    firsts = jnp.sum(count.astype(f32), axis=1, keepdims=True)
    lengths = jnp.zeros((1, LANES), jnp.int32)
    for g in range(NSEG):
        lengths = jnp.where(lane == g, len_ref[g], lengths)
    lengths = column(lengths.astype(f32))[:NSEG, :1]
    base = lengths - firsts
    for i in range(blocks):
        row = tabs[s, i : i + 1, :]
        start = jnp.sum(jnp.where(segs == row, base, 0.0), axis=0, keepdims=True)
        place = start + (s * shard + i * LANES + lane).astype(f32)
        angle = column(place) * freq_ref[...]
        cosine[i] = jnp.cos(angle)
        sine[i] = jnp.sin(angle)
        qseg[i] = column(row)
    for dz in range(3):
        for c in range(2):
            source = jnp.maximum(z - dz, 0) * 2 + c
            for i in range(blocks):
                row = tabs[source, i : i + 1, :]
                at = (dz * 2 + c) * blocks + i
                kseg[at : at + 1, :] = jnp.where(row < 0, -2, row)
    same = (column(owners) == owners) & (
        lax.broadcasted_iota(jnp.int32, (LANES, LANES), 0)
        < lax.broadcasted_iota(jnp.int32, (LANES, LANES), 1)
    )
    rank = jnp.sum(jnp.where(same, 1, 0), axis=0, keepdims=True)
    limit = jnp.sum(jnp.where(segs == owners, lengths, 0.0), axis=0, keepdims=True).astype(jnp.int32)
    filled = jnp.where(owners >= 0, jnp.clip(limit - BLK * rank, 0, BLK), 0)
    owner_col, filled_col = column(owners), column(filled)
    per = LANES // BLK
    pick = lax.broadcasted_iota(jnp.int32, (per, LANES), 0) == lane // BLK
    for i in range(n_seq * crow // LANES):
        part = slice(i * per, (i + 1) * per)
        who = jnp.sum(jnp.where(pick, owner_col[part], 0), axis=0, keepdims=True)
        many = jnp.sum(jnp.where(pick, filled_col[part], 0), axis=0, keepdims=True)
        at = 6 * blocks + i
        kseg[at : at + 1, :] = jnp.where(lane % BLK < many, who, -2)

    def kv_ref(dz, c, block):
        return keys.at[pl.ds(pl.multiple_of((dz * 2 + c) * shard + block * rows, rows), rows)]

    def kv_up(dz, r):
        return remote(
            kv_ref(dz, core, rel[r]), kv_ref(dz + 1, core, rel[r]), ku_s.at[dz, r], ku_r.at[dz, r], seq=s + 2
        )

    def kv_side(dz, r, c=None):
        ref = kv_ref(dz, core if c is None else c, rel[r])
        return remote(ref, ref, ks_s.at[dz, r], ks_r.at[dz, r], seq=mate)

    def project_kv(r):
        block = rel[r]
        y = jnp.dot(xbuf[block], wkv[...], preferred_element_type=f32)
        a, b = turn(y[:, :HD], cosine[block], sine[block], 1.0)
        at = pl.ds(pl.multiple_of(core * shard + block * rows, rows), rows)
        keys[at, : HD // 2] = a.astype(bf16)
        keys[at, HD // 2 : HD] = b.astype(bf16)
        keys[at, HD:] = y[:, HD:].astype(bf16)

        @pl.when(z < last)
        def _():
            kv_up(0, r).start()

        @pl.when(core == 0)
        def _():
            kv_side(0, r).start()

    def project_q(r):
        block = rel[r]
        y = jnp.dot(xbuf[block], wq[...], preferred_element_type=f32)
        for g in range(2):
            a, b = turn(y[:, g * HD : (g + 1) * HD], cosine[block], sine[block], HD**-0.5)
            q2[block, g * rows : (g + 1) * rows, : HD // 2] = a.astype(bf16)
            q2[block, g * rows : (g + 1) * rows, HD // 2 :] = b.astype(bf16)

    def pass_cache(k):
        @pl.when(z >= k)
        def _():
            owner = s - 2 * k
            cache_up(k - 1, owner).wait_recv()

            if k < last:
                pl.when(z < last)(lambda: cache_up(k, owner).start())

            cache_side(k, owner).start()

        @pl.when(z + k <= last)
        def _():
            owner = s + 2 * k
            cache_down(k - 1, owner).wait_recv()

            if k < last:
                pl.when(z > 0)(lambda: cache_down(k, owner).start())

            cache_side(last + k, owner).start()

    def pass_kv(r):
        @pl.when(z >= 1)
        def _():
            kv_up(0, r).wait_recv()

            @pl.when(z < last)
            def _():
                kv_up(1, r).start()

            kv_side(1, r).start()

    def pass_far(r):
        @pl.when(z >= 2)
        def _():
            kv_up(1, r).wait_recv()

            @pl.when(core == 1)
            def _():
                kv_side(2, r).start()

    tile = shard

    def attend(j, at, causal=False):
        span = pl.ds(pl.multiple_of(at * tile, tile), tile)
        scores = lax.dot_general(
            q2[j], keys[span, :HD], (((1,), (1,)), ((), ())), preferred_element_type=f32
        )
        columns = []
        total = [den[j, g * rows : (g + 1) * rows, :] for g in range(2)]
        for c in range(tile // LANES):
            allowed = qseg[j] == kseg[pl.ds(at * (tile // LANES) + c, 1), :]
            if causal:
                query = j * rows + lax.broadcasted_iota(jnp.int32, (rows, LANES), 0)
                allowed &= c * LANES + lax.broadcasted_iota(jnp.int32, (rows, LANES), 1) <= query
            pair = []
            for g in range(2):
                part = scores[g * rows : (g + 1) * rows, c * LANES : (c + 1) * LANES]
                part = jnp.exp2(jnp.tanh(part * (1.0 / SOFT_CAP)) * (SOFT_CAP * LOG2E))
                part = jnp.where(allowed, part, 0.0)
                total[g] += part
                pair.append(part.astype(bf16))
            columns.append(jnp.concatenate(pair, axis=0))
        for g in range(2):
            den[j, g * rows : (g + 1) * rows, :] = total[g]
        weights = jnp.concatenate(columns, axis=1)
        acc[j] += jnp.dot(weights, keys[span, HD:], preferred_element_type=f32)

    def attend_all(at, causal=False):
        def body(j, carry):
            attend(j, at, causal)
            return carry

        lax.fori_loop(0, 4, body, 0, unroll=4)

    def attend_cache(other):
        attend_all(6 + other)

    loads[0].wait()
    project_kv(0)
    loads[1].wait()
    project_q(0)
    gather_in[0].wait_recv()
    gather[4].start()
    gather_in[2].wait_recv()
    gather[5].start()
    pass_cache(1)
    gather_in[1].wait_recv()
    project_kv(1)
    gather_in[3].wait_recv()
    project_kv(2)
    pass_kv(0)
    project_q(1)
    project_q(2)
    pass_cache(2)
    gather_in[4].wait_recv()
    gather_in[5].wait_recv()
    project_kv(3)
    weight_copy(0, core).start()
    weight_copy(1, core).start()
    project_q(3)
    pass_kv(1)
    attend_all(core, True)
    pass_kv(2)
    loads[3].wait()
    cache_side(0, mate).wait_recv()
    attend_cache(z)

    def cache_tiles(k):
        @pl.when(z >= k)
        def _():
            cache_side(k, mate - 2 * k).wait_recv()
            attend_cache(z - k)

        @pl.when(z + k <= last)
        def _():
            cache_side(last + k, mate + 2 * k).wait_recv()
            attend_cache(z + k)

    cache_tiles(1)
    pass_kv(3)
    pass_cache(3)

    @pl.when(core == 1)
    def _():
        for r in range(4):
            kv_side(0, r, 0).wait_recv()
        attend_all(0)

    cache_tiles(2)
    pass_far(0)
    cache_tiles(3)
    pass_far(1)

    @pl.when(z >= 1)
    def _():
        for r in range(4):
            kv_side(1, r, 1 - core).wait_recv()
        attend_all(2)
        attend_all(3)

    for m in range(2):
        weight_copy(m, core).wait_recv()
        weight_copy(m + 2, core).start()
    pass_far(2)
    pass_far(3)
    loads[2].wait()

    @pl.when((z >= 2) & (core == 0))
    def _():
        for r in range(4):
            kv_side(2, r, 1).wait_recv()

    def attended(j):
        present = qseg[j] >= 0
        present = present[:, :1]
        parts = []
        for g in range(2):
            total = jnp.sum(den[j, g * rows : (g + 1) * rows, :], axis=-1, keepdims=True)
            safe = jnp.where(present, total, 1.0)
            value = acc[j, g * rows : (g + 1) * rows, :] / safe
            parts.append(jnp.where(present, value, 0.0).astype(bf16))
        return jnp.concatenate(parts, axis=1)

    def finish(j):
        @pl.when(z >= 2)
        def _():
            @pl.when(core == 0)
            def _():
                attend(j, 4)

            attend(j, 5)

        abuf[j] = attended(j)

    def rows_copy(m, block):
        there = (ax, ay)[m % 2].at[m // 2]
        return remote(abuf.at[block], there, at_s.at[m], at_r.at[m], head=(hx, hy)[m % 2])

    def sum_copy(m):
        return remote(sbuf.at[m], rbuf.at[m], rs_s.at[m], rs_r.at[m], head=(hy, hx)[m])

    def left(a, weight=None):
        return jnp.dot(a, wo[:, :wide] if weight is None else weight[...], preferred_element_type=f32)

    def right(a, weight=None):
        return jnp.dot(a, wo[:, wide:] if weight is None else weight[...], preferred_element_type=f32)

    sent = (hd, hd, hx, hy)
    finish(hd)
    rows_copy(0, hd).start()
    rows_copy(1, hd).start()
    finish(hx)
    rows_copy(2, hx).start()
    finish(hy)
    rows_copy(3, hy).start()
    for m in range(2):
        weight_copy(m + 2, 1 - core).wait_recv()
    rows_copy(0, hd).wait_recv()
    sbuf[0] = (left(abuf[hy]) + left(ax[0], wx)).astype(bf16)
    sum_copy(0).start()
    rows_copy(1, hd).wait_recv()
    sbuf[1] = (right(abuf[hx]) + right(ay[0], wy)).astype(bf16)
    sum_copy(1).start()
    finish(h)
    hold[0] = left(abuf[h])
    hold[1] = right(abuf[h])
    rows_copy(2, hx).wait_recv()
    hold[0] += left(ax[1], wx)
    rows_copy(3, hy).wait_recv()
    hold[1] += right(ay[1], wy)
    sum_copy(0).wait_recv()
    branch_l = hold[0] + rbuf[0].astype(f32)
    sum_copy(1).wait_recv()
    branch_r = hold[1] + rbuf[1].astype(f32)
    square = jnp.sum(branch_l * branch_l, axis=-1, keepdims=True) + jnp.sum(
        branch_r * branch_r, axis=-1, keepdims=True
    )
    scale = lax.rsqrt(square / (2 * wide) + EPSILON)
    out_ref[:, :wide] = (
        tok_ref[:, :wide].astype(f32) + branch_l * scale * og_ref[:, :wide]
    ).astype(bf16)
    out_ref[:, wide:] = (
        tok_ref[:, wide:].astype(f32) + branch_r * scale * og_ref[:, wide:]
    ).astype(bf16)

    for i in range(n_seq - 1):
        ints[i].wait_send()
    for copy in gather:
        copy.wait_send()
    for m in range(4):
        rows_copy(m, sent[m]).wait_send()
        weight_copy(m, core).wait_send()
    for m in range(2):
        sum_copy(m).wait_send()
    cache_side(0, s).wait_send()
    for k in range(chips - 1):
        @pl.when((z < last) & (z >= k))
        def _():
            cache_up(k, s - 2 * k).wait_send()

        @pl.when((z > 0) & (z + k <= last))
        def _():
            cache_down(k, s + 2 * k).wait_send()

    for k in range(1, chips):
        @pl.when(z >= k)
        def _():
            cache_side(k, s - 2 * k).wait_send()

        @pl.when(z + k <= last)
        def _():
            cache_side(last + k, s + 2 * k).wait_send()

    for r in range(4):
        @pl.when(z < last)
        def _():
            kv_up(0, r).wait_send()

        @pl.when(core == 0)
        def _():
            kv_side(0, r).wait_send()

        @pl.when(z >= 1)
        def _():
            kv_side(1, r).wait_send()

        @pl.when((z >= 1) & (z < last))
        def _():
            kv_up(1, r).wait_send()

        @pl.when((z >= 2) & (core == 1))
        def _():
            kv_side(2, r).wait_send()


def whole_block(
    tokens, in_gain, out_gain, query_weight, keyval_weight, out_weight, cache_entries, segment_ids,
    cache_lengths, block_owners,
):
    n_seq = lax.axis_size("seq")
    rows, width = tokens.shape
    shard = segment_ids.shape[0]
    crow = cache_entries.shape[1]
    n_keys = 6 * shard + n_seq * crow
    angle = (10000.0 ** (-np.arange(HD // 2) * 2.0 / HD)).astype(np.float32)[None]
    smem = pl.BlockSpec(memory_space=pltpu.SMEM)
    vmem, hbm = pl.BlockSpec(memory_space=pltpu.VMEM), pl.BlockSpec(memory_space=pl.ANY)
    f32, bf16, i32 = jnp.float32, jnp.bfloat16, jnp.int32
    dma = pltpu.SemaphoreType.DMA
    hops = n_seq // 2 - 1
    pairs = [dma((n,)) for n in (n_seq - 1, 6, hops, hops, 2 * hops + 1) for _ in range(2)]
    return pl.pallas_call(
        block_kernel,
        out_shape=jax.ShapeDtypeStruct((rows, width), bf16),
        in_specs=[smem] * 2 + [vmem] * 2 + [hbm] * 7,
        out_specs=vmem,
        scratch_shapes=[
            pltpu.VMEM((n_seq, 8 * -(-(shard // LANES + 1) // 8), LANES), i32),
            pltpu.VMEM((1, width), f32),
            pltpu.VMEM((1, width), f32),
            pltpu.VMEM((4, rows, width), bf16),
            pltpu.VMEM((width, 2 * HD), bf16),
            pltpu.VMEM((width, 2 * HD), bf16),
            pltpu.VMEM((2 * HD, width), bf16),
            pltpu.VMEM((n_keys, 2 * HD), bf16),
            pltpu.VMEM((n_keys // LANES, LANES), i32),
            pltpu.VMEM((4, rows, LANES), i32),
            pltpu.VMEM((4, rows, LANES), f32),
            pltpu.VMEM((4, rows, LANES), f32),
            pltpu.VMEM((4, 2 * rows, HD), bf16),
            pltpu.VMEM((4, 2 * rows, HD), f32),
            pltpu.VMEM((4, 2 * rows, LANES), f32),
            pltpu.VMEM((4, rows, 2 * HD), bf16),
            pltpu.VMEM((2, rows, 2 * HD), bf16),
            pltpu.VMEM((2, rows, 2 * HD), bf16),
            pltpu.VMEM((2 * HD, width // 2), bf16),
            pltpu.VMEM((2 * HD, width // 2), bf16),
            pltpu.VMEM((2, rows, width // 2), bf16),
            pltpu.VMEM((2, rows, width // 2), bf16),
            pltpu.VMEM((2, rows, width // 2), f32),
            dma((6 + shard // LANES,)),
            *pairs,
            dma((2, 4)), dma((2, 4)), dma((3, 4)), dma((3, 4)),
            dma((4,)), dma((4,)), dma((4,)), dma((4,)), dma((2,)), dma((2,)),
        ],
        compiler_params=pltpu.CompilerParams(
            collective_id=0, has_side_effects=True, vmem_limit_bytes=56 << 20
        ),
        cost_estimate=pl.CostEstimate(
            flops=2 * shard * (6 * HD * width + 8 * n_keys * HD // 4),
            bytes_accessed=6 * HD * 2 * width,
            transcendentals=4 * shard * n_keys,
        ),
        name="block",
    )(
        cache_lengths, block_owners, jnp.asarray(angle), tokens, segment_ids, in_gain, out_gain,
        query_weight, keyval_weight, out_weight, cache_entries,
    )


def local(
    tokens,
    in_gain,
    out_gain,
    query_weight,
    keyval_weight,
    out_weight,
    cache_entries,
    segment_ids,
    cache_lengths,
    block_owners,
):
    heads_here = query_weight.shape[1] // HD
    group_size = QH // KVH
    seq_size, head_size = lax.axis_size("seq"), lax.axis_size("head")
    seq_index = lax.axis_index("seq")
    head_index = lax.axis_index("head")
    shared_head = head_index * heads_here // group_size
    stream_rows = segment_ids.shape[0]
    normed_own = rms_scale(tokens, in_gain).astype(jnp.bfloat16)
    chunks = [[lax.all_gather(normed_own, "head", axis=0, tiled=True)]]

    cache_own = lax.dynamic_index_in_dim(cache_entries, shared_head, 0, keepdims=False)
    cache_pairs = lax.all_gather(cache_own, "seq", axis=0, tiled=True)

    table = jnp.concatenate([segment_ids, block_owners])[None]
    bits = 0
    while 1 << bits < seq_size:
        step = 1 << bits
        other = lax.ppermute(table, "seq", [(s, s ^ step) for s in range(seq_size)])
        table = jnp.concatenate([table, other], axis=0)
        bits += 1
    for bit in range(bits):
        pieces = table.reshape(-1, 2, 1 << bit, table.shape[-1])
        pieces = jnp.where((seq_index >> bit) % 2 == 1, pieces[:, ::-1], pieces)
        table = pieces.reshape(seq_size, -1)
    seg_all = table[:, :stream_rows].reshape(-1)
    owners = table[:, stream_rows:].reshape(-1)

    seg_range = jnp.arange(NSEG, dtype=jnp.int32)
    earlier = (seg_all[None, :] >= 0) & (seg_all[None, :] < seg_range[:, None])
    firsts = jnp.sum(earlier.astype(jnp.int32), axis=1)
    slots_all = jnp.arange(seg_all.shape[0], dtype=jnp.int32)
    begin = seq_index * stream_rows
    q_seg = lax.dynamic_slice_in_dim(seg_all, begin, stream_rows)
    q_slot = lax.dynamic_slice_in_dim(slots_all, begin, stream_rows)
    matches = (q_seg[:, None] == seg_range[None, :]).astype(jnp.int32)
    positions = jnp.sum(matches * (cache_lengths - firsts)[None, :], axis=1) + q_slot
    angles = positions.astype(jnp.float32)[:, None] * frequencies(HD)[None, :]
    cosine, sine = jnp.cos(angles), jnp.sin(angles)

    block_index = jnp.arange(owners.shape[0], dtype=jnp.int32)
    same = (owners[:, None] == owners[None, :]) & (block_index[None, :] < block_index[:, None])
    block_rank = jnp.sum(same.astype(jnp.int32), axis=1)
    owner_match = (owners[:, None] == seg_range[None, :]).astype(jnp.int32)
    limits = jnp.sum(owner_match * cache_lengths[None, :], axis=1)
    offsets = jnp.arange(BLK, dtype=jnp.int32)
    usable = (owners[:, None] >= 0) & (
        block_rank[:, None] * BLK + offsets[None, :] < limits[:, None]
    )
    cache_seg = jnp.where(usable, owners[:, None], -2).reshape(-1)
    cache_slot = jnp.full((cache_seg.shape[0],), -1, jnp.int32)

    chunk_rows = stream_rows // len(chunks)
    pairs = []
    for at, parts in enumerate(chunks):
        rows = slice(at * chunk_rows, (at + 1) * chunk_rows)
        pairs.append(
            project(
                keyval_kernel, parts, keyval_weight, 2 * HD, shared_head,
                cosine[rows], sine[rows], (chunk_rows, 2 * HD),
            )
        )
    queries = project(
        query_kernel, sum(chunks, []), query_weight, heads_here * HD, jnp.int32(0),
        cosine, sine, (heads_here, stream_rows, HD),
    )

    hops = seq_size // 4

    def onward(array):
        return lax.ppermute(array, "seq", [(s, s + 2) for s in range(seq_size - 2)])

    def sibling(array):
        return lax.ppermute(array, "seq", [(s, s ^ 1) for s in range(seq_size)])

    key_seg = jnp.where(seg_all >= 0, seg_all, -2)

    def shard_ints(shard):
        inside = (shard >= 0) & (shard < seq_size)
        at = jnp.clip(shard, 0, seq_size - 1) * stream_rows
        seg = lax.dynamic_slice_in_dim(key_seg, at, stream_rows)
        return jnp.where(inside, seg, -2), lax.dynamic_slice_in_dim(slots_all, at, stream_rows)

    mate = seq_index + 1 - 2 * (seq_index % 2)
    travelling = [onward(pair) for pair in pairs]
    waiting, waiting_ints = [sibling(pair) for pair in pairs], [shard_ints(mate)]
    totals = attend(
        queries, q_seg, q_slot, pairs + [cache_pairs], [shard_ints(seq_index), (cache_seg, cache_slot)]
    )
    for hop in range(1, hops + 1):
        travelling, totals = lax.optimization_barrier((travelling, totals))
        following = [onward(pair) for pair in travelling] if hop < hops else []
        beside = [sibling(pair) for pair in travelling]
        parts = waiting + travelling
        ints = waiting_ints + [shard_ints(seq_index - 2 * hop)]
        waiting, waiting_ints = beside, [shard_ints(mate - 2 * hop)]
        if hop < hops:
            totals = attend(queries, q_seg, q_slot, parts, ints, totals)
        else:
            attended = attend(
                queries, q_seg, q_slot, parts + waiting, ints + waiting_ints, totals, last=True
            )
        travelling = following

    branch = lax.psum_scatter(
        jnp.dot(attended, out_weight, preferred_element_type=jnp.float32),
        "head",
        scatter_dimension=0,
        tiled=True,
    )
    return (tokens.astype(jnp.float32) + rms_scale(branch, out_gain)).astype(jnp.bfloat16)


def solution(mesh):
    in_specs = (
        P(("seq", "head"), None),
        P(),
        P(),
        P(None, "head"),
        P(),
        P("head", None),
        P(None, "seq", None),
        P("seq"),
        P(),
        P("seq"),
    )
    out_specs = P(("seq", "head"), None)
    fits = mesh.shape["seq"] == 8 and mesh.shape["head"] == 4
    body = whole_block if fits else local
    return jax.shard_map(body, mesh=mesh, in_specs=in_specs, out_specs=out_specs, check_vma=False)
```

```python
import functools
import math

import jax
import jax.numpy as jnp
import numpy as np
from jax import lax
from jax.experimental import pallas as pl
from jax.experimental.pallas import tpu as pltpu
from jax.sharding import PartitionSpec as P

QH = 8
KVH = 4
HD = 256
NSEG = 64
BLK = 16
LANES = 128
EPSILON = 1e-06
SOFT_CAP = 50.0
FAR = 1073741824
VMEM_BYTES = 40 << 20


def rms_scale(matrix, scaling):
    matrix = matrix.astype(jnp.float32)
    mean_square = jnp.mean(matrix * matrix, axis=-1, keepdims=True)
    return matrix * lax.rsqrt(mean_square + EPSILON) * scaling


def frequencies(extent):
    return 10000.0 ** (-(jnp.arange(extent // 2, dtype=jnp.float32) * 2.0 / extent))


def turn(y, cosine, sine, scale):
    half = y.shape[1] // 2
    a, b = y[:, :half], y[:, half:]
    return (a * cosine - b * sine) * scale, (b * cosine + a * sine) * scale


def query_kernel(count, which_ref, cos_ref, sin_ref, w_ref, *rest):
    parts, out_ref = rest[:count], rest[count]
    half = HD // 2
    x = jnp.concatenate([part[...] for part in parts], axis=0)
    for h in range(w_ref.shape[1] // HD):
        y = jnp.dot(x, w_ref[:, h * HD : (h + 1) * HD], preferred_element_type=jnp.float32)
        a, b = turn(y, cos_ref[...], sin_ref[...], HD**-0.5)
        out_ref[h, :, :half] = a.astype(out_ref.dtype)
        out_ref[h, :, half:] = b.astype(out_ref.dtype)


def keyval_kernel(count, which_ref, cos_ref, sin_ref, w_ref, *rest):
    parts, out_ref = rest[:count], rest[count]
    half = HD // 2
    x = jnp.concatenate([part[...] for part in parts], axis=0)
    y = jnp.dot(x, w_ref[...], preferred_element_type=jnp.float32)
    a, b = turn(y[:, :HD], cos_ref[...], sin_ref[...], 1.0)
    out_ref[:, :half] = a.astype(out_ref.dtype)
    out_ref[:, half:HD] = b.astype(out_ref.dtype)
    out_ref[:, HD:] = y[:, HD:].astype(out_ref.dtype)


def project(body, parts, weight, columns, which, cosine, sine, out_shape):
    rows = cosine.shape[0]
    width = weight.shape[0]
    whole = [pl.BlockSpec(x.shape, lambda i, s: (0, 0)) for x in (cosine, sine)]
    return pl.pallas_call(
        functools.partial(body, len(parts)),
        grid_spec=pltpu.PrefetchScalarGridSpec(
            num_scalar_prefetch=1,
            grid=(1,),
            in_specs=whole
            + [pl.BlockSpec((width, columns), lambda i, s: (0, s[0]))]
            + [pl.BlockSpec(x.shape, lambda i, s: (0, 0)) for x in parts],
            out_specs=pl.BlockSpec(out_shape, lambda i, s: (0,) * len(out_shape)),
        ),
        out_shape=jax.ShapeDtypeStruct(out_shape, jnp.bfloat16),
        compiler_params=pltpu.CompilerParams(vmem_limit_bytes=VMEM_BYTES),
        cost_estimate=pl.CostEstimate(
            flops=2 * rows * width * columns,
            bytes_accessed=2 * width * (columns + rows),
            transcendentals=0,
        ),
        name="project",
    )(which.reshape(1), cosine, sine, weight, *parts)


def fold_blocks(
    heads, q_tile, k_tile, touch_ref, q_ref, qseg_ref, qslot_ref, kseg_ref, kslot_ref, parts, acc, den
):
    q_tiles = q_ref.shape[1] // q_tile
    blocks = kseg_ref.shape[0]
    first = 0
    for part in parts:
        here = part.shape[0] // k_tile

        def step(index, carry, part=part, here=here, first=first):
            qi = index // here
            kj = index % here

            @pl.when(touch_ref[qi * blocks + first + kj] > 0)
            def _():
                rows = pl.ds(pl.multiple_of(qi * q_tile, q_tile), q_tile)
                keys = pl.ds(pl.multiple_of(kj * k_tile, k_tile), k_tile)
                allowed = (kseg_ref[first + kj] == qseg_ref[rows, :]) & (
                    kslot_ref[first + kj] <= qslot_ref[rows, :]
                )
                for h in range(heads):
                    scores = lax.dot_general(
                        q_ref[h, rows, :],
                        part[keys, :HD],
                        (((1,), (1,)), ((), ())),
                        preferred_element_type=jnp.float32,
                    )
                    scores = jnp.tanh(scores * (1.0 / SOFT_CAP))
                    weights = jnp.where(
                        allowed, jnp.exp2(scores * (SOFT_CAP * math.log2(math.e))), 0.0
                    )
                    total = weights[:, :LANES]
                    for c in range(1, k_tile // LANES):
                        total += weights[:, c * LANES : (c + 1) * LANES]
                    den[h, rows, :] += total
                    acc[h, rows, :] += jnp.dot(
                        weights.astype(jnp.bfloat16),
                        part[keys, HD:],
                        preferred_element_type=jnp.float32,
                    )

            return carry

        lax.fori_loop(0, q_tiles * here, step, 0)
        first += here


def middle_kernel(heads, q_tile, k_tile, count, touch_ref, q_ref, qseg_ref, qslot_ref, kseg_ref, kslot_ref, *rest):
    parts, (acc_in, den_in, acc, den) = rest[:count], rest[count:]
    acc[...] = acc_in[...]
    den[...] = den_in[...]
    fold_blocks(
        heads, q_tile, k_tile, touch_ref, q_ref, qseg_ref, qslot_ref, kseg_ref, kslot_ref, parts, acc, den
    )


def first_kernel(heads, q_tile, k_tile, count, touch_ref, q_ref, qseg_ref, qslot_ref, kseg_ref, kslot_ref, *rest):
    parts, (acc, den) = rest[:count], rest[count:]
    acc[...] = jnp.zeros_like(acc)
    den[...] = jnp.zeros_like(den)
    fold_blocks(
        heads, q_tile, k_tile, touch_ref, q_ref, qseg_ref, qslot_ref, kseg_ref, kslot_ref, parts, acc, den
    )


def last_kernel(heads, q_tile, k_tile, count, touch_ref, q_ref, qseg_ref, qslot_ref, kseg_ref, kslot_ref, *rest):
    parts, (acc_in, den_in, out_ref, acc, den) = rest[:count], rest[count:]
    acc[...] = acc_in[...]
    den[...] = den_in[...]
    fold_blocks(
        heads, q_tile, k_tile, touch_ref, q_ref, qseg_ref, qslot_ref, kseg_ref, kslot_ref, parts, acc, den
    )
    present = qseg_ref[...] >= 0
    for h in range(heads):
        total = jnp.sum(den[h], axis=-1, keepdims=True)
        safe = jnp.where(present, total, 1.0)
        out_ref[:, h * HD : (h + 1) * HD] = jnp.where(present, acc[h] / safe, 0.0).astype(
            out_ref.dtype
        )


def attend(queries, q_seg, q_slot, parts, ints, totals=None, last=False):
    heads, rows, _ = queries.shape
    k_seg = jnp.concatenate([pair[0] for pair in ints])
    k_slot = jnp.concatenate([pair[1] for pair in ints])
    q_tile = math.gcd(rows, 256)
    k_tile = math.gcd(*[part.shape[0] for part in parts], 512)
    blocks = k_seg.shape[0] // k_tile
    seg_tiles = q_seg.reshape(-1, q_tile)
    lowest = jnp.min(jnp.where(seg_tiles >= 0, seg_tiles, FAR), axis=1)[:, None]
    highest = jnp.max(seg_tiles, axis=1)[:, None]
    latest = jnp.max(q_slot.reshape(-1, q_tile), axis=1)[:, None]
    near = (k_seg[None] >= lowest) & (k_seg[None] <= highest) & (k_slot[None] <= latest)
    touch = jnp.max(near.astype(jnp.int32).reshape(-1, blocks, k_tile), axis=2).reshape(-1)
    operands = [
        touch,
        queries,
        q_seg[:, None],
        q_slot[:, None],
        k_seg.reshape(blocks, 1, k_tile),
        k_slot.reshape(blocks, 1, k_tile),
        *parts,
    ]
    vmem = pl.BlockSpec(memory_space=pltpu.VMEM)
    sums = [
        jax.ShapeDtypeStruct((heads, rows, HD), jnp.float32),
        jax.ShapeDtypeStruct((heads, rows, LANES), jnp.float32),
    ]
    body, out_shape, out_specs, scratch = first_kernel, sums, [vmem, vmem], []
    if totals is not None:
        operands += list(totals)
        body = middle_kernel
    if last:
        body = last_kernel
        out_shape = jax.ShapeDtypeStruct((rows, heads * HD), jnp.bfloat16)
        out_specs = vmem
        scratch = [pltpu.VMEM(s.shape, s.dtype) for s in sums]
    pairs = heads * rows * k_seg.shape[0]
    return pl.pallas_call(
        functools.partial(body, heads, q_tile, k_tile, len(parts)),
        in_specs=[pl.BlockSpec(memory_space=pltpu.SMEM)] + [vmem] * (len(operands) - 1),
        out_specs=out_specs,
        out_shape=out_shape,
        scratch_shapes=scratch,
        compiler_params=pltpu.CompilerParams(vmem_limit_bytes=VMEM_BYTES),
        cost_estimate=pl.CostEstimate(
            flops=4 * pairs * HD, bytes_accessed=4 * HD * k_seg.shape[0], transcendentals=2 * pairs
        ),
        name="attend",
    )(*operands)


MESH = pl.DeviceIdType.MESH
LOG2E = math.log2(math.e)


def block_kernel(
    len_ref, own_ref, freq_ref, tok_ref, seg_hbm, ig_hbm, og_hbm, wq_hbm, wkv_hbm, wo_hbm, cache_hbm,
    out_ref,
    tabs, ig_ref, og_ref, xbuf, wq, wkv, wo, keys, kseg, qseg, cosine, sine, q2, acc, den, qfar, qsegf, pacc, pden, pay, dpay, dfar, abuf, ax, ay, wx, wy, sbuf, rbuf, hold,
    load_sem, int_s, int_r, ag_s, ag_r, cu_s, cu_r, cd_s, cd_r, cs_s, cs_r, ku_s, ku_r, ks_s, ks_r,
    qd_s, qd_r, pd_s, pd_r, w_s, w_r, at_s, at_r, rs_s, rs_r,
):
    s, h = lax.axis_index("seq"), lax.axis_index("head")
    n_seq = tabs.shape[0]
    chips = n_seq // 2
    z, core = s // 2, s % 2
    mate = s + 1 - 2 * core
    hx, hy, hd = h + 1 - 2 * (h % 2), (h + 2) % 4, 3 - h
    rel = (h, hx, hy, hd)
    rows = tok_ref.shape[0]
    shard = 4 * rows
    half = rows // 2
    wide = out_ref.shape[1] // 2
    crow = cache_hbm.shape[1]
    cbase = 6 * shard
    f32, bf16 = jnp.float32, jnp.bfloat16

    def remote(src, dst, send, recv, seq=None, head=None):
        device = {"seq": s if seq is None else seq, "head": h if head is None else head}
        return pltpu.make_async_remote_copy(
            src_ref=src, dst_ref=dst, send_sem=send, recv_sem=recv, device_id=device, device_id_type=MESH
        )

    barrier = pltpu.get_barrier_semaphore()
    peers = [lax.rem(s + d, n_seq) for d in range(1, n_seq)]
    for peer in peers:
        pl.semaphore_signal(barrier, inc=1, device_id={"seq": peer, "head": h}, device_id_type=MESH)
    for head in (hx, hy):
        pl.semaphore_signal(barrier, inc=1, device_id={"seq": s, "head": head}, device_id_type=MESH)

    kv_cols = pl.ds(pl.multiple_of(h * 2 * HD, 2 * HD), 2 * HD)
    own_cache = keys.at[pl.ds(pl.multiple_of(cbase + s * crow, crow), crow)]
    blocks = shard // LANES
    loads = [
        pltpu.make_async_copy(wkv_hbm.at[:, kv_cols], wkv, load_sem.at[0]),
        pltpu.make_async_copy(wq_hbm, wq, load_sem.at[1]),
        pltpu.make_async_copy(wo_hbm, wo, load_sem.at[2]),
        pltpu.make_async_copy(cache_hbm.at[h], own_cache, load_sem.at[3]),
    ]
    early = [
        pltpu.make_async_copy(ig_hbm, ig_ref.at[0], load_sem.at[4]),
        pltpu.make_async_copy(og_hbm, og_ref.at[0], load_sem.at[5]),
    ] + [
        pltpu.make_async_copy(seg_hbm.at[pl.ds(i * LANES, LANES)], tabs.at[s, i], load_sem.at[6 + i])
        for i in range(blocks)
    ]
    for load in early + loads:
        load.start()

    pl.semaphore_wait(barrier, n_seq + 1)

    ints = [
        remote(tabs.at[s], tabs.at[s], int_s.at[d], int_r.at[d], seq=peers[d]) for d in range(n_seq - 1)
    ]
    top, bottom = pl.ds(0, half), pl.ds(half, half)

    def token_copy(m, block, part, head):
        ref = xbuf.at[block, part]
        return remote(ref, ref, ag_s.at[m], ag_r.at[m], head=head)

    gather = [
        token_copy(0, h, top, hx), token_copy(1, h, bottom, hx), token_copy(2, h, bottom, hy),
        token_copy(3, h, top, hy), token_copy(4, hx, top, hy), token_copy(5, hy, bottom, hx),
    ]
    gather_in = [
        token_copy(0, hx, top, hx), token_copy(1, hx, bottom, hx), token_copy(2, hy, bottom, hy),
        token_copy(3, hy, top, hy), token_copy(4, hd, top, hy), token_copy(5, hd, bottom, hx),
    ]

    def cache_ref(owner):
        return keys.at[pl.ds(pl.multiple_of(cbase + owner * crow, crow), crow)]

    def cache_up(k, owner):
        src = cache_hbm.at[h] if k == 0 else cache_ref(owner)
        return remote(src, cache_ref(owner), cu_s.at[k], cu_r.at[k], seq=s + 2)

    def cache_down(k, owner):
        src = cache_hbm.at[h] if k == 0 else cache_ref(owner)
        return remote(src, cache_ref(owner), cd_s.at[k], cd_r.at[k], seq=s - 2)

    def cache_side(i, owner):
        src = cache_hbm.at[h] if i == 0 else cache_ref(owner)
        return remote(src, cache_ref(owner), cs_s.at[i], cs_r.at[i], seq=mate)

    part_rows = wx.shape[0] // 2

    def weight_copy(m, c):
        span = pl.ds(pl.multiple_of(c * part_rows, part_rows), part_rows)
        there = (wx, wy)[m % 2].at[span]
        if m < 2:
            columns = pl.ds(m * wide, wide)
            return remote(wo_hbm.at[span, columns], there, w_s.at[m], w_r.at[m], head=(hx, hy)[m])
        return remote(there, there, w_s.at[m], w_r.at[m], seq=mate)

    last = chips - 1
    lane = lax.broadcasted_iota(jnp.int32, (1, LANES), 1)
    owned = jnp.zeros((1, LANES), jnp.int32)
    for i in range(own_ref.shape[0]):
        owned = jnp.where(lane == s * own_ref.shape[0] + i, own_ref[i], owned)
    tabs[s, blocks : blocks + 1, :] = owned
    for load in early:
        load.wait()

    for i in range(n_seq - 1):
        ints[i].start()

    @pl.when(z < last)
    def _():
        cache_up(0, s).start()

    @pl.when(z > 0)
    def _():
        cache_down(0, s).start()

    cache_side(0, s).start()

    x = tok_ref[...].astype(f32)
    scale = lax.rsqrt(jnp.mean(x * x, axis=-1, keepdims=True) + EPSILON)
    xbuf[h] = (x * scale * ig_ref[...]).astype(bf16)
    for m in (0, 2, 1, 3):
        gather[m].start()

    acc[...] = jnp.zeros_like(acc)
    den[...] = jnp.zeros_like(den)
    for d in range(n_seq - 1):
        source = lax.rem(s + n_seq - 1 - d, n_seq)
        remote(tabs.at[source], tabs.at[source], int_s.at[d], int_r.at[d], seq=source).wait_recv()

    def column(row):
        return jnp.broadcast_to(row, (LANES, LANES)).T

    segs = lax.broadcasted_iota(jnp.int32, (NSEG, LANES), 0)
    count = jnp.zeros((NSEG, LANES), jnp.int32)
    owners = jnp.zeros((1, LANES), jnp.int32)
    for p in range(n_seq):
        for i in range(blocks):
            row = tabs[p, i : i + 1, :]
            count += jnp.where((row >= 0) & (row < segs), 1, 0)
        owners += tabs[p, blocks : blocks + 1, :]
    firsts = jnp.sum(count.astype(f32), axis=1, keepdims=True)
    lengths = jnp.zeros((1, LANES), jnp.int32)
    for g in range(NSEG):
        lengths = jnp.where(lane == g, len_ref[g], lengths)
    lengths = column(lengths.astype(f32))[:NSEG, :1]
    base = lengths - firsts
    for i in range(blocks):
        row = tabs[s, i : i + 1, :]
        start = jnp.sum(jnp.where(segs == row, base, 0.0), axis=0, keepdims=True)
        place = start + (s * shard + i * LANES + lane).astype(f32)
        angle = column(place) * freq_ref[...]
        cosine[i] = jnp.cos(angle)
        sine[i] = jnp.sin(angle)
        qseg[i] = column(row)
        qsegf[i] = column(tabs[jnp.minimum(s + 1, n_seq - 1), i : i + 1, :])

    def spans(b):
        ahead = tabs[jnp.clip(2 * b, 0, n_seq - 2), 0:1, :][:, :1]
        behind = tabs[jnp.clip(2 * b - 4, 0, n_seq - 2), blocks - 1 : blocks, :][:, LANES - 1 :]
        return (ahead == behind) & (ahead >= 0)

    for dz in range(3):
        for c in range(2):
            source = jnp.maximum(z - dz, 0) * 2 + c
            for i in range(blocks):
                row = tabs[source, i : i + 1, :]
                at = (dz * 2 + c) * blocks + i
                hidden = (row < 0) | spans(z) if dz == 2 else row < 0
                kseg[at : at + 1, :] = jnp.where(hidden, -2, row)
    same = (column(owners) == owners) & (
        lax.broadcasted_iota(jnp.int32, (LANES, LANES), 0)
        < lax.broadcasted_iota(jnp.int32, (LANES, LANES), 1)
    )
    rank = jnp.sum(jnp.where(same, 1, 0), axis=0, keepdims=True)
    limit = jnp.sum(jnp.where(segs == owners, lengths, 0.0), axis=0, keepdims=True).astype(jnp.int32)
    filled = jnp.where(owners >= 0, jnp.clip(limit - BLK * rank, 0, BLK), 0)
    owner_col, filled_col = column(owners), column(filled)
    per = LANES // BLK
    pick = lax.broadcasted_iota(jnp.int32, (per, LANES), 0) == lane // BLK
    for i in range(n_seq * crow // LANES):
        part = slice(i * per, (i + 1) * per)
        who = jnp.sum(jnp.where(pick, owner_col[part], 0), axis=0, keepdims=True)
        many = jnp.sum(jnp.where(pick, filled_col[part], 0), axis=0, keepdims=True)
        at = 6 * blocks + i
        kseg[at : at + 1, :] = jnp.where(lane % BLK < many, who, -2)

    def kv_ref(dz, c, block):
        return keys.at[pl.ds(pl.multiple_of((dz * 2 + c) * shard + block * rows, rows), rows)]

    def kv_up(dz, r):
        return remote(
            kv_ref(dz, core, rel[r]), kv_ref(dz + 1, core, rel[r]), ku_s.at[dz, r], ku_r.at[dz, r], seq=s + 2
        )

    def kv_side(dz, r, c=None):
        ref = kv_ref(dz, core if c is None else c, rel[r])
        return remote(ref, ref, ks_s.at[dz, r], ks_r.at[dz, r], seq=mate)

    def project_kv(r):
        block = rel[r]
        y = jnp.dot(xbuf[block], wkv[...], preferred_element_type=f32)
        a, b = turn(y[:, :HD], cosine[block], sine[block], 1.0)
        at = pl.ds(pl.multiple_of(core * shard + block * rows, rows), rows)
        keys[at, : HD // 2] = a.astype(bf16)
        keys[at, HD // 2 : HD] = b.astype(bf16)
        keys[at, HD:] = y[:, HD:].astype(bf16)

        @pl.when(z < last)
        def _():
            kv_up(0, r).start()

        @pl.when(core == 0)
        def _():
            kv_side(0, r).start()

    def project_q(r):
        block = rel[r]
        y = jnp.dot(xbuf[block], wq[...], preferred_element_type=f32)
        for g in range(2):
            a, b = turn(y[:, g * HD : (g + 1) * HD], cosine[block], sine[block], HD**-0.5)
            q2[block, g * rows : (g + 1) * rows, : HD // 2] = a.astype(bf16)
            q2[block, g * rows : (g + 1) * rows, HD // 2 :] = b.astype(bf16)
        pl.when((z >= 2) & (core == 0))(lambda: query_down(r).start())

    def pass_cache(k):
        @pl.when(z >= k)
        def _():
            owner = s - 2 * k
            cache_up(k - 1, owner).wait_recv()

            if k < last:
                pl.when(z < last)(lambda: cache_up(k, owner).start())

            cache_side(k, owner).start()

        @pl.when(z + k <= last)
        def _():
            owner = s + 2 * k
            cache_down(k - 1, owner).wait_recv()

            if k < last:
                pl.when(z > 0)(lambda: cache_down(k, owner).start())

            cache_side(last + k, owner).start()

    def pass_kv(r):
        @pl.when(z >= 1)
        def _():
            kv_up(0, r).wait_recv()
            kv_side(1, r).start()

    def query_down(r):
        block = rel[r]
        return remote(q2.at[block], qfar.at[block], qd_s.at[r], qd_r.at[r], seq=s - 1)

    def far_rows(j):
        return pl.ds(j * rows, rows)

    def far_up(j):
        there = keys.at[pl.ds(5 * shard + j * rows, rows)]
        return remote(pay.at[far_rows(j)], there, ku_s.at[1, j], ku_r.at[1, j], seq=s + 2)

    def far_side(j):
        there = keys.at[pl.ds(5 * shard + j * rows, rows)]
        return remote(there, there, ks_s.at[2, j], ks_r.at[2, j], seq=mate)

    total_up = remote(dpay, dfar, pd_s.at[0], pd_r.at[0], seq=s + 2)
    total_side = remote(dfar, dfar, pd_s.at[1], pd_r.at[1], seq=mate)

    tile = shard

    def attend(j, at, causal=False, own=(q2, qseg, acc, den)):
        q2, qseg, acc, den = own
        span = pl.ds(pl.multiple_of(at * tile, tile), tile)
        scores = lax.dot_general(
            q2[j], keys[span, :HD], (((1,), (1,)), ((), ())), preferred_element_type=f32
        )
        columns = []
        total = [den[j, g * rows : (g + 1) * rows, :] for g in range(2)]
        for c in range(tile // LANES):
            allowed = qseg[j] == kseg[pl.ds(at * (tile // LANES) + c, 1), :]
            if causal:
                query = j * rows + lax.broadcasted_iota(jnp.int32, (rows, LANES), 0)
                allowed &= c * LANES + lax.broadcasted_iota(jnp.int32, (rows, LANES), 1) <= query
            pair = []
            for g in range(2):
                part = scores[g * rows : (g + 1) * rows, c * LANES : (c + 1) * LANES]
                part = jnp.exp2(jnp.tanh(part * (1.0 / SOFT_CAP)) * (SOFT_CAP * LOG2E))
                part = jnp.where(allowed, part, 0.0)
                total[g] += part
                pair.append(part.astype(bf16))
            columns.append(jnp.concatenate(pair, axis=0))
        for g in range(2):
            den[j, g * rows : (g + 1) * rows, :] = total[g]
        weights = jnp.concatenate(columns, axis=1)
        acc[j] += jnp.dot(weights, keys[span, HD:], preferred_element_type=f32)

    def attend_all(at, causal=False, own=(q2, qseg, acc, den)):
        def body(j, carry):
            attend(j, at, causal, own)
            return carry

        lax.fori_loop(0, 4, body, 0, unroll=4)

    def attend_cache(other):
        attend_all(6 + other)

    loads[0].wait()
    project_kv(0)
    loads[1].wait()
    project_q(0)
    pass_cache(1)
    pass_kv(0)
    gather_in[0].wait_recv()
    gather[4].start()
    gather_in[2].wait_recv()
    gather[5].start()
    weight_copy(0, core).start()
    weight_copy(1, core).start()
    gather_in[1].wait_recv()
    project_kv(1)
    gather_in[3].wait_recv()
    project_kv(2)
    pass_cache(2)
    project_q(1)
    project_q(2)
    gather_in[4].wait_recv()
    gather_in[5].wait_recv()
    project_kv(3)
    project_q(3)
    pass_kv(1)
    attend_all(core, True)
    pass_kv(2)
    loads[3].wait()
    cache_side(0, mate).wait_recv()
    attend_cache(z)

    def cache_tiles(k):
        @pl.when(z >= k)
        def _():
            cache_side(k, mate - 2 * k).wait_recv()
            attend_cache(z - k)

        @pl.when(z + k <= last)
        def _():
            cache_side(last + k, mate + 2 * k).wait_recv()
            attend_cache(z + k)

    cache_tiles(1)
    pass_kv(3)

    @pl.when(z >= 1)
    def _():
        for r in range(4):
            kv_side(1, r, 1 - core).wait_recv()

    @pl.when((z >= 1) & (z < last) & (core == 1))
    def _():
        pacc[...] = jnp.zeros_like(pacc)
        pden[...] = jnp.zeros_like(pden)
        for r in range(4):
            query_down(r).wait_recv()
        own = (qfar, qsegf, pacc, pden)
        attend_all(2, own=own)
        attend_all(3, own=own)
        flag = spans(z + 1)
        for j in range(4):
            for g in range(2):
                part = pl.ds(g * rows, rows)
                total = jnp.sum(pden[j, part, :], axis=-1, keepdims=True)
                dpay[2 * j + g : 2 * j + g + 1, :] = jnp.broadcast_to(total, (rows, LANES)).T[:1]
                columns = pl.ds(g * HD, HD)
                kept = keys[pl.ds(3 * shard + j * rows, rows), columns]
                pay[far_rows(j), columns] = jnp.where(flag, pacc[j, part, :].astype(bf16), kept)
            far_up(j).start()
        total_up.start()

    pass_cache(3)

    @pl.when(core == 1)
    def _():
        for r in range(4):
            kv_side(0, r, 0).wait_recv()
        attend_all(0)

    cache_tiles(2)

    @pl.when(z >= 1)
    def _():
        attend_all(2)
        attend_all(3)

    cache_tiles(3)

    for m in range(2):
        weight_copy(m, core).wait_recv()
        weight_copy(m + 2, core).start()
    loads[2].wait()

    @pl.when((z >= 2) & (core == 1))
    def _():
        for j in range(4):
            far_up(j).wait_recv()
            far_side(j).start()
        total_up.wait_recv()
        total_side.start()

    @pl.when((z >= 2) & (core == 0))
    def _():
        for j in range(4):
            far_side(j).wait_recv()
        total_side.wait_recv()

    def attended(j):
        present = qseg[j] >= 0
        present = present[:, :1]
        parts = []
        for g in range(2):
            total = jnp.sum(den[j, g * rows : (g + 1) * rows, :], axis=-1, keepdims=True)
            safe = jnp.where(present, total, 1.0)
            value = acc[j, g * rows : (g + 1) * rows, :] / safe
            parts.append(jnp.where(present, value, 0.0).astype(bf16))
        return jnp.concatenate(parts, axis=1)

    def finish(j):
        @pl.when(z >= 2)
        def _():
            attend(j, 5)

            @pl.when(core == 0)
            def _():
                flag = spans(z)
                at = pl.ds(pl.multiple_of(5 * shard + j * rows, rows), rows)
                for g in range(2):
                    part = pl.ds(g * rows, rows)
                    more = keys[at, g * HD : (g + 1) * HD].astype(f32)
                    acc[j, part, :] += jnp.where(flag, more, 0.0)
                    total = column(dfar[pl.ds(2 * j + g, 1), :])
                    den[j, part, :] += jnp.where(flag & (lane == 0), total, 0.0)

        abuf[j] = attended(j)

    def rows_copy(m, block):
        there = (ax, ay)[m % 2].at[m // 2]
        return remote(abuf.at[block], there, at_s.at[m], at_r.at[m], head=(hx, hy)[m % 2])

    def sum_copy(m):
        return remote(sbuf.at[m], rbuf.at[m], rs_s.at[m], rs_r.at[m], head=(hy, hx)[m])

    def left(a, weight=None):
        return jnp.dot(a, wo[:, :wide] if weight is None else weight[...], preferred_element_type=f32)

    def right(a, weight=None):
        return jnp.dot(a, wo[:, wide:] if weight is None else weight[...], preferred_element_type=f32)

    sent = (hd, hd, hx, hy)
    finish(hd)
    rows_copy(0, hd).start()
    rows_copy(1, hd).start()
    finish(hx)
    rows_copy(2, hx).start()
    finish(hy)
    rows_copy(3, hy).start()
    for m in range(2):
        weight_copy(m + 2, 1 - core).wait_recv()
    rows_copy(0, hd).wait_recv()
    sbuf[0] = (left(abuf[hy]) + left(ax[0], wx)).astype(bf16)
    sum_copy(0).start()
    rows_copy(1, hd).wait_recv()
    sbuf[1] = (right(abuf[hx]) + right(ay[0], wy)).astype(bf16)
    sum_copy(1).start()
    finish(h)
    hold[0] = left(abuf[h])
    hold[1] = right(abuf[h])
    rows_copy(2, hx).wait_recv()
    hold[0] += left(ax[1], wx)
    rows_copy(3, hy).wait_recv()
    hold[1] += right(ay[1], wy)
    sum_copy(0).wait_recv()
    branch_l = hold[0] + rbuf[0].astype(f32)
    sum_copy(1).wait_recv()
    branch_r = hold[1] + rbuf[1].astype(f32)
    square = jnp.sum(branch_l * branch_l, axis=-1, keepdims=True) + jnp.sum(
        branch_r * branch_r, axis=-1, keepdims=True
    )
    scale = lax.rsqrt(square / (2 * wide) + EPSILON)
    out_ref[:, :wide] = (
        tok_ref[:, :wide].astype(f32) + branch_l * scale * og_ref[:, :wide]
    ).astype(bf16)
    out_ref[:, wide:] = (
        tok_ref[:, wide:].astype(f32) + branch_r * scale * og_ref[:, wide:]
    ).astype(bf16)

    for i in range(n_seq - 1):
        ints[i].wait_send()
    for copy in gather:
        copy.wait_send()
    for m in range(4):
        rows_copy(m, sent[m]).wait_send()
        weight_copy(m, core).wait_send()
    for m in range(2):
        sum_copy(m).wait_send()
    cache_side(0, s).wait_send()
    for k in range(chips - 1):
        @pl.when((z < last) & (z >= k))
        def _():
            cache_up(k, s - 2 * k).wait_send()

        @pl.when((z > 0) & (z + k <= last))
        def _():
            cache_down(k, s + 2 * k).wait_send()

    for k in range(1, chips):
        @pl.when(z >= k)
        def _():
            cache_side(k, s - 2 * k).wait_send()

        @pl.when(z + k <= last)
        def _():
            cache_side(last + k, s + 2 * k).wait_send()

    for r in range(4):
        @pl.when(z < last)
        def _():
            kv_up(0, r).wait_send()

        @pl.when(core == 0)
        def _():
            kv_side(0, r).wait_send()

        @pl.when(z >= 1)
        def _():
            kv_side(1, r).wait_send()

        @pl.when((z >= 2) & (core == 0))
        def _():
            query_down(r).wait_send()

        @pl.when((z >= 1) & (z < last) & (core == 1))
        def _():
            far_up(r).wait_send()

        @pl.when((z >= 2) & (core == 1))
        def _():
            far_side(r).wait_send()

    @pl.when((z >= 1) & (z < last) & (core == 1))
    def _():
        total_up.wait_send()

    @pl.when((z >= 2) & (core == 1))
    def _():
        total_side.wait_send()


def whole_block(
    tokens, in_gain, out_gain, query_weight, keyval_weight, out_weight, cache_entries, segment_ids,
    cache_lengths, block_owners,
):
    n_seq = lax.axis_size("seq")
    rows, width = tokens.shape
    shard = segment_ids.shape[0]
    crow = cache_entries.shape[1]
    n_keys = 6 * shard + n_seq * crow
    angle = (10000.0 ** (-np.arange(HD // 2) * 2.0 / HD)).astype(np.float32)[None]
    smem = pl.BlockSpec(memory_space=pltpu.SMEM)
    vmem, hbm = pl.BlockSpec(memory_space=pltpu.VMEM), pl.BlockSpec(memory_space=pl.ANY)
    f32, bf16, i32 = jnp.float32, jnp.bfloat16, jnp.int32
    dma = pltpu.SemaphoreType.DMA
    hops = n_seq // 2 - 1
    pairs = [dma((n,)) for n in (n_seq - 1, 6, hops, hops, 2 * hops + 1) for _ in range(2)]
    return pl.pallas_call(
        block_kernel,
        out_shape=jax.ShapeDtypeStruct((rows, width), bf16),
        in_specs=[smem] * 2 + [vmem] * 2 + [hbm] * 7,
        out_specs=vmem,
        scratch_shapes=[
            pltpu.VMEM((n_seq, 8 * -(-(shard // LANES + 1) // 8), LANES), i32),
            pltpu.VMEM((1, width), f32),
            pltpu.VMEM((1, width), f32),
            pltpu.VMEM((4, rows, width), bf16),
            pltpu.VMEM((width, 2 * HD), bf16),
            pltpu.VMEM((width, 2 * HD), bf16),
            pltpu.VMEM((2 * HD, width), bf16),
            pltpu.VMEM((n_keys, 2 * HD), bf16),
            pltpu.VMEM((n_keys // LANES, LANES), i32),
            pltpu.VMEM((4, rows, LANES), i32),
            pltpu.VMEM((4, rows, LANES), f32),
            pltpu.VMEM((4, rows, LANES), f32),
            pltpu.VMEM((4, 2 * rows, HD), bf16),
            pltpu.VMEM((4, 2 * rows, HD), f32),
            pltpu.VMEM((4, 2 * rows, LANES), f32),
            pltpu.VMEM((4, 2 * rows, HD), bf16),
            pltpu.VMEM((4, rows, LANES), i32),
            pltpu.VMEM((4, 2 * rows, HD), f32),
            pltpu.VMEM((4, 2 * rows, LANES), f32),
            pltpu.VMEM((shard, 2 * HD), bf16),
            pltpu.VMEM((8, LANES), f32),
            pltpu.VMEM((8, LANES), f32),
            pltpu.VMEM((4, rows, 2 * HD), bf16),
            pltpu.VMEM((2, rows, 2 * HD), bf16),
            pltpu.VMEM((2, rows, 2 * HD), bf16),
            pltpu.VMEM((2 * HD, width // 2), bf16),
            pltpu.VMEM((2 * HD, width // 2), bf16),
            pltpu.VMEM((2, rows, width // 2), bf16),
            pltpu.VMEM((2, rows, width // 2), bf16),
            pltpu.VMEM((2, rows, width // 2), f32),
            dma((6 + shard // LANES,)),
            *pairs,
            dma((2, 4)), dma((2, 4)), dma((3, 4)), dma((3, 4)),
            dma((4,)), dma((4,)), dma((2,)), dma((2,)),
            dma((4,)), dma((4,)), dma((4,)), dma((4,)), dma((2,)), dma((2,)),
        ],
        compiler_params=pltpu.CompilerParams(
            collective_id=0, has_side_effects=True, vmem_limit_bytes=56 << 20
        ),
        cost_estimate=pl.CostEstimate(
            flops=2 * shard * (6 * HD * width + 8 * n_keys * HD // 4),
            bytes_accessed=6 * HD * 2 * width,
            transcendentals=4 * shard * n_keys,
        ),
        name="block",
    )(
        cache_lengths, block_owners, jnp.asarray(angle), tokens, segment_ids, in_gain, out_gain,
        query_weight, keyval_weight, out_weight, cache_entries,
    )


def local(
    tokens,
    in_gain,
    out_gain,
    query_weight,
    keyval_weight,
    out_weight,
    cache_entries,
    segment_ids,
    cache_lengths,
    block_owners,
):
    heads_here = query_weight.shape[1] // HD
    group_size = QH // KVH
    seq_size, head_size = lax.axis_size("seq"), lax.axis_size("head")
    seq_index = lax.axis_index("seq")
    head_index = lax.axis_index("head")
    shared_head = head_index * heads_here // group_size
    stream_rows = segment_ids.shape[0]
    normed_own = rms_scale(tokens, in_gain).astype(jnp.bfloat16)
    chunks = [[lax.all_gather(normed_own, "head", axis=0, tiled=True)]]

    cache_own = lax.dynamic_index_in_dim(cache_entries, shared_head, 0, keepdims=False)
    cache_pairs = lax.all_gather(cache_own, "seq", axis=0, tiled=True)

    table = jnp.concatenate([segment_ids, block_owners])[None]
    bits = 0
    while 1 << bits < seq_size:
        step = 1 << bits
        other = lax.ppermute(table, "seq", [(s, s ^ step) for s in range(seq_size)])
        table = jnp.concatenate([table, other], axis=0)
        bits += 1
    for bit in range(bits):
        pieces = table.reshape(-1, 2, 1 << bit, table.shape[-1])
        pieces = jnp.where((seq_index >> bit) % 2 == 1, pieces[:, ::-1], pieces)
        table = pieces.reshape(seq_size, -1)
    seg_all = table[:, :stream_rows].reshape(-1)
    owners = table[:, stream_rows:].reshape(-1)

    seg_range = jnp.arange(NSEG, dtype=jnp.int32)
    earlier = (seg_all[None, :] >= 0) & (seg_all[None, :] < seg_range[:, None])
    firsts = jnp.sum(earlier.astype(jnp.int32), axis=1)
    slots_all = jnp.arange(seg_all.shape[0], dtype=jnp.int32)
    begin = seq_index * stream_rows
    q_seg = lax.dynamic_slice_in_dim(seg_all, begin, stream_rows)
    q_slot = lax.dynamic_slice_in_dim(slots_all, begin, stream_rows)
    matches = (q_seg[:, None] == seg_range[None, :]).astype(jnp.int32)
    positions = jnp.sum(matches * (cache_lengths - firsts)[None, :], axis=1) + q_slot
    angles = positions.astype(jnp.float32)[:, None] * frequencies(HD)[None, :]
    cosine, sine = jnp.cos(angles), jnp.sin(angles)

    block_index = jnp.arange(owners.shape[0], dtype=jnp.int32)
    same = (owners[:, None] == owners[None, :]) & (block_index[None, :] < block_index[:, None])
    block_rank = jnp.sum(same.astype(jnp.int32), axis=1)
    owner_match = (owners[:, None] == seg_range[None, :]).astype(jnp.int32)
    limits = jnp.sum(owner_match * cache_lengths[None, :], axis=1)
    offsets = jnp.arange(BLK, dtype=jnp.int32)
    usable = (owners[:, None] >= 0) & (
        block_rank[:, None] * BLK + offsets[None, :] < limits[:, None]
    )
    cache_seg = jnp.where(usable, owners[:, None], -2).reshape(-1)
    cache_slot = jnp.full((cache_seg.shape[0],), -1, jnp.int32)

    chunk_rows = stream_rows // len(chunks)
    pairs = []
    for at, parts in enumerate(chunks):
        rows = slice(at * chunk_rows, (at + 1) * chunk_rows)
        pairs.append(
            project(
                keyval_kernel, parts, keyval_weight, 2 * HD, shared_head,
                cosine[rows], sine[rows], (chunk_rows, 2 * HD),
            )
        )
    queries = project(
        query_kernel, sum(chunks, []), query_weight, heads_here * HD, jnp.int32(0),
        cosine, sine, (heads_here, stream_rows, HD),
    )

    hops = seq_size // 4

    def onward(array):
        return lax.ppermute(array, "seq", [(s, s + 2) for s in range(seq_size - 2)])

    def sibling(array):
        return lax.ppermute(array, "seq", [(s, s ^ 1) for s in range(seq_size)])

    key_seg = jnp.where(seg_all >= 0, seg_all, -2)

    def shard_ints(shard):
        inside = (shard >= 0) & (shard < seq_size)
        at = jnp.clip(shard, 0, seq_size - 1) * stream_rows
        seg = lax.dynamic_slice_in_dim(key_seg, at, stream_rows)
        return jnp.where(inside, seg, -2), lax.dynamic_slice_in_dim(slots_all, at, stream_rows)

    mate = seq_index + 1 - 2 * (seq_index % 2)
    travelling = [onward(pair) for pair in pairs]
    waiting, waiting_ints = [sibling(pair) for pair in pairs], [shard_ints(mate)]
    totals = attend(
        queries, q_seg, q_slot, pairs + [cache_pairs], [shard_ints(seq_index), (cache_seg, cache_slot)]
    )
    for hop in range(1, hops + 1):
        travelling, totals = lax.optimization_barrier((travelling, totals))
        following = [onward(pair) for pair in travelling] if hop < hops else []
        beside = [sibling(pair) for pair in travelling]
        parts = waiting + travelling
        ints = waiting_ints + [shard_ints(seq_index - 2 * hop)]
        waiting, waiting_ints = beside, [shard_ints(mate - 2 * hop)]
        if hop < hops:
            totals = attend(queries, q_seg, q_slot, parts, ints, totals)
        else:
            attended = attend(
                queries, q_seg, q_slot, parts + waiting, ints + waiting_ints, totals, last=True
            )
        travelling = following

    branch = lax.psum_scatter(
        jnp.dot(attended, out_weight, preferred_element_type=jnp.float32),
        "head",
        scatter_dimension=0,
        tiled=True,
    )
    return (tokens.astype(jnp.float32) + rms_scale(branch, out_gain)).astype(jnp.bfloat16)


def solution(mesh):
    in_specs = (
        P(("seq", "head"), None),
        P(),
        P(),
        P(None, "head"),
        P(),
        P("head", None),
        P(None, "seq", None),
        P("seq"),
        P(),
        P("seq"),
    )
    out_specs = P(("seq", "head"), None)
    fits = mesh.shape["seq"] == 8 and mesh.shape["head"] == 4
    body = whole_block if fits else local
    return jax.shard_map(body, mesh=mesh, in_specs=in_specs, out_specs=out_specs, check_vma=False)
```

```python
import functools
import math

import jax
import jax.numpy as jnp
import numpy as np
from jax import lax
from jax.experimental import pallas as pl
from jax.experimental.pallas import tpu as pltpu
from jax.sharding import PartitionSpec as P

QH = 8
KVH = 4
HD = 256
NSEG = 64
BLK = 16
LANES = 128
EPSILON = 1e-06
SOFT_CAP = 50.0
FAR = 1073741824
VMEM_BYTES = 40 << 20


def rms_scale(matrix, scaling):
    matrix = matrix.astype(jnp.float32)
    mean_square = jnp.mean(matrix * matrix, axis=-1, keepdims=True)
    return matrix * lax.rsqrt(mean_square + EPSILON) * scaling


def frequencies(extent):
    return 10000.0 ** (-(jnp.arange(extent // 2, dtype=jnp.float32) * 2.0 / extent))


def turn(y, cosine, sine, scale):
    half = y.shape[1] // 2
    a, b = y[:, :half], y[:, half:]
    return (a * cosine - b * sine) * scale, (b * cosine + a * sine) * scale


def query_kernel(count, which_ref, cos_ref, sin_ref, w_ref, *rest):
    parts, out_ref = rest[:count], rest[count]
    half = HD // 2
    x = jnp.concatenate([part[...] for part in parts], axis=0)
    for h in range(w_ref.shape[1] // HD):
        y = jnp.dot(x, w_ref[:, h * HD : (h + 1) * HD], preferred_element_type=jnp.float32)
        a, b = turn(y, cos_ref[...], sin_ref[...], HD**-0.5)
        out_ref[h, :, :half] = a.astype(out_ref.dtype)
        out_ref[h, :, half:] = b.astype(out_ref.dtype)


def keyval_kernel(count, which_ref, cos_ref, sin_ref, w_ref, *rest):
    parts, out_ref = rest[:count], rest[count]
    half = HD // 2
    x = jnp.concatenate([part[...] for part in parts], axis=0)
    y = jnp.dot(x, w_ref[...], preferred_element_type=jnp.float32)
    a, b = turn(y[:, :HD], cos_ref[...], sin_ref[...], 1.0)
    out_ref[:, :half] = a.astype(out_ref.dtype)
    out_ref[:, half:HD] = b.astype(out_ref.dtype)
    out_ref[:, HD:] = y[:, HD:].astype(out_ref.dtype)


def project(body, parts, weight, columns, which, cosine, sine, out_shape):
    rows = cosine.shape[0]
    width = weight.shape[0]
    whole = [pl.BlockSpec(x.shape, lambda i, s: (0, 0)) for x in (cosine, sine)]
    return pl.pallas_call(
        functools.partial(body, len(parts)),
        grid_spec=pltpu.PrefetchScalarGridSpec(
            num_scalar_prefetch=1,
            grid=(1,),
            in_specs=whole
            + [pl.BlockSpec((width, columns), lambda i, s: (0, s[0]))]
            + [pl.BlockSpec(x.shape, lambda i, s: (0, 0)) for x in parts],
            out_specs=pl.BlockSpec(out_shape, lambda i, s: (0,) * len(out_shape)),
        ),
        out_shape=jax.ShapeDtypeStruct(out_shape, jnp.bfloat16),
        compiler_params=pltpu.CompilerParams(vmem_limit_bytes=VMEM_BYTES),
        cost_estimate=pl.CostEstimate(
            flops=2 * rows * width * columns,
            bytes_accessed=2 * width * (columns + rows),
            transcendentals=0,
        ),
        name="project",
    )(which.reshape(1), cosine, sine, weight, *parts)


def fold_blocks(
    heads, q_tile, k_tile, touch_ref, q_ref, qseg_ref, qslot_ref, kseg_ref, kslot_ref, parts, acc, den
):
    q_tiles = q_ref.shape[1] // q_tile
    blocks = kseg_ref.shape[0]
    first = 0
    for part in parts:
        here = part.shape[0] // k_tile

        def step(index, carry, part=part, here=here, first=first):
            qi = index // here
            kj = index % here

            @pl.when(touch_ref[qi * blocks + first + kj] > 0)
            def _():
                rows = pl.ds(pl.multiple_of(qi * q_tile, q_tile), q_tile)
                keys = pl.ds(pl.multiple_of(kj * k_tile, k_tile), k_tile)
                allowed = (kseg_ref[first + kj] == qseg_ref[rows, :]) & (
                    kslot_ref[first + kj] <= qslot_ref[rows, :]
                )
                for h in range(heads):
                    scores = lax.dot_general(
                        q_ref[h, rows, :],
                        part[keys, :HD],
                        (((1,), (1,)), ((), ())),
                        preferred_element_type=jnp.float32,
                    )
                    scores = jnp.tanh(scores * (1.0 / SOFT_CAP))
                    weights = jnp.where(
                        allowed, jnp.exp2(scores * (SOFT_CAP * math.log2(math.e))), 0.0
                    )
                    total = weights[:, :LANES]
                    for c in range(1, k_tile // LANES):
                        total += weights[:, c * LANES : (c + 1) * LANES]
                    den[h, rows, :] += total
                    acc[h, rows, :] += jnp.dot(
                        weights.astype(jnp.bfloat16),
                        part[keys, HD:],
                        preferred_element_type=jnp.float32,
                    )

            return carry

        lax.fori_loop(0, q_tiles * here, step, 0)
        first += here


def middle_kernel(heads, q_tile, k_tile, count, touch_ref, q_ref, qseg_ref, qslot_ref, kseg_ref, kslot_ref, *rest):
    parts, (acc_in, den_in, acc, den) = rest[:count], rest[count:]
    acc[...] = acc_in[...]
    den[...] = den_in[...]
    fold_blocks(
        heads, q_tile, k_tile, touch_ref, q_ref, qseg_ref, qslot_ref, kseg_ref, kslot_ref, parts, acc, den
    )


def first_kernel(heads, q_tile, k_tile, count, touch_ref, q_ref, qseg_ref, qslot_ref, kseg_ref, kslot_ref, *rest):
    parts, (acc, den) = rest[:count], rest[count:]
    acc[...] = jnp.zeros_like(acc)
    den[...] = jnp.zeros_like(den)
    fold_blocks(
        heads, q_tile, k_tile, touch_ref, q_ref, qseg_ref, qslot_ref, kseg_ref, kslot_ref, parts, acc, den
    )


def last_kernel(heads, q_tile, k_tile, count, touch_ref, q_ref, qseg_ref, qslot_ref, kseg_ref, kslot_ref, *rest):
    parts, (acc_in, den_in, out_ref, acc, den) = rest[:count], rest[count:]
    acc[...] = acc_in[...]
    den[...] = den_in[...]
    fold_blocks(
        heads, q_tile, k_tile, touch_ref, q_ref, qseg_ref, qslot_ref, kseg_ref, kslot_ref, parts, acc, den
    )
    present = qseg_ref[...] >= 0
    for h in range(heads):
        total = jnp.sum(den[h], axis=-1, keepdims=True)
        safe = jnp.where(present, total, 1.0)
        out_ref[:, h * HD : (h + 1) * HD] = jnp.where(present, acc[h] / safe, 0.0).astype(
            out_ref.dtype
        )


def attend(queries, q_seg, q_slot, parts, ints, totals=None, last=False):
    heads, rows, _ = queries.shape
    k_seg = jnp.concatenate([pair[0] for pair in ints])
    k_slot = jnp.concatenate([pair[1] for pair in ints])
    q_tile = math.gcd(rows, 256)
    k_tile = math.gcd(*[part.shape[0] for part in parts], 512)
    blocks = k_seg.shape[0] // k_tile
    seg_tiles = q_seg.reshape(-1, q_tile)
    lowest = jnp.min(jnp.where(seg_tiles >= 0, seg_tiles, FAR), axis=1)[:, None]
    highest = jnp.max(seg_tiles, axis=1)[:, None]
    latest = jnp.max(q_slot.reshape(-1, q_tile), axis=1)[:, None]
    near = (k_seg[None] >= lowest) & (k_seg[None] <= highest) & (k_slot[None] <= latest)
    touch = jnp.max(near.astype(jnp.int32).reshape(-1, blocks, k_tile), axis=2).reshape(-1)
    operands = [
        touch,
        queries,
        q_seg[:, None],
        q_slot[:, None],
        k_seg.reshape(blocks, 1, k_tile),
        k_slot.reshape(blocks, 1, k_tile),
        *parts,
    ]
    vmem = pl.BlockSpec(memory_space=pltpu.VMEM)
    sums = [
        jax.ShapeDtypeStruct((heads, rows, HD), jnp.float32),
        jax.ShapeDtypeStruct((heads, rows, LANES), jnp.float32),
    ]
    body, out_shape, out_specs, scratch = first_kernel, sums, [vmem, vmem], []
    if totals is not None:
        operands += list(totals)
        body = middle_kernel
    if last:
        body = last_kernel
        out_shape = jax.ShapeDtypeStruct((rows, heads * HD), jnp.bfloat16)
        out_specs = vmem
        scratch = [pltpu.VMEM(s.shape, s.dtype) for s in sums]
    pairs = heads * rows * k_seg.shape[0]
    return pl.pallas_call(
        functools.partial(body, heads, q_tile, k_tile, len(parts)),
        in_specs=[pl.BlockSpec(memory_space=pltpu.SMEM)] + [vmem] * (len(operands) - 1),
        out_specs=out_specs,
        out_shape=out_shape,
        scratch_shapes=scratch,
        compiler_params=pltpu.CompilerParams(vmem_limit_bytes=VMEM_BYTES),
        cost_estimate=pl.CostEstimate(
            flops=4 * pairs * HD, bytes_accessed=4 * HD * k_seg.shape[0], transcendentals=2 * pairs
        ),
        name="attend",
    )(*operands)


MESH = pl.DeviceIdType.MESH
LOG2E = math.log2(math.e)


def block_kernel(
    tok_ref, small, table, wq_hbm, wkv_hbm, wo_hbm, cache_hbm,
    out_ref,
    tabs, line, freq, ig_ref, og_ref, xbuf, wq, wkv, wo, keys, kseg, qseg, cosine, sine, q2, acc, den, qfar, qsegf, pacc, pden, pay, dpay, dfar, abuf, ax, ay, wx, wy, sbuf, rbuf, hold,
    load_sem, int_s, int_r, ag_s, ag_r, cu_s, cu_r, cd_s, cd_r, cs_s, cs_r, ku_s, ku_r, ks_s, ks_r,
    qd_s, qd_r, pd_s, pd_r, w_s, w_r, at_s, at_r, rs_s, rs_r,
):
    s, h = lax.axis_index("seq"), lax.axis_index("head")
    n_seq = tabs.shape[0]
    chips = n_seq // 2
    z, core = s // 2, s % 2
    mate = s + 1 - 2 * core
    hx, hy, hd = h + 1 - 2 * (h % 2), (h + 2) % 4, 3 - h
    rel = (h, hx, hy, hd)
    rows = tok_ref.shape[0]
    shard = 4 * rows
    half = rows // 2
    wide = out_ref.shape[1] // 2
    crow = cache_hbm.shape[1]
    cbase = 6 * shard
    f32, bf16 = jnp.float32, jnp.bfloat16

    def remote(src, dst, send, recv, seq=None, head=None):
        device = {"seq": s if seq is None else seq, "head": h if head is None else head}
        return pltpu.make_async_remote_copy(
            src_ref=src, dst_ref=dst, send_sem=send, recv_sem=recv, device_id=device, device_id_type=MESH
        )

    barrier = pltpu.get_barrier_semaphore()
    peers = [lax.rem(s + d, n_seq) for d in range(1, n_seq)]
    for peer in peers:
        pl.semaphore_signal(barrier, inc=1, device_id={"seq": peer, "head": h}, device_id_type=MESH)
    for head in (hx, hy):
        pl.semaphore_signal(barrier, inc=1, device_id={"seq": s, "head": head}, device_id_type=MESH)

    kv_cols = pl.ds(pl.multiple_of(h * 2 * HD, 2 * HD), 2 * HD)
    own_cache = keys.at[pl.ds(pl.multiple_of(cbase + s * crow, crow), crow)]
    blocks = shard // LANES
    loads = [
        pltpu.make_async_copy(wkv_hbm.at[:, kv_cols], wkv, load_sem.at[0]),
        pltpu.make_async_copy(wq_hbm, wq, load_sem.at[1]),
        pltpu.make_async_copy(wo_hbm, wo, load_sem.at[2]),
        pltpu.make_async_copy(cache_hbm.at[h], own_cache, load_sem.at[3]),
    ]
    width = 2 * wide
    width = 2 * wide
    early = [
        pltpu.make_async_copy(
            table.at[pl.ds(i * LANES, LANES)],
            tabs.at[s, i] if i < blocks else line.at[i - blocks],
            load_sem.at[7 + i],
        )
        for i in range(blocks + 2)
    ] + [
        pltpu.make_async_copy(small.at[pl.ds(0, width)], ig_ref.at[0], load_sem.at[4]),
        pltpu.make_async_copy(small.at[pl.ds(width, width)], og_ref.at[0], load_sem.at[5]),
        pltpu.make_async_copy(small.at[pl.ds(2 * width, LANES)], freq.at[0], load_sem.at[6]),
    ]
    for load in early + loads:
        load.start()

    pl.semaphore_wait(barrier, n_seq + 1)

    ints = [
        remote(tabs.at[s], tabs.at[s], int_s.at[d], int_r.at[d], seq=peers[d]) for d in range(n_seq - 1)
    ]
    top, bottom = pl.ds(0, half), pl.ds(half, half)

    def token_copy(m, block, part, head):
        ref = xbuf.at[block, part]
        return remote(ref, ref, ag_s.at[m], ag_r.at[m], head=head)

    gather = [
        token_copy(0, h, top, hx), token_copy(1, h, bottom, hx), token_copy(2, h, bottom, hy),
        token_copy(3, h, top, hy), token_copy(4, hx, top, hy), token_copy(5, hy, bottom, hx),
    ]
    gather_in = [
        token_copy(0, hx, top, hx), token_copy(1, hx, bottom, hx), token_copy(2, hy, bottom, hy),
        token_copy(3, hy, top, hy), token_copy(4, hd, top, hy), token_copy(5, hd, bottom, hx),
    ]

    def cache_ref(owner):
        return keys.at[pl.ds(pl.multiple_of(cbase + owner * crow, crow), crow)]

    def cache_up(k, owner):
        src = cache_hbm.at[h] if k == 0 else cache_ref(owner)
        return remote(src, cache_ref(owner), cu_s.at[k], cu_r.at[k], seq=s + 2)

    def cache_down(k, owner):
        src = cache_hbm.at[h] if k == 0 else cache_ref(owner)
        return remote(src, cache_ref(owner), cd_s.at[k], cd_r.at[k], seq=s - 2)

    def cache_side(i, owner):
        src = cache_hbm.at[h] if i == 0 else cache_ref(owner)
        return remote(src, cache_ref(owner), cs_s.at[i], cs_r.at[i], seq=mate)

    part_rows = wx.shape[0] // 2

    def weight_copy(m, c):
        span = pl.ds(pl.multiple_of(c * part_rows, part_rows), part_rows)
        there = (wx, wy)[m % 2].at[span]
        if m < 2:
            columns = pl.ds(m * wide, wide)
            return remote(wo_hbm.at[span, columns], there, w_s.at[m], w_r.at[m], head=(hx, hy)[m])
        return remote(there, there, w_s.at[m], w_r.at[m], seq=mate)

    last = chips - 1
    lane = lax.broadcasted_iota(jnp.int32, (1, LANES), 1)
    for load in early:
        load.wait()

    def column(row):
        return jnp.broadcast_to(row, (LANES, LANES)).T

    here = crow // BLK
    mine = lax.broadcasted_iota(jnp.int32, (here, LANES), 0) == lane - s * here
    owned = jnp.where(mine, column(line[:1, :])[:here], 0)
    tabs[s, blocks : blocks + 1, :] = jnp.sum(owned, axis=0, keepdims=True)
    for i in range(n_seq - 1):
        ints[i].start()

    @pl.when(z < last)
    def _():
        cache_up(0, s).start()

    @pl.when(z > 0)
    def _():
        cache_down(0, s).start()

    cache_side(0, s).start()

    x = tok_ref[...].astype(f32)
    scale = lax.rsqrt(jnp.mean(x * x, axis=-1, keepdims=True) + EPSILON)
    xbuf[h] = (x * scale * ig_ref[...]).astype(bf16)
    for m in (0, 2, 1, 3):
        gather[m].start()

    acc[...] = jnp.zeros_like(acc)
    den[...] = jnp.zeros_like(den)
    for d in range(n_seq - 1):
        source = lax.rem(s + n_seq - 1 - d, n_seq)
        remote(tabs.at[source], tabs.at[source], int_s.at[d], int_r.at[d], seq=source).wait_recv()

    segs = lax.broadcasted_iota(jnp.int32, (NSEG, LANES), 0)
    count = jnp.zeros((NSEG, LANES), jnp.int32)
    owners = jnp.zeros((1, LANES), jnp.int32)
    for p in range(n_seq):
        for i in range(blocks):
            row = tabs[p, i : i + 1, :]
            count += jnp.where((row >= 0) & (row < segs), 1, 0)
        owners += tabs[p, blocks : blocks + 1, :]
    firsts = jnp.sum(count.astype(f32), axis=1, keepdims=True)
    lengths = column(line[1:2, :].astype(f32))[:NSEG, :1]
    base = lengths - firsts
    for i in range(blocks):
        row = tabs[s, i : i + 1, :]
        start = jnp.sum(jnp.where(segs == row, base, 0.0), axis=0, keepdims=True)
        place = start + (s * shard + i * LANES + lane).astype(f32)
        angle = column(place) * freq[:1, :]
        cosine[i] = jnp.cos(angle)
        sine[i] = jnp.sin(angle)
        qseg[i] = column(row)
        qsegf[i] = column(tabs[jnp.minimum(s + 1, n_seq - 1), i : i + 1, :])

    def spans(b):
        ahead = tabs[jnp.clip(2 * b, 0, n_seq - 2), 0:1, :][:, :1]
        behind = tabs[jnp.clip(2 * b - 4, 0, n_seq - 2), blocks - 1 : blocks, :][:, LANES - 1 :]
        return (ahead == behind) & (ahead >= 0)

    for dz in range(3):
        for c in range(2):
            source = jnp.maximum(z - dz, 0) * 2 + c
            for i in range(blocks):
                row = tabs[source, i : i + 1, :]
                at = (dz * 2 + c) * blocks + i
                hidden = (row < 0) | spans(z) if dz == 2 else row < 0
                kseg[at : at + 1, :] = jnp.where(hidden, -2, row)
    same = (column(owners) == owners) & (
        lax.broadcasted_iota(jnp.int32, (LANES, LANES), 0)
        < lax.broadcasted_iota(jnp.int32, (LANES, LANES), 1)
    )
    rank = jnp.sum(jnp.where(same, 1, 0), axis=0, keepdims=True)
    limit = jnp.sum(jnp.where(segs == owners, lengths, 0.0), axis=0, keepdims=True).astype(jnp.int32)
    filled = jnp.where(owners >= 0, jnp.clip(limit - BLK * rank, 0, BLK), 0)
    owner_col, filled_col = column(owners), column(filled)
    per = LANES // BLK
    pick = lax.broadcasted_iota(jnp.int32, (per, LANES), 0) == lane // BLK
    for i in range(n_seq * crow // LANES):
        part = slice(i * per, (i + 1) * per)
        who = jnp.sum(jnp.where(pick, owner_col[part], 0), axis=0, keepdims=True)
        many = jnp.sum(jnp.where(pick, filled_col[part], 0), axis=0, keepdims=True)
        at = 6 * blocks + i
        kseg[at : at + 1, :] = jnp.where(lane % BLK < many, who, -2)

    def kv_ref(dz, c, block):
        return keys.at[pl.ds(pl.multiple_of((dz * 2 + c) * shard + block * rows, rows), rows)]

    def kv_up(dz, r):
        return remote(
            kv_ref(dz, core, rel[r]), kv_ref(dz + 1, core, rel[r]), ku_s.at[dz, r], ku_r.at[dz, r], seq=s + 2
        )

    def kv_side(dz, r, c=None):
        ref = kv_ref(dz, core if c is None else c, rel[r])
        return remote(ref, ref, ks_s.at[dz, r], ks_r.at[dz, r], seq=mate)

    def project_kv(r):
        block = rel[r]
        y = jnp.dot(xbuf[block], wkv[...], preferred_element_type=f32)
        a, b = turn(y[:, :HD], cosine[block], sine[block], 1.0)
        at = pl.ds(pl.multiple_of(core * shard + block * rows, rows), rows)
        keys[at, : HD // 2] = a.astype(bf16)
        keys[at, HD // 2 : HD] = b.astype(bf16)
        keys[at, HD:] = y[:, HD:].astype(bf16)

        @pl.when(z < last)
        def _():
            kv_up(0, r).start()

        @pl.when(core == 0)
        def _():
            kv_side(0, r).start()

    def project_q(r):
        block = rel[r]
        y = jnp.dot(xbuf[block], wq[...], preferred_element_type=f32)
        for g in range(2):
            a, b = turn(y[:, g * HD : (g + 1) * HD], cosine[block], sine[block], HD**-0.5)
            q2[block, g * rows : (g + 1) * rows, : HD // 2] = a.astype(bf16)
            q2[block, g * rows : (g + 1) * rows, HD // 2 :] = b.astype(bf16)
        pl.when((z >= 2) & (core == 0))(lambda: query_down(r).start())

    def pass_cache(k):
        @pl.when(z >= k)
        def _():
            owner = s - 2 * k
            cache_up(k - 1, owner).wait_recv()

            if k < last:
                pl.when(z < last)(lambda: cache_up(k, owner).start())

            cache_side(k, owner).start()

        @pl.when(z + k <= last)
        def _():
            owner = s + 2 * k
            cache_down(k - 1, owner).wait_recv()

            if k < last:
                pl.when(z > 0)(lambda: cache_down(k, owner).start())

            cache_side(last + k, owner).start()

    def pass_kv(r):
        @pl.when(z >= 1)
        def _():
            kv_up(0, r).wait_recv()
            kv_side(1, r).start()

    def query_down(r):
        block = rel[r]
        return remote(q2.at[block], qfar.at[block], qd_s.at[r], qd_r.at[r], seq=s - 1)

    def far_rows(j):
        return pl.ds(j * rows, rows)

    def far_up(j):
        there = keys.at[pl.ds(5 * shard + j * rows, rows)]
        return remote(pay.at[far_rows(j)], there, ku_s.at[1, j], ku_r.at[1, j], seq=s + 2)

    def far_side(j):
        there = keys.at[pl.ds(5 * shard + j * rows, rows)]
        return remote(there, there, ks_s.at[2, j], ks_r.at[2, j], seq=mate)

    total_up = remote(dpay, dfar, pd_s.at[0], pd_r.at[0], seq=s + 2)
    total_side = remote(dfar, dfar, pd_s.at[1], pd_r.at[1], seq=mate)

    tile = shard

    def attend(j, at, causal=False, own=(q2, qseg, acc, den)):
        q2, qseg, acc, den = own
        span = pl.ds(pl.multiple_of(at * tile, tile), tile)
        scores = lax.dot_general(
            q2[j], keys[span, :HD], (((1,), (1,)), ((), ())), preferred_element_type=f32
        )
        columns = []
        total = [den[j, g * rows : (g + 1) * rows, :] for g in range(2)]
        for c in range(tile // LANES):
            allowed = qseg[j] == kseg[pl.ds(at * (tile // LANES) + c, 1), :]
            if causal:
                query = j * rows + lax.broadcasted_iota(jnp.int32, (rows, LANES), 0)
                allowed &= c * LANES + lax.broadcasted_iota(jnp.int32, (rows, LANES), 1) <= query
            pair = []
            for g in range(2):
                part = scores[g * rows : (g + 1) * rows, c * LANES : (c + 1) * LANES]
                part = jnp.exp2(jnp.tanh(part * (1.0 / SOFT_CAP)) * (SOFT_CAP * LOG2E))
                part = jnp.where(allowed, part, 0.0)
                total[g] += part
                pair.append(part.astype(bf16))
            columns.append(jnp.concatenate(pair, axis=0))
        for g in range(2):
            den[j, g * rows : (g + 1) * rows, :] = total[g]
        weights = jnp.concatenate(columns, axis=1)
        acc[j] += jnp.dot(weights, keys[span, HD:], preferred_element_type=f32)

    def attend_all(at, causal=False, own=(q2, qseg, acc, den)):
        def body(j, carry):
            attend(j, at, causal, own)
            return carry

        lax.fori_loop(0, 4, body, 0, unroll=4)

    def attend_cache(other):
        attend_all(6 + other)

    loads[0].wait()
    project_kv(0)
    loads[1].wait()
    project_q(0)
    pass_cache(1)
    pass_kv(0)
    gather_in[0].wait_recv()
    gather[4].start()
    gather_in[2].wait_recv()
    gather[5].start()
    weight_copy(0, core).start()
    weight_copy(1, core).start()
    gather_in[1].wait_recv()
    project_kv(1)
    gather_in[3].wait_recv()
    project_kv(2)
    pass_cache(2)
    project_q(1)
    project_q(2)
    gather_in[4].wait_recv()
    gather_in[5].wait_recv()
    project_kv(3)
    project_q(3)
    pass_kv(1)
    attend_all(core, True)
    pass_kv(2)
    loads[3].wait()
    cache_side(0, mate).wait_recv()
    attend_cache(z)

    def cache_tiles(k):
        @pl.when(z >= k)
        def _():
            cache_side(k, mate - 2 * k).wait_recv()
            attend_cache(z - k)

        @pl.when(z + k <= last)
        def _():
            cache_side(last + k, mate + 2 * k).wait_recv()
            attend_cache(z + k)

    pass_kv(3)

    @pl.when(z >= 1)
    def _():
        for r in range(4):
            kv_side(1, r, 1 - core).wait_recv()

    @pl.when((z >= 1) & (z < last) & (core == 1))
    def _():
        pacc[...] = jnp.zeros_like(pacc)
        pden[...] = jnp.zeros_like(pden)
        for r in range(4):
            query_down(r).wait_recv()
        own = (qfar, qsegf, pacc, pden)
        attend_all(2, own=own)
        attend_all(3, own=own)
        flag = spans(z + 1)
        for j in range(4):
            for g in range(2):
                part = pl.ds(g * rows, rows)
                total = jnp.sum(pden[j, part, :], axis=-1, keepdims=True)
                dpay[2 * j + g : 2 * j + g + 1, :] = jnp.broadcast_to(total, (rows, LANES)).T[:1]
                columns = pl.ds(g * HD, HD)
                kept = keys[pl.ds(3 * shard + j * rows, rows), columns]
                pay[far_rows(j), columns] = jnp.where(flag, pacc[j, part, :].astype(bf16), kept)
            far_up(j).start()
        total_up.start()

    cache_tiles(1)
    pass_cache(3)

    @pl.when(core == 1)
    def _():
        for r in range(4):
            kv_side(0, r, 0).wait_recv()
        attend_all(0)

    cache_tiles(2)

    @pl.when(z >= 1)
    def _():
        attend_all(2)
        attend_all(3)

    cache_tiles(3)

    @pl.when((z >= 2) & (core == 1))
    def _():
        for j in range(4):
            far_up(j).wait_recv()
            far_side(j).start()
        total_up.wait_recv()
        total_side.start()

    for m in range(2):
        weight_copy(m, core).wait_recv()
        weight_copy(m + 2, core).start()
    loads[2].wait()

    @pl.when((z >= 2) & (core == 0))
    def _():
        for j in range(4):
            far_side(j).wait_recv()
        total_side.wait_recv()

    def attended(j):
        present = qseg[j] >= 0
        present = present[:, :1]
        parts = []
        for g in range(2):
            total = jnp.sum(den[j, g * rows : (g + 1) * rows, :], axis=-1, keepdims=True)
            safe = jnp.where(present, total, 1.0)
            value = acc[j, g * rows : (g + 1) * rows, :] / safe
            parts.append(jnp.where(present, value, 0.0).astype(bf16))
        return jnp.concatenate(parts, axis=1)

    def finish(j):
        @pl.when(z >= 2)
        def _():
            attend(j, 5)

            @pl.when(core == 0)
            def _():
                flag = spans(z)
                at = pl.ds(pl.multiple_of(5 * shard + j * rows, rows), rows)
                for g in range(2):
                    part = pl.ds(g * rows, rows)
                    more = keys[at, g * HD : (g + 1) * HD].astype(f32)
                    acc[j, part, :] += jnp.where(flag, more, 0.0)
                    total = column(dfar[pl.ds(2 * j + g, 1), :])
                    den[j, part, :] += jnp.where(flag & (lane == 0), total, 0.0)

        abuf[j] = attended(j)

    def rows_copy(m, block):
        there = (ax, ay)[m % 2].at[m // 2]
        return remote(abuf.at[block], there, at_s.at[m], at_r.at[m], head=(hx, hy)[m % 2])

    def sum_copy(m):
        return remote(sbuf.at[m], rbuf.at[m], rs_s.at[m], rs_r.at[m], head=(hy, hx)[m])

    def left(a, weight=None):
        return jnp.dot(a, wo[:, :wide] if weight is None else weight[...], preferred_element_type=f32)

    def right(a, weight=None):
        return jnp.dot(a, wo[:, wide:] if weight is None else weight[...], preferred_element_type=f32)

    sent = (hd, hd, hx, hy)
    finish(hd)
    rows_copy(0, hd).start()
    rows_copy(1, hd).start()
    finish(hx)
    rows_copy(2, hx).start()
    finish(hy)
    rows_copy(3, hy).start()
    for m in range(2):
        weight_copy(m + 2, 1 - core).wait_recv()
    rows_copy(0, hd).wait_recv()
    sbuf[0] = (left(abuf[hy]) + left(ax[0], wx)).astype(bf16)
    sum_copy(0).start()
    rows_copy(1, hd).wait_recv()
    sbuf[1] = (right(abuf[hx]) + right(ay[0], wy)).astype(bf16)
    sum_copy(1).start()
    finish(h)
    hold[0] = left(abuf[h])
    hold[1] = right(abuf[h])
    rows_copy(2, hx).wait_recv()
    hold[0] += left(ax[1], wx)
    rows_copy(3, hy).wait_recv()
    hold[1] += right(ay[1], wy)
    sum_copy(0).wait_recv()
    branch_l = hold[0] + rbuf[0].astype(f32)
    sum_copy(1).wait_recv()
    branch_r = hold[1] + rbuf[1].astype(f32)
    square = jnp.sum(branch_l * branch_l, axis=-1, keepdims=True) + jnp.sum(
        branch_r * branch_r, axis=-1, keepdims=True
    )
    scale = lax.rsqrt(square / (2 * wide) + EPSILON)
    out_ref[:, :wide] = (
        tok_ref[:, :wide].astype(f32) + branch_l * scale * og_ref[:, :wide]
    ).astype(bf16)
    out_ref[:, wide:] = (
        tok_ref[:, wide:].astype(f32) + branch_r * scale * og_ref[:, wide:]
    ).astype(bf16)

    for i in range(n_seq - 1):
        ints[i].wait_send()
    for copy in gather:
        copy.wait_send()
    for m in range(4):
        rows_copy(m, sent[m]).wait_send()
        weight_copy(m, core).wait_send()
    for m in range(2):
        sum_copy(m).wait_send()
    cache_side(0, s).wait_send()
    for k in range(chips - 1):
        @pl.when((z < last) & (z >= k))
        def _():
            cache_up(k, s - 2 * k).wait_send()

        @pl.when((z > 0) & (z + k <= last))
        def _():
            cache_down(k, s + 2 * k).wait_send()

    for k in range(1, chips):
        @pl.when(z >= k)
        def _():
            cache_side(k, s - 2 * k).wait_send()

        @pl.when(z + k <= last)
        def _():
            cache_side(last + k, s + 2 * k).wait_send()

    for r in range(4):
        @pl.when(z < last)
        def _():
            kv_up(0, r).wait_send()

        @pl.when(core == 0)
        def _():
            kv_side(0, r).wait_send()

        @pl.when(z >= 1)
        def _():
            kv_side(1, r).wait_send()

        @pl.when((z >= 2) & (core == 0))
        def _():
            query_down(r).wait_send()

        @pl.when((z >= 1) & (z < last) & (core == 1))
        def _():
            far_up(r).wait_send()

        @pl.when((z >= 2) & (core == 1))
        def _():
            far_side(r).wait_send()

    @pl.when((z >= 1) & (z < last) & (core == 1))
    def _():
        total_up.wait_send()

    @pl.when((z >= 2) & (core == 1))
    def _():
        total_side.wait_send()


def whole_block(
    tokens, in_gain, out_gain, query_weight, keyval_weight, out_weight, cache_entries, segment_ids,
    cache_lengths, block_owners,
):
    n_seq = lax.axis_size("seq")
    rows, width = tokens.shape
    shard = segment_ids.shape[0]
    crow = cache_entries.shape[1]
    n_keys = 6 * shard + n_seq * crow
    angle = (10000.0 ** (-np.arange(HD // 2) * 2.0 / HD)).astype(np.float32)
    vmem, hbm = pl.BlockSpec(memory_space=pltpu.VMEM), pl.BlockSpec(memory_space=pl.ANY)
    f32, bf16, i32 = jnp.float32, jnp.bfloat16, jnp.int32
    dma = pltpu.SemaphoreType.DMA
    hops = n_seq // 2 - 1
    pairs = [dma((n,)) for n in (n_seq - 1, 6, hops, hops, 2 * hops + 1) for _ in range(2)]

    def pack(parts):
        ends = np.cumsum([-(-x.shape[0] // LANES) * LANES for x in parts]).tolist()
        starts = [0] + ends[:-1]
        return sum(jnp.pad(x, (at, ends[-1] - at - x.shape[0])) for x, at in zip(parts, starts))

    small = pack((in_gain, out_gain, jnp.asarray(angle)))
    table = pack((segment_ids, block_owners, cache_lengths))
    return pl.pallas_call(
        block_kernel,
        out_shape=jax.ShapeDtypeStruct((rows, width), bf16),
        in_specs=[vmem] + [hbm] * 6,
        out_specs=vmem,
        scratch_shapes=[
            pltpu.VMEM((n_seq, 8 * -(-(shard // LANES + 1) // 8), LANES), i32),
            pltpu.VMEM((8, LANES), i32),
            pltpu.VMEM((8, LANES), f32),
            pltpu.VMEM((1, width), f32),
            pltpu.VMEM((1, width), f32),
            pltpu.VMEM((4, rows, width), bf16),
            pltpu.VMEM((width, 2 * HD), bf16),
            pltpu.VMEM((width, 2 * HD), bf16),
            pltpu.VMEM((2 * HD, width), bf16),
            pltpu.VMEM((n_keys, 2 * HD), bf16),
            pltpu.VMEM((n_keys // LANES, LANES), i32),
            pltpu.VMEM((4, rows, LANES), i32),
            pltpu.VMEM((4, rows, LANES), f32),
            pltpu.VMEM((4, rows, LANES), f32),
            pltpu.VMEM((4, 2 * rows, HD), bf16),
            pltpu.VMEM((4, 2 * rows, HD), f32),
            pltpu.VMEM((4, 2 * rows, LANES), f32),
            pltpu.VMEM((4, 2 * rows, HD), bf16),
            pltpu.VMEM((4, rows, LANES), i32),
            pltpu.VMEM((4, 2 * rows, HD), f32),
            pltpu.VMEM((4, 2 * rows, LANES), f32),
            pltpu.VMEM((shard, 2 * HD), bf16),
            pltpu.VMEM((8, LANES), f32),
            pltpu.VMEM((8, LANES), f32),
            pltpu.VMEM((4, rows, 2 * HD), bf16),
            pltpu.VMEM((2, rows, 2 * HD), bf16),
            pltpu.VMEM((2, rows, 2 * HD), bf16),
            pltpu.VMEM((2 * HD, width // 2), bf16),
            pltpu.VMEM((2 * HD, width // 2), bf16),
            pltpu.VMEM((2, rows, width // 2), bf16),
            pltpu.VMEM((2, rows, width // 2), bf16),
            pltpu.VMEM((2, rows, width // 2), f32),
            dma((9 + shard // LANES,)),
            *pairs,
            dma((2, 4)), dma((2, 4)), dma((3, 4)), dma((3, 4)),
            dma((4,)), dma((4,)), dma((2,)), dma((2,)),
            dma((4,)), dma((4,)), dma((4,)), dma((4,)), dma((2,)), dma((2,)),
        ],
        compiler_params=pltpu.CompilerParams(
            collective_id=0, has_side_effects=True, vmem_limit_bytes=52 << 20
        ),
        cost_estimate=pl.CostEstimate(
            flops=2 * shard * (6 * HD * width + 8 * n_keys * HD // 4),
            bytes_accessed=6 * HD * 2 * width,
            transcendentals=4 * shard * n_keys,
        ),
        name="block",
    )(
        tokens, small, table, query_weight, keyval_weight, out_weight, cache_entries,
    )


def local(
    tokens,
    in_gain,
    out_gain,
    query_weight,
    keyval_weight,
    out_weight,
    cache_entries,
    segment_ids,
    cache_lengths,
    block_owners,
):
    heads_here = query_weight.shape[1] // HD
    group_size = QH // KVH
    seq_size, head_size = lax.axis_size("seq"), lax.axis_size("head")
    seq_index = lax.axis_index("seq")
    head_index = lax.axis_index("head")
    shared_head = head_index * heads_here // group_size
    stream_rows = segment_ids.shape[0]
    normed_own = rms_scale(tokens, in_gain).astype(jnp.bfloat16)
    chunks = [[lax.all_gather(normed_own, "head", axis=0, tiled=True)]]

    cache_own = lax.dynamic_index_in_dim(cache_entries, shared_head, 0, keepdims=False)
    cache_pairs = lax.all_gather(cache_own, "seq", axis=0, tiled=True)

    table = jnp.concatenate([segment_ids, block_owners])[None]
    bits = 0
    while 1 << bits < seq_size:
        step = 1 << bits
        other = lax.ppermute(table, "seq", [(s, s ^ step) for s in range(seq_size)])
        table = jnp.concatenate([table, other], axis=0)
        bits += 1
    for bit in range(bits):
        pieces = table.reshape(-1, 2, 1 << bit, table.shape[-1])
        pieces = jnp.where((seq_index >> bit) % 2 == 1, pieces[:, ::-1], pieces)
        table = pieces.reshape(seq_size, -1)
    seg_all = table[:, :stream_rows].reshape(-1)
    owners = table[:, stream_rows:].reshape(-1)

    seg_range = jnp.arange(NSEG, dtype=jnp.int32)
    earlier = (seg_all[None, :] >= 0) & (seg_all[None, :] < seg_range[:, None])
    firsts = jnp.sum(earlier.astype(jnp.int32), axis=1)
    slots_all = jnp.arange(seg_all.shape[0], dtype=jnp.int32)
    begin = seq_index * stream_rows
    q_seg = lax.dynamic_slice_in_dim(seg_all, begin, stream_rows)
    q_slot = lax.dynamic_slice_in_dim(slots_all, begin, stream_rows)
    matches = (q_seg[:, None] == seg_range[None, :]).astype(jnp.int32)
    positions = jnp.sum(matches * (cache_lengths - firsts)[None, :], axis=1) + q_slot
    angles = positions.astype(jnp.float32)[:, None] * frequencies(HD)[None, :]
    cosine, sine = jnp.cos(angles), jnp.sin(angles)

    block_index = jnp.arange(owners.shape[0], dtype=jnp.int32)
    same = (owners[:, None] == owners[None, :]) & (block_index[None, :] < block_index[:, None])
    block_rank = jnp.sum(same.astype(jnp.int32), axis=1)
    owner_match = (owners[:, None] == seg_range[None, :]).astype(jnp.int32)
    limits = jnp.sum(owner_match * cache_lengths[None, :], axis=1)
    offsets = jnp.arange(BLK, dtype=jnp.int32)
    usable = (owners[:, None] >= 0) & (
        block_rank[:, None] * BLK + offsets[None, :] < limits[:, None]
    )
    cache_seg = jnp.where(usable, owners[:, None], -2).reshape(-1)
    cache_slot = jnp.full((cache_seg.shape[0],), -1, jnp.int32)

    chunk_rows = stream_rows // len(chunks)
    pairs = []
    for at, parts in enumerate(chunks):
        rows = slice(at * chunk_rows, (at + 1) * chunk_rows)
        pairs.append(
            project(
                keyval_kernel, parts, keyval_weight, 2 * HD, shared_head,
                cosine[rows], sine[rows], (chunk_rows, 2 * HD),
            )
        )
    queries = project(
        query_kernel, sum(chunks, []), query_weight, heads_here * HD, jnp.int32(0),
        cosine, sine, (heads_here, stream_rows, HD),
    )

    hops = seq_size // 4

    def onward(array):
        return lax.ppermute(array, "seq", [(s, s + 2) for s in range(seq_size - 2)])

    def sibling(array):
        return lax.ppermute(array, "seq", [(s, s ^ 1) for s in range(seq_size)])

    key_seg = jnp.where(seg_all >= 0, seg_all, -2)

    def shard_ints(shard):
        inside = (shard >= 0) & (shard < seq_size)
        at = jnp.clip(shard, 0, seq_size - 1) * stream_rows
        seg = lax.dynamic_slice_in_dim(key_seg, at, stream_rows)
        return jnp.where(inside, seg, -2), lax.dynamic_slice_in_dim(slots_all, at, stream_rows)

    mate = seq_index + 1 - 2 * (seq_index % 2)
    travelling = [onward(pair) for pair in pairs]
    waiting, waiting_ints = [sibling(pair) for pair in pairs], [shard_ints(mate)]
    totals = attend(
        queries, q_seg, q_slot, pairs + [cache_pairs], [shard_ints(seq_index), (cache_seg, cache_slot)]
    )
    for hop in range(1, hops + 1):
        travelling, totals = lax.optimization_barrier((travelling, totals))
        following = [onward(pair) for pair in travelling] if hop < hops else []
        beside = [sibling(pair) for pair in travelling]
        parts = waiting + travelling
        ints = waiting_ints + [shard_ints(seq_index - 2 * hop)]
        waiting, waiting_ints = beside, [shard_ints(mate - 2 * hop)]
        if hop < hops:
            totals = attend(queries, q_seg, q_slot, parts, ints, totals)
        else:
            attended = attend(
                queries, q_seg, q_slot, parts + waiting, ints + waiting_ints, totals, last=True
            )
        travelling = following

    branch = lax.psum_scatter(
        jnp.dot(attended, out_weight, preferred_element_type=jnp.float32),
        "head",
        scatter_dimension=0,
        tiled=True,
    )
    return (tokens.astype(jnp.float32) + rms_scale(branch, out_gain)).astype(jnp.bfloat16)


def solution(mesh):
    in_specs = (
        P(("seq", "head"), None),
        P(),
        P(),
        P(None, "head"),
        P(),
        P("head", None),
        P(None, "seq", None),
        P("seq"),
        P(),
        P("seq"),
    )
    out_specs = P(("seq", "head"), None)
    fits = mesh.shape["seq"] == 8 and mesh.shape["head"] == 4
    body = whole_block if fits else local
    return jax.shard_map(body, mesh=mesh, in_specs=in_specs, out_specs=out_specs, check_vma=False)
```

```python
import functools
import math

import jax
import jax.numpy as jnp
import numpy as np
from jax import lax
from jax.experimental import pallas as pl
from jax.experimental.pallas import tpu as pltpu
from jax.sharding import PartitionSpec as P

QH = 8
KVH = 4
HD = 256
NSEG = 64
BLK = 16
LANES = 128
EPSILON = 1e-06
SOFT_CAP = 50.0
FAR = 1073741824
VMEM_BYTES = 40 << 20


def rms_scale(matrix, scaling):
    matrix = matrix.astype(jnp.float32)
    mean_square = jnp.mean(matrix * matrix, axis=-1, keepdims=True)
    return matrix * lax.rsqrt(mean_square + EPSILON) * scaling


def frequencies(extent):
    return 10000.0 ** (-(jnp.arange(extent // 2, dtype=jnp.float32) * 2.0 / extent))


def turn(y, cosine, sine, scale):
    half = y.shape[1] // 2
    a, b = y[:, :half], y[:, half:]
    return (a * cosine - b * sine) * scale, (b * cosine + a * sine) * scale


def query_kernel(count, which_ref, cos_ref, sin_ref, w_ref, *rest):
    parts, out_ref = rest[:count], rest[count]
    half = HD // 2
    x = jnp.concatenate([part[...] for part in parts], axis=0)
    for h in range(w_ref.shape[1] // HD):
        y = jnp.dot(x, w_ref[:, h * HD : (h + 1) * HD], preferred_element_type=jnp.float32)
        a, b = turn(y, cos_ref[...], sin_ref[...], HD**-0.5)
        out_ref[h, :, :half] = a.astype(out_ref.dtype)
        out_ref[h, :, half:] = b.astype(out_ref.dtype)


def keyval_kernel(count, which_ref, cos_ref, sin_ref, w_ref, *rest):
    parts, out_ref = rest[:count], rest[count]
    half = HD // 2
    x = jnp.concatenate([part[...] for part in parts], axis=0)
    y = jnp.dot(x, w_ref[...], preferred_element_type=jnp.float32)
    a, b = turn(y[:, :HD], cos_ref[...], sin_ref[...], 1.0)
    out_ref[:, :half] = a.astype(out_ref.dtype)
    out_ref[:, half:HD] = b.astype(out_ref.dtype)
    out_ref[:, HD:] = y[:, HD:].astype(out_ref.dtype)


def project(body, parts, weight, columns, which, cosine, sine, out_shape):
    rows = cosine.shape[0]
    width = weight.shape[0]
    whole = [pl.BlockSpec(x.shape, lambda i, s: (0, 0)) for x in (cosine, sine)]
    return pl.pallas_call(
        functools.partial(body, len(parts)),
        grid_spec=pltpu.PrefetchScalarGridSpec(
            num_scalar_prefetch=1,
            grid=(1,),
            in_specs=whole
            + [pl.BlockSpec((width, columns), lambda i, s: (0, s[0]))]
            + [pl.BlockSpec(x.shape, lambda i, s: (0, 0)) for x in parts],
            out_specs=pl.BlockSpec(out_shape, lambda i, s: (0,) * len(out_shape)),
        ),
        out_shape=jax.ShapeDtypeStruct(out_shape, jnp.bfloat16),
        compiler_params=pltpu.CompilerParams(vmem_limit_bytes=VMEM_BYTES),
        cost_estimate=pl.CostEstimate(
            flops=2 * rows * width * columns,
            bytes_accessed=2 * width * (columns + rows),
            transcendentals=0,
        ),
        name="project",
    )(which.reshape(1), cosine, sine, weight, *parts)


def fold_blocks(
    heads, q_tile, k_tile, touch_ref, q_ref, qseg_ref, qslot_ref, kseg_ref, kslot_ref, parts, acc, den
):
    q_tiles = q_ref.shape[1] // q_tile
    blocks = kseg_ref.shape[0]
    first = 0
    for part in parts:
        here = part.shape[0] // k_tile

        def step(index, carry, part=part, here=here, first=first):
            qi = index // here
            kj = index % here

            @pl.when(touch_ref[qi * blocks + first + kj] > 0)
            def _():
                rows = pl.ds(pl.multiple_of(qi * q_tile, q_tile), q_tile)
                keys = pl.ds(pl.multiple_of(kj * k_tile, k_tile), k_tile)
                allowed = (kseg_ref[first + kj] == qseg_ref[rows, :]) & (
                    kslot_ref[first + kj] <= qslot_ref[rows, :]
                )
                for h in range(heads):
                    scores = lax.dot_general(
                        q_ref[h, rows, :],
                        part[keys, :HD],
                        (((1,), (1,)), ((), ())),
                        preferred_element_type=jnp.float32,
                    )
                    scores = jnp.tanh(scores * (1.0 / SOFT_CAP))
                    weights = jnp.where(
                        allowed, jnp.exp2(scores * (SOFT_CAP * math.log2(math.e))), 0.0
                    )
                    total = weights[:, :LANES]
                    for c in range(1, k_tile // LANES):
                        total += weights[:, c * LANES : (c + 1) * LANES]
                    den[h, rows, :] += total
                    acc[h, rows, :] += jnp.dot(
                        weights.astype(jnp.bfloat16),
                        part[keys, HD:],
                        preferred_element_type=jnp.float32,
                    )

            return carry

        lax.fori_loop(0, q_tiles * here, step, 0)
        first += here


def middle_kernel(heads, q_tile, k_tile, count, touch_ref, q_ref, qseg_ref, qslot_ref, kseg_ref, kslot_ref, *rest):
    parts, (acc_in, den_in, acc, den) = rest[:count], rest[count:]
    acc[...] = acc_in[...]
    den[...] = den_in[...]
    fold_blocks(
        heads, q_tile, k_tile, touch_ref, q_ref, qseg_ref, qslot_ref, kseg_ref, kslot_ref, parts, acc, den
    )


def first_kernel(heads, q_tile, k_tile, count, touch_ref, q_ref, qseg_ref, qslot_ref, kseg_ref, kslot_ref, *rest):
    parts, (acc, den) = rest[:count], rest[count:]
    acc[...] = jnp.zeros_like(acc)
    den[...] = jnp.zeros_like(den)
    fold_blocks(
        heads, q_tile, k_tile, touch_ref, q_ref, qseg_ref, qslot_ref, kseg_ref, kslot_ref, parts, acc, den
    )


def last_kernel(heads, q_tile, k_tile, count, touch_ref, q_ref, qseg_ref, qslot_ref, kseg_ref, kslot_ref, *rest):
    parts, (acc_in, den_in, out_ref, acc, den) = rest[:count], rest[count:]
    acc[...] = acc_in[...]
    den[...] = den_in[...]
    fold_blocks(
        heads, q_tile, k_tile, touch_ref, q_ref, qseg_ref, qslot_ref, kseg_ref, kslot_ref, parts, acc, den
    )
    present = qseg_ref[...] >= 0
    for h in range(heads):
        total = jnp.sum(den[h], axis=-1, keepdims=True)
        safe = jnp.where(present, total, 1.0)
        out_ref[:, h * HD : (h + 1) * HD] = jnp.where(present, acc[h] / safe, 0.0).astype(
            out_ref.dtype
        )


def attend(queries, q_seg, q_slot, parts, ints, totals=None, last=False):
    heads, rows, _ = queries.shape
    k_seg = jnp.concatenate([pair[0] for pair in ints])
    k_slot = jnp.concatenate([pair[1] for pair in ints])
    q_tile = math.gcd(rows, 256)
    k_tile = math.gcd(*[part.shape[0] for part in parts], 512)
    blocks = k_seg.shape[0] // k_tile
    seg_tiles = q_seg.reshape(-1, q_tile)
    lowest = jnp.min(jnp.where(seg_tiles >= 0, seg_tiles, FAR), axis=1)[:, None]
    highest = jnp.max(seg_tiles, axis=1)[:, None]
    latest = jnp.max(q_slot.reshape(-1, q_tile), axis=1)[:, None]
    near = (k_seg[None] >= lowest) & (k_seg[None] <= highest) & (k_slot[None] <= latest)
    touch = jnp.max(near.astype(jnp.int32).reshape(-1, blocks, k_tile), axis=2).reshape(-1)
    operands = [
        touch,
        queries,
        q_seg[:, None],
        q_slot[:, None],
        k_seg.reshape(blocks, 1, k_tile),
        k_slot.reshape(blocks, 1, k_tile),
        *parts,
    ]
    vmem = pl.BlockSpec(memory_space=pltpu.VMEM)
    sums = [
        jax.ShapeDtypeStruct((heads, rows, HD), jnp.float32),
        jax.ShapeDtypeStruct((heads, rows, LANES), jnp.float32),
    ]
    body, out_shape, out_specs, scratch = first_kernel, sums, [vmem, vmem], []
    if totals is not None:
        operands += list(totals)
        body = middle_kernel
    if last:
        body = last_kernel
        out_shape = jax.ShapeDtypeStruct((rows, heads * HD), jnp.bfloat16)
        out_specs = vmem
        scratch = [pltpu.VMEM(s.shape, s.dtype) for s in sums]
    pairs = heads * rows * k_seg.shape[0]
    return pl.pallas_call(
        functools.partial(body, heads, q_tile, k_tile, len(parts)),
        in_specs=[pl.BlockSpec(memory_space=pltpu.SMEM)] + [vmem] * (len(operands) - 1),
        out_specs=out_specs,
        out_shape=out_shape,
        scratch_shapes=scratch,
        compiler_params=pltpu.CompilerParams(vmem_limit_bytes=VMEM_BYTES),
        cost_estimate=pl.CostEstimate(
            flops=4 * pairs * HD, bytes_accessed=4 * HD * k_seg.shape[0], transcendentals=2 * pairs
        ),
        name="attend",
    )(*operands)


MESH = pl.DeviceIdType.MESH
LOG2E = math.log2(math.e)


def block_kernel(
    tok_ref, small, table, wq_hbm, wkv_hbm, wo_hbm, cache_hbm,
    out_ref,
    tabs, line, freq, ig_ref, og_ref, xbuf, wq, wkv, wo, keys, kseg, qseg, cosine, sine, q2, acc, den, qfar, qsegf, pacc, pden, pay, dpay, dfar, abuf, ax, ay, wx, wy, sbuf, rbuf, hold,
    load_sem, int_s, int_r, ag_s, ag_r, cu_s, cu_r, cd_s, cd_r, cs_s, cs_r, ku_s, ku_r, ks_s, ks_r,
    qd_s, qd_r, pd_s, pd_r, w_s, w_r, at_s, at_r, rs_s, rs_r,
):
    s, h = lax.axis_index("seq"), lax.axis_index("head")
    n_seq = tabs.shape[0]
    chips = n_seq // 2
    z, core = s // 2, s % 2
    mate = s + 1 - 2 * core
    hx, hy, hd = h + 1 - 2 * (h % 2), (h + 2) % 4, 3 - h
    rel = (h, hx, hy, hd)
    rows = tok_ref.shape[0]
    shard = 4 * rows
    half = rows // 2
    wide = out_ref.shape[1] // 2
    crow = cache_hbm.shape[1]
    cbase = 6 * shard
    f32, bf16 = jnp.float32, jnp.bfloat16

    def remote(src, dst, send, recv, seq=None, head=None):
        device = {"seq": s if seq is None else seq, "head": h if head is None else head}
        return pltpu.make_async_remote_copy(
            src_ref=src, dst_ref=dst, send_sem=send, recv_sem=recv, device_id=device, device_id_type=MESH
        )

    barrier = pltpu.get_barrier_semaphore()
    peers = [lax.rem(s + d, n_seq) for d in range(1, n_seq)]
    for peer in peers:
        pl.semaphore_signal(barrier, inc=1, device_id={"seq": peer, "head": h}, device_id_type=MESH)
    for head in (hx, hy):
        pl.semaphore_signal(barrier, inc=1, device_id={"seq": s, "head": head}, device_id_type=MESH)

    kv_cols = pl.ds(pl.multiple_of(h * 2 * HD, 2 * HD), 2 * HD)
    own_cache = keys.at[pl.ds(pl.multiple_of(cbase + s * crow, crow), crow)]
    blocks = shard // LANES
    loads = [
        pltpu.make_async_copy(wkv_hbm.at[:, kv_cols], wkv, load_sem.at[0]),
        pltpu.make_async_copy(wq_hbm, wq, load_sem.at[1]),
        pltpu.make_async_copy(wo_hbm, wo, load_sem.at[2]),
        pltpu.make_async_copy(cache_hbm.at[h], own_cache, load_sem.at[3]),
    ]
    width = 2 * wide
    width = 2 * wide
    early = [
        pltpu.make_async_copy(
            table.at[pl.ds(i * LANES, LANES)],
            tabs.at[s, i] if i < blocks else line.at[i - blocks],
            load_sem.at[7 + i],
        )
        for i in range(blocks + 2)
    ] + [
        pltpu.make_async_copy(small.at[pl.ds(0, width)], ig_ref.at[0], load_sem.at[4]),
        pltpu.make_async_copy(small.at[pl.ds(width, width)], og_ref.at[0], load_sem.at[5]),
        pltpu.make_async_copy(small.at[pl.ds(2 * width, LANES)], freq.at[0], load_sem.at[6]),
    ]
    for load in early + loads:
        load.start()

    for load in early:
        load.wait()

    x = tok_ref[...].astype(f32)
    scale = lax.rsqrt(jnp.mean(x * x, axis=-1, keepdims=True) + EPSILON)
    xbuf[h] = (x * scale * ig_ref[...]).astype(bf16)

    pl.semaphore_wait(barrier, n_seq + 1)

    ints = [
        remote(tabs.at[s], tabs.at[s], int_s.at[d], int_r.at[d], seq=peers[d]) for d in range(n_seq - 1)
    ]
    top, bottom = pl.ds(0, half), pl.ds(half, half)

    def token_copy(m, block, part, head):
        ref = xbuf.at[block, part]
        return remote(ref, ref, ag_s.at[m], ag_r.at[m], head=head)

    gather = [
        token_copy(0, h, top, hx), token_copy(1, h, bottom, hx), token_copy(2, h, bottom, hy),
        token_copy(3, h, top, hy), token_copy(4, hx, top, hy), token_copy(5, hy, bottom, hx),
    ]
    gather_in = [
        token_copy(0, hx, top, hx), token_copy(1, hx, bottom, hx), token_copy(2, hy, bottom, hy),
        token_copy(3, hy, top, hy), token_copy(4, hd, top, hy), token_copy(5, hd, bottom, hx),
    ]

    def cache_ref(owner):
        return keys.at[pl.ds(pl.multiple_of(cbase + owner * crow, crow), crow)]

    def cache_up(k, owner):
        src = cache_hbm.at[h] if k == 0 else cache_ref(owner)
        return remote(src, cache_ref(owner), cu_s.at[k], cu_r.at[k], seq=s + 2)

    def cache_down(k, owner):
        src = cache_hbm.at[h] if k == 0 else cache_ref(owner)
        return remote(src, cache_ref(owner), cd_s.at[k], cd_r.at[k], seq=s - 2)

    def cache_side(i, owner):
        src = cache_hbm.at[h] if i == 0 else cache_ref(owner)
        return remote(src, cache_ref(owner), cs_s.at[i], cs_r.at[i], seq=mate)

    part_rows = wx.shape[0] // 2

    def weight_copy(m, c):
        span = pl.ds(pl.multiple_of(c * part_rows, part_rows), part_rows)
        there = (wx, wy)[m % 2].at[span]
        if m < 2:
            columns = pl.ds(m * wide, wide)
            return remote(wo_hbm.at[span, columns], there, w_s.at[m], w_r.at[m], head=(hx, hy)[m])
        return remote(there, there, w_s.at[m], w_r.at[m], seq=mate)

    last = chips - 1
    lane = lax.broadcasted_iota(jnp.int32, (1, LANES), 1)

    def column(row):
        return jnp.broadcast_to(row, (LANES, LANES)).T

    here = crow // BLK
    mine = lax.broadcasted_iota(jnp.int32, (here, LANES), 0) == lane - s * here
    owned = jnp.where(mine, column(line[:1, :])[:here], 0)
    tabs[s, blocks : blocks + 1, :] = jnp.sum(owned, axis=0, keepdims=True)
    for i in range(n_seq - 1):
        ints[i].start()

    @pl.when(z < last)
    def _():
        cache_up(0, s).start()

    @pl.when(z > 0)
    def _():
        cache_down(0, s).start()

    cache_side(0, s).start()

    for m in (0, 2, 1, 3):
        gather[m].start()

    acc[...] = jnp.zeros_like(acc)
    den[...] = jnp.zeros_like(den)
    for d in range(n_seq - 1):
        source = lax.rem(s + n_seq - 1 - d, n_seq)
        remote(tabs.at[source], tabs.at[source], int_s.at[d], int_r.at[d], seq=source).wait_recv()

    segs = lax.broadcasted_iota(jnp.int32, (NSEG, LANES), 0)
    count = jnp.zeros((NSEG, LANES), jnp.int32)
    owners = jnp.zeros((1, LANES), jnp.int32)
    for p in range(n_seq):
        for i in range(blocks):
            row = tabs[p, i : i + 1, :]
            count += jnp.where((row >= 0) & (row < segs), 1, 0)
        owners += tabs[p, blocks : blocks + 1, :]
    firsts = jnp.sum(count.astype(f32), axis=1, keepdims=True)
    lengths = column(line[1:2, :].astype(f32))[:NSEG, :1]
    base = lengths - firsts
    for i in range(blocks):
        row = tabs[s, i : i + 1, :]
        start = jnp.sum(jnp.where(segs == row, base, 0.0), axis=0, keepdims=True)
        place = start + (s * shard + i * LANES + lane).astype(f32)
        angle = column(place) * freq[:1, :]
        cosine[i] = jnp.cos(angle)
        sine[i] = jnp.sin(angle)
        qseg[i] = column(row)
        qsegf[i] = column(tabs[jnp.minimum(s + 1, n_seq - 1), i : i + 1, :])

    def spans(b):
        ahead = tabs[jnp.clip(2 * b, 0, n_seq - 2), 0:1, :][:, :1]
        behind = tabs[jnp.clip(2 * b - 4, 0, n_seq - 2), blocks - 1 : blocks, :][:, LANES - 1 :]
        return (ahead == behind) & (ahead >= 0)

    for dz in range(3):
        for c in range(2):
            source = jnp.maximum(z - dz, 0) * 2 + c
            for i in range(blocks):
                row = tabs[source, i : i + 1, :]
                at = (dz * 2 + c) * blocks + i
                hidden = (row < 0) | spans(z) if dz == 2 else row < 0
                kseg[at : at + 1, :] = jnp.where(hidden, -2, row)
    same = (column(owners) == owners) & (
        lax.broadcasted_iota(jnp.int32, (LANES, LANES), 0)
        < lax.broadcasted_iota(jnp.int32, (LANES, LANES), 1)
    )
    rank = jnp.sum(jnp.where(same, 1, 0), axis=0, keepdims=True)
    limit = jnp.sum(jnp.where(segs == owners, lengths, 0.0), axis=0, keepdims=True).astype(jnp.int32)
    filled = jnp.where(owners >= 0, jnp.clip(limit - BLK * rank, 0, BLK), 0)
    owner_col, filled_col = column(owners), column(filled)
    per = LANES // BLK
    pick = lax.broadcasted_iota(jnp.int32, (per, LANES), 0) == lane // BLK
    for i in range(n_seq * crow // LANES):
        part = slice(i * per, (i + 1) * per)
        who = jnp.sum(jnp.where(pick, owner_col[part], 0), axis=0, keepdims=True)
        many = jnp.sum(jnp.where(pick, filled_col[part], 0), axis=0, keepdims=True)
        at = 6 * blocks + i
        kseg[at : at + 1, :] = jnp.where(lane % BLK < many, who, -2)

    def kv_ref(dz, c, block):
        return keys.at[pl.ds(pl.multiple_of((dz * 2 + c) * shard + block * rows, rows), rows)]

    def kv_up(dz, r):
        return remote(
            kv_ref(dz, core, rel[r]), kv_ref(dz + 1, core, rel[r]), ku_s.at[dz, r], ku_r.at[dz, r], seq=s + 2
        )

    def kv_side(dz, r, c=None):
        ref = kv_ref(dz, core if c is None else c, rel[r])
        return remote(ref, ref, ks_s.at[dz, r], ks_r.at[dz, r], seq=mate)

    def project_kv(r):
        block = rel[r]
        y = jnp.dot(xbuf[block], wkv[...], preferred_element_type=f32)
        a, b = turn(y[:, :HD], cosine[block], sine[block], 1.0)
        at = pl.ds(pl.multiple_of(core * shard + block * rows, rows), rows)
        keys[at, : HD // 2] = a.astype(bf16)
        keys[at, HD // 2 : HD] = b.astype(bf16)
        keys[at, HD:] = y[:, HD:].astype(bf16)

        @pl.when(z < last)
        def _():
            kv_up(0, r).start()

        @pl.when(core == 0)
        def _():
            kv_side(0, r).start()

    def project_q(r):
        block = rel[r]
        y = jnp.dot(xbuf[block], wq[...], preferred_element_type=f32)
        for g in range(2):
            a, b = turn(y[:, g * HD : (g + 1) * HD], cosine[block], sine[block], HD**-0.5)
            q2[block, g * rows : (g + 1) * rows, : HD // 2] = a.astype(bf16)
            q2[block, g * rows : (g + 1) * rows, HD // 2 :] = b.astype(bf16)
        pl.when((z >= 2) & (core == 0))(lambda: query_down(r).start())

    def pass_cache(k):
        @pl.when(z >= k)
        def _():
            owner = s - 2 * k
            cache_up(k - 1, owner).wait_recv()

            if k < last:
                pl.when(z < last)(lambda: cache_up(k, owner).start())

            cache_side(k, owner).start()

        @pl.when(z + k <= last)
        def _():
            owner = s + 2 * k
            cache_down(k - 1, owner).wait_recv()

            if k < last:
                pl.when(z > 0)(lambda: cache_down(k, owner).start())

            cache_side(last + k, owner).start()

    def pass_kv(r):
        @pl.when(z >= 1)
        def _():
            kv_up(0, r).wait_recv()
            kv_side(1, r).start()

    def query_down(r):
        block = rel[r]
        return remote(q2.at[block], qfar.at[block], qd_s.at[r], qd_r.at[r], seq=s - 1)

    def far_rows(j):
        return pl.ds(j * rows, rows)

    def far_up(j):
        there = keys.at[pl.ds(5 * shard + j * rows, rows)]
        return remote(pay.at[far_rows(j)], there, ku_s.at[1, j], ku_r.at[1, j], seq=s + 2)

    def far_side(j):
        there = keys.at[pl.ds(5 * shard + j * rows, rows)]
        return remote(there, there, ks_s.at[2, j], ks_r.at[2, j], seq=mate)

    total_up = remote(dpay, dfar, pd_s.at[0], pd_r.at[0], seq=s + 2)
    total_side = remote(dfar, dfar, pd_s.at[1], pd_r.at[1], seq=mate)

    tile = shard

    def attend(j, at, causal=False, own=(q2, qseg, acc, den)):
        q2, qseg, acc, den = own
        span = pl.ds(pl.multiple_of(at * tile, tile), tile)
        scores = lax.dot_general(
            q2[j], keys[span, :HD], (((1,), (1,)), ((), ())), preferred_element_type=f32
        )
        columns = []
        total = [den[j, g * rows : (g + 1) * rows, :] for g in range(2)]
        for c in range(tile // LANES):
            allowed = qseg[j] == kseg[pl.ds(at * (tile // LANES) + c, 1), :]
            if causal:
                query = j * rows + lax.broadcasted_iota(jnp.int32, (rows, LANES), 0)
                allowed &= c * LANES + lax.broadcasted_iota(jnp.int32, (rows, LANES), 1) <= query
            pair = []
            for g in range(2):
                part = scores[g * rows : (g + 1) * rows, c * LANES : (c + 1) * LANES]
                part = jnp.exp2(jnp.tanh(part * (1.0 / SOFT_CAP)) * (SOFT_CAP * LOG2E))
                part = jnp.where(allowed, part, 0.0)
                total[g] += part
                pair.append(part.astype(bf16))
            columns.append(jnp.concatenate(pair, axis=0))
        for g in range(2):
            den[j, g * rows : (g + 1) * rows, :] = total[g]
        weights = jnp.concatenate(columns, axis=1)
        acc[j] += jnp.dot(weights, keys[span, HD:], preferred_element_type=f32)

    def attend_all(at, causal=False, own=(q2, qseg, acc, den)):
        def body(j, carry):
            attend(j, at, causal, own)
            return carry

        lax.fori_loop(0, 4, body, 0, unroll=4)

    def attend_cache(other):
        attend_all(6 + other)

    loads[0].wait()
    project_kv(0)
    loads[1].wait()
    project_q(0)
    pass_cache(1)
    pass_kv(0)
    gather_in[0].wait_recv()
    gather[4].start()
    gather_in[2].wait_recv()
    gather[5].start()
    weight_copy(0, core).start()
    weight_copy(1, core).start()
    gather_in[1].wait_recv()
    project_kv(1)
    gather_in[3].wait_recv()
    project_kv(2)
    pass_cache(2)
    project_q(1)
    project_q(2)
    gather_in[4].wait_recv()
    gather_in[5].wait_recv()
    project_kv(3)
    project_q(3)
    pass_kv(1)
    attend_all(core, True)
    pass_kv(2)
    loads[3].wait()
    cache_side(0, mate).wait_recv()
    attend_cache(z)

    def cache_tiles(k):
        @pl.when(z >= k)
        def _():
            cache_side(k, mate - 2 * k).wait_recv()
            attend_cache(z - k)

        @pl.when(z + k <= last)
        def _():
            cache_side(last + k, mate + 2 * k).wait_recv()
            attend_cache(z + k)

    pass_kv(3)

    @pl.when(z >= 1)
    def _():
        for r in range(4):
            kv_side(1, r, 1 - core).wait_recv()

    @pl.when((z >= 1) & (z < last) & (core == 1))
    def _():
        pacc[...] = jnp.zeros_like(pacc)
        pden[...] = jnp.zeros_like(pden)
        for r in range(4):
            query_down(r).wait_recv()
        own = (qfar, qsegf, pacc, pden)
        attend_all(2, own=own)
        attend_all(3, own=own)
        flag = spans(z + 1)
        for j in range(4):
            for g in range(2):
                part = pl.ds(g * rows, rows)
                total = jnp.sum(pden[j, part, :], axis=-1, keepdims=True)
                dpay[2 * j + g : 2 * j + g + 1, :] = jnp.broadcast_to(total, (rows, LANES)).T[:1]
                columns = pl.ds(g * HD, HD)
                kept = keys[pl.ds(3 * shard + j * rows, rows), columns]
                pay[far_rows(j), columns] = jnp.where(flag, pacc[j, part, :].astype(bf16), kept)
            far_up(j).start()
        total_up.start()

    cache_tiles(1)
    pass_cache(3)

    @pl.when(core == 1)
    def _():
        for r in range(4):
            kv_side(0, r, 0).wait_recv()
        attend_all(0)

    cache_tiles(2)

    @pl.when(z >= 1)
    def _():
        attend_all(2)
        attend_all(3)

    cache_tiles(3)

    @pl.when((z >= 2) & (core == 1))
    def _():
        for j in range(4):
            far_up(j).wait_recv()
            far_side(j).start()
        total_up.wait_recv()
        total_side.start()

    for m in range(2):
        weight_copy(m, core).wait_recv()
        weight_copy(m + 2, core).start()
    loads[2].wait()

    @pl.when((z >= 2) & (core == 0))
    def _():
        for j in range(4):
            far_side(j).wait_recv()
        total_side.wait_recv()

    def attended(j):
        present = qseg[j] >= 0
        present = present[:, :1]
        parts = []
        for g in range(2):
            total = jnp.sum(den[j, g * rows : (g + 1) * rows, :], axis=-1, keepdims=True)
            safe = jnp.where(present, total, 1.0)
            value = acc[j, g * rows : (g + 1) * rows, :] / safe
            parts.append(jnp.where(present, value, 0.0).astype(bf16))
        return jnp.concatenate(parts, axis=1)

    def finish(j):
        @pl.when(z >= 2)
        def _():
            attend(j, 5)

            @pl.when(core == 0)
            def _():
                flag = spans(z)
                at = pl.ds(pl.multiple_of(5 * shard + j * rows, rows), rows)
                for g in range(2):
                    part = pl.ds(g * rows, rows)
                    more = keys[at, g * HD : (g + 1) * HD].astype(f32)
                    acc[j, part, :] += jnp.where(flag, more, 0.0)
                    total = column(dfar[pl.ds(2 * j + g, 1), :])
                    den[j, part, :] += jnp.where(flag & (lane == 0), total, 0.0)

        abuf[j] = attended(j)

    def rows_copy(m, block):
        there = (ax, ay)[m % 2].at[m // 2]
        return remote(abuf.at[block], there, at_s.at[m], at_r.at[m], head=(hx, hy)[m % 2])

    def sum_copy(m):
        return remote(sbuf.at[m], rbuf.at[m], rs_s.at[m], rs_r.at[m], head=(hy, hx)[m])

    def left(a, weight=None):
        return jnp.dot(a, wo[:, :wide] if weight is None else weight[...], preferred_element_type=f32)

    def right(a, weight=None):
        return jnp.dot(a, wo[:, wide:] if weight is None else weight[...], preferred_element_type=f32)

    sent = (hd, hd, hx, hy)
    finish(hd)
    rows_copy(0, hd).start()
    rows_copy(1, hd).start()
    finish(hx)
    rows_copy(2, hx).start()
    finish(hy)
    rows_copy(3, hy).start()
    for m in range(2):
        weight_copy(m + 2, 1 - core).wait_recv()
    rows_copy(0, hd).wait_recv()
    sbuf[0] = (left(abuf[hy]) + left(ax[0], wx)).astype(bf16)
    sum_copy(0).start()
    rows_copy(1, hd).wait_recv()
    sbuf[1] = (right(abuf[hx]) + right(ay[0], wy)).astype(bf16)
    sum_copy(1).start()
    finish(h)
    hold[0] = left(abuf[h])
    hold[1] = right(abuf[h])
    rows_copy(2, hx).wait_recv()
    hold[0] += left(ax[1], wx)
    rows_copy(3, hy).wait_recv()
    hold[1] += right(ay[1], wy)
    sum_copy(0).wait_recv()
    branch_l = hold[0] + rbuf[0].astype(f32)
    sum_copy(1).wait_recv()
    branch_r = hold[1] + rbuf[1].astype(f32)
    square = jnp.sum(branch_l * branch_l, axis=-1, keepdims=True) + jnp.sum(
        branch_r * branch_r, axis=-1, keepdims=True
    )
    scale = lax.rsqrt(square / (2 * wide) + EPSILON)
    out_ref[:, :wide] = (
        tok_ref[:, :wide].astype(f32) + branch_l * scale * og_ref[:, :wide]
    ).astype(bf16)
    out_ref[:, wide:] = (
        tok_ref[:, wide:].astype(f32) + branch_r * scale * og_ref[:, wide:]
    ).astype(bf16)

    for i in range(n_seq - 1):
        ints[i].wait_send()
    for copy in gather:
        copy.wait_send()
    for m in range(4):
        rows_copy(m, sent[m]).wait_send()
        weight_copy(m, core).wait_send()
    for m in range(2):
        sum_copy(m).wait_send()
    cache_side(0, s).wait_send()
    for k in range(chips - 1):
        @pl.when((z < last) & (z >= k))
        def _():
            cache_up(k, s - 2 * k).wait_send()

        @pl.when((z > 0) & (z + k <= last))
        def _():
            cache_down(k, s + 2 * k).wait_send()

    for k in range(1, chips):
        @pl.when(z >= k)
        def _():
            cache_side(k, s - 2 * k).wait_send()

        @pl.when(z + k <= last)
        def _():
            cache_side(last + k, s + 2 * k).wait_send()

    for r in range(4):
        @pl.when(z < last)
        def _():
            kv_up(0, r).wait_send()

        @pl.when(core == 0)
        def _():
            kv_side(0, r).wait_send()

        @pl.when(z >= 1)
        def _():
            kv_side(1, r).wait_send()

        @pl.when((z >= 2) & (core == 0))
        def _():
            query_down(r).wait_send()

        @pl.when((z >= 1) & (z < last) & (core == 1))
        def _():
            far_up(r).wait_send()

        @pl.when((z >= 2) & (core == 1))
        def _():
            far_side(r).wait_send()

    @pl.when((z >= 1) & (z < last) & (core == 1))
    def _():
        total_up.wait_send()

    @pl.when((z >= 2) & (core == 1))
    def _():
        total_side.wait_send()


def whole_block(
    tokens, in_gain, out_gain, query_weight, keyval_weight, out_weight, cache_entries, segment_ids,
    cache_lengths, block_owners,
):
    n_seq = lax.axis_size("seq")
    rows, width = tokens.shape
    shard = segment_ids.shape[0]
    crow = cache_entries.shape[1]
    n_keys = 6 * shard + n_seq * crow
    angle = (10000.0 ** (-np.arange(HD // 2) * 2.0 / HD)).astype(np.float32)
    vmem, hbm = pl.BlockSpec(memory_space=pltpu.VMEM), pl.BlockSpec(memory_space=pl.ANY)
    f32, bf16, i32 = jnp.float32, jnp.bfloat16, jnp.int32
    dma = pltpu.SemaphoreType.DMA
    hops = n_seq // 2 - 1
    pairs = [dma((n,)) for n in (n_seq - 1, 6, hops, hops, 2 * hops + 1) for _ in range(2)]

    def pack(parts):
        ends = np.cumsum([-(-x.shape[0] // LANES) * LANES for x in parts]).tolist()
        starts = [0] + ends[:-1]
        return sum(jnp.pad(x, (at, ends[-1] - at - x.shape[0])) for x, at in zip(parts, starts))

    small = pack((in_gain, out_gain, jnp.asarray(angle)))
    table = pack((segment_ids, block_owners, cache_lengths))
    return pl.pallas_call(
        block_kernel,
        out_shape=jax.ShapeDtypeStruct((rows, width), bf16),
        in_specs=[vmem] + [hbm] * 6,
        out_specs=vmem,
        scratch_shapes=[
            pltpu.VMEM((n_seq, 8 * -(-(shard // LANES + 1) // 8), LANES), i32),
            pltpu.VMEM((8, LANES), i32),
            pltpu.VMEM((8, LANES), f32),
            pltpu.VMEM((1, width), f32),
            pltpu.VMEM((1, width), f32),
            pltpu.VMEM((4, rows, width), bf16),
            pltpu.VMEM((width, 2 * HD), bf16),
            pltpu.VMEM((width, 2 * HD), bf16),
            pltpu.VMEM((2 * HD, width), bf16),
            pltpu.VMEM((n_keys, 2 * HD), bf16),
            pltpu.VMEM((n_keys // LANES, LANES), i32),
            pltpu.VMEM((4, rows, LANES), i32),
            pltpu.VMEM((4, rows, LANES), f32),
            pltpu.VMEM((4, rows, LANES), f32),
            pltpu.VMEM((4, 2 * rows, HD), bf16),
            pltpu.VMEM((4, 2 * rows, HD), f32),
            pltpu.VMEM((4, 2 * rows, LANES), f32),
            pltpu.VMEM((4, 2 * rows, HD), bf16),
            pltpu.VMEM((4, rows, LANES), i32),
            pltpu.VMEM((4, 2 * rows, HD), f32),
            pltpu.VMEM((4, 2 * rows, LANES), f32),
            pltpu.VMEM((shard, 2 * HD), bf16),
            pltpu.VMEM((8, LANES), f32),
            pltpu.VMEM((8, LANES), f32),
            pltpu.VMEM((4, rows, 2 * HD), bf16),
            pltpu.VMEM((2, rows, 2 * HD), bf16),
            pltpu.VMEM((2, rows, 2 * HD), bf16),
            pltpu.VMEM((2 * HD, width // 2), bf16),
            pltpu.VMEM((2 * HD, width // 2), bf16),
            pltpu.VMEM((2, rows, width // 2), bf16),
            pltpu.VMEM((2, rows, width // 2), bf16),
            pltpu.VMEM((2, rows, width // 2), f32),
            dma((9 + shard // LANES,)),
            *pairs,
            dma((2, 4)), dma((2, 4)), dma((3, 4)), dma((3, 4)),
            dma((4,)), dma((4,)), dma((2,)), dma((2,)),
            dma((4,)), dma((4,)), dma((4,)), dma((4,)), dma((2,)), dma((2,)),
        ],
        compiler_params=pltpu.CompilerParams(
            collective_id=0, has_side_effects=True, vmem_limit_bytes=52 << 20
        ),
        cost_estimate=pl.CostEstimate(
            flops=2 * shard * (6 * HD * width + 8 * n_keys * HD // 4),
            bytes_accessed=6 * HD * 2 * width,
            transcendentals=4 * shard * n_keys,
        ),
        name="block",
    )(
        tokens, small, table, query_weight, keyval_weight, out_weight, cache_entries,
    )


def local(
    tokens,
    in_gain,
    out_gain,
    query_weight,
    keyval_weight,
    out_weight,
    cache_entries,
    segment_ids,
    cache_lengths,
    block_owners,
):
    heads_here = query_weight.shape[1] // HD
    group_size = QH // KVH
    seq_size, head_size = lax.axis_size("seq"), lax.axis_size("head")
    seq_index = lax.axis_index("seq")
    head_index = lax.axis_index("head")
    shared_head = head_index * heads_here // group_size
    stream_rows = segment_ids.shape[0]
    normed_own = rms_scale(tokens, in_gain).astype(jnp.bfloat16)
    chunks = [[lax.all_gather(normed_own, "head", axis=0, tiled=True)]]

    cache_own = lax.dynamic_index_in_dim(cache_entries, shared_head, 0, keepdims=False)
    cache_pairs = lax.all_gather(cache_own, "seq", axis=0, tiled=True)

    table = jnp.concatenate([segment_ids, block_owners])[None]
    bits = 0
    while 1 << bits < seq_size:
        step = 1 << bits
        other = lax.ppermute(table, "seq", [(s, s ^ step) for s in range(seq_size)])
        table = jnp.concatenate([table, other], axis=0)
        bits += 1
    for bit in range(bits):
        pieces = table.reshape(-1, 2, 1 << bit, table.shape[-1])
        pieces = jnp.where((seq_index >> bit) % 2 == 1, pieces[:, ::-1], pieces)
        table = pieces.reshape(seq_size, -1)
    seg_all = table[:, :stream_rows].reshape(-1)
    owners = table[:, stream_rows:].reshape(-1)

    seg_range = jnp.arange(NSEG, dtype=jnp.int32)
    earlier = (seg_all[None, :] >= 0) & (seg_all[None, :] < seg_range[:, None])
    firsts = jnp.sum(earlier.astype(jnp.int32), axis=1)
    slots_all = jnp.arange(seg_all.shape[0], dtype=jnp.int32)
    begin = seq_index * stream_rows
    q_seg = lax.dynamic_slice_in_dim(seg_all, begin, stream_rows)
    q_slot = lax.dynamic_slice_in_dim(slots_all, begin, stream_rows)
    matches = (q_seg[:, None] == seg_range[None, :]).astype(jnp.int32)
    positions = jnp.sum(matches * (cache_lengths - firsts)[None, :], axis=1) + q_slot
    angles = positions.astype(jnp.float32)[:, None] * frequencies(HD)[None, :]
    cosine, sine = jnp.cos(angles), jnp.sin(angles)

    block_index = jnp.arange(owners.shape[0], dtype=jnp.int32)
    same = (owners[:, None] == owners[None, :]) & (block_index[None, :] < block_index[:, None])
    block_rank = jnp.sum(same.astype(jnp.int32), axis=1)
    owner_match = (owners[:, None] == seg_range[None, :]).astype(jnp.int32)
    limits = jnp.sum(owner_match * cache_lengths[None, :], axis=1)
    offsets = jnp.arange(BLK, dtype=jnp.int32)
    usable = (owners[:, None] >= 0) & (
        block_rank[:, None] * BLK + offsets[None, :] < limits[:, None]
    )
    cache_seg = jnp.where(usable, owners[:, None], -2).reshape(-1)
    cache_slot = jnp.full((cache_seg.shape[0],), -1, jnp.int32)

    chunk_rows = stream_rows // len(chunks)
    pairs = []
    for at, parts in enumerate(chunks):
        rows = slice(at * chunk_rows, (at + 1) * chunk_rows)
        pairs.append(
            project(
                keyval_kernel, parts, keyval_weight, 2 * HD, shared_head,
                cosine[rows], sine[rows], (chunk_rows, 2 * HD),
            )
        )
    queries = project(
        query_kernel, sum(chunks, []), query_weight, heads_here * HD, jnp.int32(0),
        cosine, sine, (heads_here, stream_rows, HD),
    )

    hops = seq_size // 4

    def onward(array):
        return lax.ppermute(array, "seq", [(s, s + 2) for s in range(seq_size - 2)])

    def sibling(array):
        return lax.ppermute(array, "seq", [(s, s ^ 1) for s in range(seq_size)])

    key_seg = jnp.where(seg_all >= 0, seg_all, -2)

    def shard_ints(shard):
        inside = (shard >= 0) & (shard < seq_size)
        at = jnp.clip(shard, 0, seq_size - 1) * stream_rows
        seg = lax.dynamic_slice_in_dim(key_seg, at, stream_rows)
        return jnp.where(inside, seg, -2), lax.dynamic_slice_in_dim(slots_all, at, stream_rows)

    mate = seq_index + 1 - 2 * (seq_index % 2)
    travelling = [onward(pair) for pair in pairs]
    waiting, waiting_ints = [sibling(pair) for pair in pairs], [shard_ints(mate)]
    totals = attend(
        queries, q_seg, q_slot, pairs + [cache_pairs], [shard_ints(seq_index), (cache_seg, cache_slot)]
    )
    for hop in range(1, hops + 1):
        travelling, totals = lax.optimization_barrier((travelling, totals))
        following = [onward(pair) for pair in travelling] if hop < hops else []
        beside = [sibling(pair) for pair in travelling]
        parts = waiting + travelling
        ints = waiting_ints + [shard_ints(seq_index - 2 * hop)]
        waiting, waiting_ints = beside, [shard_ints(mate - 2 * hop)]
        if hop < hops:
            totals = attend(queries, q_seg, q_slot, parts, ints, totals)
        else:
            attended = attend(
                queries, q_seg, q_slot, parts + waiting, ints + waiting_ints, totals, last=True
            )
        travelling = following

    branch = lax.psum_scatter(
        jnp.dot(attended, out_weight, preferred_element_type=jnp.float32),
        "head",
        scatter_dimension=0,
        tiled=True,
    )
    return (tokens.astype(jnp.float32) + rms_scale(branch, out_gain)).astype(jnp.bfloat16)


def solution(mesh):
    in_specs = (
        P(("seq", "head"), None),
        P(),
        P(),
        P(None, "head"),
        P(),
        P("head", None),
        P(None, "seq", None),
        P("seq"),
        P(),
        P("seq"),
    )
    out_specs = P(("seq", "head"), None)
    fits = mesh.shape["seq"] == 8 and mesh.shape["head"] == 4
    body = whole_block if fits else local
    return jax.shard_map(body, mesh=mesh, in_specs=in_specs, out_specs=out_specs, check_vma=False)
```

```python
import functools
import math

import jax
import jax.numpy as jnp
import numpy as np
from jax import lax
from jax.experimental import pallas as pl
from jax.experimental.pallas import tpu as pltpu
from jax.sharding import PartitionSpec as P

QH = 8
KVH = 4
HD = 256
NSEG = 64
BLK = 16
LANES = 128
EPSILON = 1e-06
SOFT_CAP = 50.0
FAR = 1073741824
VMEM_BYTES = 40 << 20


def rms_scale(matrix, scaling):
    matrix = matrix.astype(jnp.float32)
    mean_square = jnp.mean(matrix * matrix, axis=-1, keepdims=True)
    return matrix * lax.rsqrt(mean_square + EPSILON) * scaling


def frequencies(extent):
    return 10000.0 ** (-(jnp.arange(extent // 2, dtype=jnp.float32) * 2.0 / extent))


def turn(y, cosine, sine, scale):
    half = y.shape[1] // 2
    a, b = y[:, :half], y[:, half:]
    return (a * cosine - b * sine) * scale, (b * cosine + a * sine) * scale


def query_kernel(count, which_ref, cos_ref, sin_ref, w_ref, *rest):
    parts, out_ref = rest[:count], rest[count]
    half = HD // 2
    x = jnp.concatenate([part[...] for part in parts], axis=0)
    for h in range(w_ref.shape[1] // HD):
        y = jnp.dot(x, w_ref[:, h * HD : (h + 1) * HD], preferred_element_type=jnp.float32)
        a, b = turn(y, cos_ref[...], sin_ref[...], HD**-0.5)
        out_ref[h, :, :half] = a.astype(out_ref.dtype)
        out_ref[h, :, half:] = b.astype(out_ref.dtype)


def keyval_kernel(count, which_ref, cos_ref, sin_ref, w_ref, *rest):
    parts, out_ref = rest[:count], rest[count]
    half = HD // 2
    x = jnp.concatenate([part[...] for part in parts], axis=0)
    y = jnp.dot(x, w_ref[...], preferred_element_type=jnp.float32)
    a, b = turn(y[:, :HD], cos_ref[...], sin_ref[...], 1.0)
    out_ref[:, :half] = a.astype(out_ref.dtype)
    out_ref[:, half:HD] = b.astype(out_ref.dtype)
    out_ref[:, HD:] = y[:, HD:].astype(out_ref.dtype)


def project(body, parts, weight, columns, which, cosine, sine, out_shape):
    rows = cosine.shape[0]
    width = weight.shape[0]
    whole = [pl.BlockSpec(x.shape, lambda i, s: (0, 0)) for x in (cosine, sine)]
    return pl.pallas_call(
        functools.partial(body, len(parts)),
        grid_spec=pltpu.PrefetchScalarGridSpec(
            num_scalar_prefetch=1,
            grid=(1,),
            in_specs=whole
            + [pl.BlockSpec((width, columns), lambda i, s: (0, s[0]))]
            + [pl.BlockSpec(x.shape, lambda i, s: (0, 0)) for x in parts],
            out_specs=pl.BlockSpec(out_shape, lambda i, s: (0,) * len(out_shape)),
        ),
        out_shape=jax.ShapeDtypeStruct(out_shape, jnp.bfloat16),
        compiler_params=pltpu.CompilerParams(vmem_limit_bytes=VMEM_BYTES),
        cost_estimate=pl.CostEstimate(
            flops=2 * rows * width * columns,
            bytes_accessed=2 * width * (columns + rows),
            transcendentals=0,
        ),
        name="project",
    )(which.reshape(1), cosine, sine, weight, *parts)


def fold_blocks(
    heads, q_tile, k_tile, touch_ref, q_ref, qseg_ref, qslot_ref, kseg_ref, kslot_ref, parts, acc, den
):
    q_tiles = q_ref.shape[1] // q_tile
    blocks = kseg_ref.shape[0]
    first = 0
    for part in parts:
        here = part.shape[0] // k_tile

        def step(index, carry, part=part, here=here, first=first):
            qi = index // here
            kj = index % here

            @pl.when(touch_ref[qi * blocks + first + kj] > 0)
            def _():
                rows = pl.ds(pl.multiple_of(qi * q_tile, q_tile), q_tile)
                keys = pl.ds(pl.multiple_of(kj * k_tile, k_tile), k_tile)
                allowed = (kseg_ref[first + kj] == qseg_ref[rows, :]) & (
                    kslot_ref[first + kj] <= qslot_ref[rows, :]
                )
                for h in range(heads):
                    scores = lax.dot_general(
                        q_ref[h, rows, :],
                        part[keys, :HD],
                        (((1,), (1,)), ((), ())),
                        preferred_element_type=jnp.float32,
                    )
                    scores = jnp.tanh(scores * (1.0 / SOFT_CAP))
                    weights = jnp.where(
                        allowed, jnp.exp2(scores * (SOFT_CAP * math.log2(math.e))), 0.0
                    )
                    total = weights[:, :LANES]
                    for c in range(1, k_tile // LANES):
                        total += weights[:, c * LANES : (c + 1) * LANES]
                    den[h, rows, :] += total
                    acc[h, rows, :] += jnp.dot(
                        weights.astype(jnp.bfloat16),
                        part[keys, HD:],
                        preferred_element_type=jnp.float32,
                    )

            return carry

        lax.fori_loop(0, q_tiles * here, step, 0)
        first += here


def middle_kernel(heads, q_tile, k_tile, count, touch_ref, q_ref, qseg_ref, qslot_ref, kseg_ref, kslot_ref, *rest):
    parts, (acc_in, den_in, acc, den) = rest[:count], rest[count:]
    acc[...] = acc_in[...]
    den[...] = den_in[...]
    fold_blocks(
        heads, q_tile, k_tile, touch_ref, q_ref, qseg_ref, qslot_ref, kseg_ref, kslot_ref, parts, acc, den
    )


def first_kernel(heads, q_tile, k_tile, count, touch_ref, q_ref, qseg_ref, qslot_ref, kseg_ref, kslot_ref, *rest):
    parts, (acc, den) = rest[:count], rest[count:]
    acc[...] = jnp.zeros_like(acc)
    den[...] = jnp.zeros_like(den)
    fold_blocks(
        heads, q_tile, k_tile, touch_ref, q_ref, qseg_ref, qslot_ref, kseg_ref, kslot_ref, parts, acc, den
    )


def last_kernel(heads, q_tile, k_tile, count, touch_ref, q_ref, qseg_ref, qslot_ref, kseg_ref, kslot_ref, *rest):
    parts, (acc_in, den_in, out_ref, acc, den) = rest[:count], rest[count:]
    acc[...] = acc_in[...]
    den[...] = den_in[...]
    fold_blocks(
        heads, q_tile, k_tile, touch_ref, q_ref, qseg_ref, qslot_ref, kseg_ref, kslot_ref, parts, acc, den
    )
    present = qseg_ref[...] >= 0
    for h in range(heads):
        total = jnp.sum(den[h], axis=-1, keepdims=True)
        safe = jnp.where(present, total, 1.0)
        out_ref[:, h * HD : (h + 1) * HD] = jnp.where(present, acc[h] / safe, 0.0).astype(
            out_ref.dtype
        )


def attend(queries, q_seg, q_slot, parts, ints, totals=None, last=False):
    heads, rows, _ = queries.shape
    k_seg = jnp.concatenate([pair[0] for pair in ints])
    k_slot = jnp.concatenate([pair[1] for pair in ints])
    q_tile = math.gcd(rows, 256)
    k_tile = math.gcd(*[part.shape[0] for part in parts], 512)
    blocks = k_seg.shape[0] // k_tile
    seg_tiles = q_seg.reshape(-1, q_tile)
    lowest = jnp.min(jnp.where(seg_tiles >= 0, seg_tiles, FAR), axis=1)[:, None]
    highest = jnp.max(seg_tiles, axis=1)[:, None]
    latest = jnp.max(q_slot.reshape(-1, q_tile), axis=1)[:, None]
    near = (k_seg[None] >= lowest) & (k_seg[None] <= highest) & (k_slot[None] <= latest)
    touch = jnp.max(near.astype(jnp.int32).reshape(-1, blocks, k_tile), axis=2).reshape(-1)
    operands = [
        touch,
        queries,
        q_seg[:, None],
        q_slot[:, None],
        k_seg.reshape(blocks, 1, k_tile),
        k_slot.reshape(blocks, 1, k_tile),
        *parts,
    ]
    vmem = pl.BlockSpec(memory_space=pltpu.VMEM)
    sums = [
        jax.ShapeDtypeStruct((heads, rows, HD), jnp.float32),
        jax.ShapeDtypeStruct((heads, rows, LANES), jnp.float32),
    ]
    body, out_shape, out_specs, scratch = first_kernel, sums, [vmem, vmem], []
    if totals is not None:
        operands += list(totals)
        body = middle_kernel
    if last:
        body = last_kernel
        out_shape = jax.ShapeDtypeStruct((rows, heads * HD), jnp.bfloat16)
        out_specs = vmem
        scratch = [pltpu.VMEM(s.shape, s.dtype) for s in sums]
    pairs = heads * rows * k_seg.shape[0]
    return pl.pallas_call(
        functools.partial(body, heads, q_tile, k_tile, len(parts)),
        in_specs=[pl.BlockSpec(memory_space=pltpu.SMEM)] + [vmem] * (len(operands) - 1),
        out_specs=out_specs,
        out_shape=out_shape,
        scratch_shapes=scratch,
        compiler_params=pltpu.CompilerParams(vmem_limit_bytes=VMEM_BYTES),
        cost_estimate=pl.CostEstimate(
            flops=4 * pairs * HD, bytes_accessed=4 * HD * k_seg.shape[0], transcendentals=2 * pairs
        ),
        name="attend",
    )(*operands)


MESH = pl.DeviceIdType.MESH
LOG2E = math.log2(math.e)


def block_kernel(
    tok_ref, small, table, wq_hbm, wkv_hbm, wo_hbm, cache_hbm,
    out_ref,
    tabs, line, freq, ig_ref, og_ref, xbuf, wq, wkv, wo, keys, kseg, qseg, cosine, sine, q2, acc, den, qfar, qsegf, pacc, pden, pay, dpay, dfar, abuf, ax, ay, wx, wy, sbuf, rbuf, hold,
    load_sem, int_s, int_r, ag_s, ag_r, cu_s, cu_r, cd_s, cd_r, cs_s, cs_r, ku_s, ku_r, ks_s, ks_r,
    qd_s, qd_r, pd_s, pd_r, w_s, w_r, at_s, at_r, rs_s, rs_r,
):
    s, h = lax.axis_index("seq"), lax.axis_index("head")
    n_seq = tabs.shape[0]
    chips = n_seq // 2
    z, core = s // 2, s % 2
    mate = s + 1 - 2 * core
    hx, hy, hd = h + 1 - 2 * (h % 2), (h + 2) % 4, 3 - h
    rel = (h, hx, hy, hd)
    rows = tok_ref.shape[0]
    shard = 4 * rows
    half = rows // 2
    wide = out_ref.shape[1] // 2
    crow = cache_hbm.shape[1]
    cbase = 6 * shard
    f32, bf16 = jnp.float32, jnp.bfloat16

    def remote(src, dst, send, recv, seq=None, head=None):
        device = {"seq": s if seq is None else seq, "head": h if head is None else head}
        return pltpu.make_async_remote_copy(
            src_ref=src, dst_ref=dst, send_sem=send, recv_sem=recv, device_id=device, device_id_type=MESH
        )

    barrier = pltpu.get_barrier_semaphore()
    peers = [lax.rem(s + d, n_seq) for d in range(1, n_seq)]
    for peer in peers:
        pl.semaphore_signal(barrier, inc=1, device_id={"seq": peer, "head": h}, device_id_type=MESH)
    for head in (hx, hy):
        pl.semaphore_signal(barrier, inc=1, device_id={"seq": s, "head": head}, device_id_type=MESH)

    kv_cols = pl.ds(pl.multiple_of(h * 2 * HD, 2 * HD), 2 * HD)
    own_cache = keys.at[pl.ds(pl.multiple_of(cbase + s * crow, crow), crow)]
    blocks = shard // LANES
    loads = [
        pltpu.make_async_copy(wkv_hbm.at[:, kv_cols], wkv, load_sem.at[0]),
        pltpu.make_async_copy(wq_hbm, wq, load_sem.at[1]),
        pltpu.make_async_copy(wo_hbm, wo, load_sem.at[2]),
        pltpu.make_async_copy(cache_hbm.at[h], own_cache, load_sem.at[3]),
    ]
    width = 2 * wide
    width = 2 * wide
    early = [
        pltpu.make_async_copy(
            table.at[pl.ds(i * LANES, LANES)],
            tabs.at[s, i] if i < blocks else line.at[i - blocks],
            load_sem.at[7 + i],
        )
        for i in range(blocks + 2)
    ] + [
        pltpu.make_async_copy(small.at[pl.ds(0, width)], ig_ref.at[0], load_sem.at[4]),
        pltpu.make_async_copy(small.at[pl.ds(width, width)], og_ref.at[0], load_sem.at[5]),
        pltpu.make_async_copy(small.at[pl.ds(2 * width, LANES)], freq.at[0], load_sem.at[6]),
    ]
    for load in early + loads:
        load.start()

    for load in early:
        load.wait()

    x = tok_ref[...].astype(f32)
    scale = lax.rsqrt(jnp.mean(x * x, axis=-1, keepdims=True) + EPSILON)
    xbuf[h] = (x * scale * ig_ref[...]).astype(bf16)

    pl.semaphore_wait(barrier, n_seq + 1)

    ints = [
        remote(tabs.at[s], tabs.at[s], int_s.at[d], int_r.at[d], seq=peers[d]) for d in range(n_seq - 1)
    ]
    top, bottom = pl.ds(0, half), pl.ds(half, half)

    def token_copy(m, block, part, head):
        ref = xbuf.at[block, part]
        return remote(ref, ref, ag_s.at[m], ag_r.at[m], head=head)

    gather = [
        token_copy(0, h, top, hx), token_copy(1, h, bottom, hx), token_copy(2, h, bottom, hy),
        token_copy(3, h, top, hy), token_copy(4, hx, top, hy), token_copy(5, hy, bottom, hx),
    ]
    gather_in = [
        token_copy(0, hx, top, hx), token_copy(1, hx, bottom, hx), token_copy(2, hy, bottom, hy),
        token_copy(3, hy, top, hy), token_copy(4, hd, top, hy), token_copy(5, hd, bottom, hx),
    ]

    def cache_ref(owner):
        return keys.at[pl.ds(pl.multiple_of(cbase + owner * crow, crow), crow)]

    def cache_up(k, owner):
        src = cache_hbm.at[h] if k == 0 else cache_ref(owner)
        return remote(src, cache_ref(owner), cu_s.at[k], cu_r.at[k], seq=s + 2)

    def cache_down(k, owner):
        src = cache_hbm.at[h] if k == 0 else cache_ref(owner)
        return remote(src, cache_ref(owner), cd_s.at[k], cd_r.at[k], seq=s - 2)

    def cache_side(i, owner):
        src = cache_hbm.at[h] if i == 0 else cache_ref(owner)
        return remote(src, cache_ref(owner), cs_s.at[i], cs_r.at[i], seq=mate)

    part_rows = wx.shape[0] // 2

    def weight_copy(m, c):
        span = pl.ds(pl.multiple_of(c * part_rows, part_rows), part_rows)
        there = (wx, wy)[m % 2].at[span]
        if m < 2:
            columns = pl.ds(m * wide, wide)
            return remote(wo_hbm.at[span, columns], there, w_s.at[m], w_r.at[m], head=(hx, hy)[m])
        return remote(there, there, w_s.at[m], w_r.at[m], seq=mate)

    last = chips - 1
    lane = lax.broadcasted_iota(jnp.int32, (1, LANES), 1)

    def column(row):
        return jnp.broadcast_to(row, (LANES, LANES)).T

    here = crow // BLK
    mine = lax.broadcasted_iota(jnp.int32, (here, LANES), 0) == lane - s * here
    owned = jnp.where(mine, column(line[:1, :])[:here], 0)
    tabs[s, blocks : blocks + 1, :] = jnp.sum(owned, axis=0, keepdims=True)
    for i in range(n_seq - 1):
        ints[i].start()


    for m in (0, 2, 1, 3):
        gather[m].start()

    @pl.when(z < last)
    def _():
        cache_up(0, s).start()

    @pl.when(z > 0)
    def _():
        cache_down(0, s).start()

    cache_side(0, s).start()

    acc[...] = jnp.zeros_like(acc)
    den[...] = jnp.zeros_like(den)
    for d in range(n_seq - 1):
        source = lax.rem(s + n_seq - 1 - d, n_seq)
        remote(tabs.at[source], tabs.at[source], int_s.at[d], int_r.at[d], seq=source).wait_recv()

    segs = lax.broadcasted_iota(jnp.int32, (NSEG, LANES), 0)
    count = jnp.zeros((NSEG, LANES), jnp.int32)
    owners = jnp.zeros((1, LANES), jnp.int32)
    for p in range(n_seq):
        for i in range(blocks):
            row = tabs[p, i : i + 1, :]
            count += jnp.where((row >= 0) & (row < segs), 1, 0)
        owners += tabs[p, blocks : blocks + 1, :]
    firsts = jnp.sum(count.astype(f32), axis=1, keepdims=True)
    lengths = column(line[1:2, :].astype(f32))[:NSEG, :1]
    base = lengths - firsts
    for i in range(blocks):
        row = tabs[s, i : i + 1, :]
        start = jnp.sum(jnp.where(segs == row, base, 0.0), axis=0, keepdims=True)
        place = start + (s * shard + i * LANES + lane).astype(f32)
        angle = column(place) * freq[:1, :]
        cosine[i] = jnp.cos(angle)
        sine[i] = jnp.sin(angle)
        qseg[i] = column(row)
        qsegf[i] = column(tabs[jnp.minimum(s + 1, n_seq - 1), i : i + 1, :])

    def spans(b):
        ahead = tabs[jnp.clip(2 * b, 0, n_seq - 2), 0:1, :][:, :1]
        behind = tabs[jnp.clip(2 * b - 4, 0, n_seq - 2), blocks - 1 : blocks, :][:, LANES - 1 :]
        return (ahead == behind) & (ahead >= 0)

    for dz in range(3):
        for c in range(2):
            source = jnp.maximum(z - dz, 0) * 2 + c
            for i in range(blocks):
                row = tabs[source, i : i + 1, :]
                at = (dz * 2 + c) * blocks + i
                hidden = (row < 0) | spans(z) if dz == 2 else row < 0
                kseg[at : at + 1, :] = jnp.where(hidden, -2, row)
    same = (column(owners) == owners) & (
        lax.broadcasted_iota(jnp.int32, (LANES, LANES), 0)
        < lax.broadcasted_iota(jnp.int32, (LANES, LANES), 1)
    )
    rank = jnp.sum(jnp.where(same, 1, 0), axis=0, keepdims=True)
    limit = jnp.sum(jnp.where(segs == owners, lengths, 0.0), axis=0, keepdims=True).astype(jnp.int32)
    filled = jnp.where(owners >= 0, jnp.clip(limit - BLK * rank, 0, BLK), 0)
    owner_col, filled_col = column(owners), column(filled)
    per = LANES // BLK
    pick = lax.broadcasted_iota(jnp.int32, (per, LANES), 0) == lane // BLK
    for i in range(n_seq * crow // LANES):
        part = slice(i * per, (i + 1) * per)
        who = jnp.sum(jnp.where(pick, owner_col[part], 0), axis=0, keepdims=True)
        many = jnp.sum(jnp.where(pick, filled_col[part], 0), axis=0, keepdims=True)
        at = 6 * blocks + i
        kseg[at : at + 1, :] = jnp.where(lane % BLK < many, who, -2)

    def kv_ref(dz, c, block):
        return keys.at[pl.ds(pl.multiple_of((dz * 2 + c) * shard + block * rows, rows), rows)]

    def kv_up(dz, r):
        return remote(
            kv_ref(dz, core, rel[r]), kv_ref(dz + 1, core, rel[r]), ku_s.at[dz, r], ku_r.at[dz, r], seq=s + 2
        )

    def kv_side(dz, r, c=None):
        ref = kv_ref(dz, core if c is None else c, rel[r])
        return remote(ref, ref, ks_s.at[dz, r], ks_r.at[dz, r], seq=mate)

    def project_kv(r):
        block = rel[r]
        y = jnp.dot(xbuf[block], wkv[...], preferred_element_type=f32)
        a, b = turn(y[:, :HD], cosine[block], sine[block], 1.0)
        at = pl.ds(pl.multiple_of(core * shard + block * rows, rows), rows)
        keys[at, : HD // 2] = a.astype(bf16)
        keys[at, HD // 2 : HD] = b.astype(bf16)
        keys[at, HD:] = y[:, HD:].astype(bf16)

        @pl.when(z < last)
        def _():
            kv_up(0, r).start()

        @pl.when(core == 0)
        def _():
            kv_side(0, r).start()

    def project_q(r):
        block = rel[r]
        y = jnp.dot(xbuf[block], wq[...], preferred_element_type=f32)
        for g in range(2):
            a, b = turn(y[:, g * HD : (g + 1) * HD], cosine[block], sine[block], HD**-0.5)
            q2[block, g * rows : (g + 1) * rows, : HD // 2] = a.astype(bf16)
            q2[block, g * rows : (g + 1) * rows, HD // 2 :] = b.astype(bf16)
        pl.when((z >= 2) & (core == 0))(lambda: query_down(r).start())

    def pass_cache(k):
        @pl.when(z >= k)
        def _():
            owner = s - 2 * k
            cache_up(k - 1, owner).wait_recv()

            if k < last:
                pl.when(z < last)(lambda: cache_up(k, owner).start())

            cache_side(k, owner).start()

        @pl.when(z + k <= last)
        def _():
            owner = s + 2 * k
            cache_down(k - 1, owner).wait_recv()

            if k < last:
                pl.when(z > 0)(lambda: cache_down(k, owner).start())

            cache_side(last + k, owner).start()

    def pass_kv(r):
        @pl.when(z >= 1)
        def _():
            kv_up(0, r).wait_recv()
            kv_side(1, r).start()

    def query_down(r):
        block = rel[r]
        return remote(q2.at[block], qfar.at[block], qd_s.at[r], qd_r.at[r], seq=s - 1)

    def far_rows(j):
        return pl.ds(j * rows, rows)

    def far_up(j):
        there = keys.at[pl.ds(5 * shard + j * rows, rows)]
        return remote(pay.at[far_rows(j)], there, ku_s.at[1, j], ku_r.at[1, j], seq=s + 2)

    def far_side(j):
        there = keys.at[pl.ds(5 * shard + j * rows, rows)]
        return remote(there, there, ks_s.at[2, j], ks_r.at[2, j], seq=mate)

    total_up = remote(dpay, dfar, pd_s.at[0], pd_r.at[0], seq=s + 2)
    total_side = remote(dfar, dfar, pd_s.at[1], pd_r.at[1], seq=mate)

    tile = shard

    def attend(j, at, causal=False, own=(q2, qseg, acc, den)):
        q2, qseg, acc, den = own
        span = pl.ds(pl.multiple_of(at * tile, tile), tile)
        scores = lax.dot_general(
            q2[j], keys[span, :HD], (((1,), (1,)), ((), ())), preferred_element_type=f32
        )
        columns = []
        total = [den[j, g * rows : (g + 1) * rows, :] for g in range(2)]
        for c in range(tile // LANES):
            allowed = qseg[j] == kseg[pl.ds(at * (tile // LANES) + c, 1), :]
            if causal:
                query = j * rows + lax.broadcasted_iota(jnp.int32, (rows, LANES), 0)
                allowed &= c * LANES + lax.broadcasted_iota(jnp.int32, (rows, LANES), 1) <= query
            pair = []
            for g in range(2):
                part = scores[g * rows : (g + 1) * rows, c * LANES : (c + 1) * LANES]
                part = jnp.exp2(jnp.tanh(part * (1.0 / SOFT_CAP)) * (SOFT_CAP * LOG2E))
                part = jnp.where(allowed, part, 0.0)
                total[g] += part
                pair.append(part.astype(bf16))
            columns.append(jnp.concatenate(pair, axis=0))
        for g in range(2):
            den[j, g * rows : (g + 1) * rows, :] = total[g]
        weights = jnp.concatenate(columns, axis=1)
        acc[j] += jnp.dot(weights, keys[span, HD:], preferred_element_type=f32)

    def attend_all(at, causal=False, own=(q2, qseg, acc, den)):
        def body(j, carry):
            attend(j, at, causal, own)
            return carry

        lax.fori_loop(0, 4, body, 0, unroll=4)

    def attend_cache(other):
        attend_all(6 + other)

    loads[0].wait()
    project_kv(0)
    loads[1].wait()
    project_q(0)
    pass_cache(1)
    pass_kv(0)
    gather_in[0].wait_recv()
    gather[4].start()
    gather_in[2].wait_recv()
    gather[5].start()
    weight_copy(0, core).start()
    weight_copy(1, core).start()
    gather_in[1].wait_recv()
    project_kv(1)
    gather_in[3].wait_recv()
    project_kv(2)
    pass_cache(2)
    project_q(1)
    project_q(2)
    gather_in[4].wait_recv()
    gather_in[5].wait_recv()
    project_kv(3)
    project_q(3)
    pass_kv(1)
    attend_all(core, True)
    pass_kv(2)
    loads[3].wait()
    cache_side(0, mate).wait_recv()
    attend_cache(z)

    def cache_tiles(k):
        @pl.when(z >= k)
        def _():
            cache_side(k, mate - 2 * k).wait_recv()
            attend_cache(z - k)

        @pl.when(z + k <= last)
        def _():
            cache_side(last + k, mate + 2 * k).wait_recv()
            attend_cache(z + k)

    pass_kv(3)

    @pl.when(z >= 1)
    def _():
        for r in range(4):
            kv_side(1, r, 1 - core).wait_recv()

    @pl.when((z >= 1) & (z < last) & (core == 1))
    def _():
        pacc[...] = jnp.zeros_like(pacc)
        pden[...] = jnp.zeros_like(pden)
        for r in range(4):
            query_down(r).wait_recv()
        own = (qfar, qsegf, pacc, pden)
        attend_all(2, own=own)
        attend_all(3, own=own)
        flag = spans(z + 1)
        for j in range(4):
            for g in range(2):
                part = pl.ds(g * rows, rows)
                total = jnp.sum(pden[j, part, :], axis=-1, keepdims=True)
                dpay[2 * j + g : 2 * j + g + 1, :] = jnp.broadcast_to(total, (rows, LANES)).T[:1]
                columns = pl.ds(g * HD, HD)
                kept = keys[pl.ds(3 * shard + j * rows, rows), columns]
                pay[far_rows(j), columns] = jnp.where(flag, pacc[j, part, :].astype(bf16), kept)
            far_up(j).start()
        total_up.start()

    cache_tiles(1)
    pass_cache(3)

    @pl.when(core == 1)
    def _():
        for r in range(4):
            kv_side(0, r, 0).wait_recv()
        attend_all(0)

    cache_tiles(2)

    @pl.when(z >= 1)
    def _():
        attend_all(2)
        attend_all(3)

    cache_tiles(3)

    @pl.when((z >= 2) & (core == 1))
    def _():
        for j in range(4):
            far_up(j).wait_recv()
            far_side(j).start()
        total_up.wait_recv()
        total_side.start()

    for m in range(2):
        weight_copy(m, core).wait_recv()
        weight_copy(m + 2, core).start()
    loads[2].wait()

    @pl.when((z >= 2) & (core == 0))
    def _():
        for j in range(4):
            far_side(j).wait_recv()
        total_side.wait_recv()

    def attended(j):
        present = qseg[j] >= 0
        present = present[:, :1]
        parts = []
        for g in range(2):
            total = jnp.sum(den[j, g * rows : (g + 1) * rows, :], axis=-1, keepdims=True)
            safe = jnp.where(present, total, 1.0)
            value = acc[j, g * rows : (g + 1) * rows, :] / safe
            parts.append(jnp.where(present, value, 0.0).astype(bf16))
        return jnp.concatenate(parts, axis=1)

    def finish(j):
        @pl.when(z >= 2)
        def _():
            attend(j, 5)

            @pl.when(core == 0)
            def _():
                flag = spans(z)
                at = pl.ds(pl.multiple_of(5 * shard + j * rows, rows), rows)
                for g in range(2):
                    part = pl.ds(g * rows, rows)
                    more = keys[at, g * HD : (g + 1) * HD].astype(f32)
                    acc[j, part, :] += jnp.where(flag, more, 0.0)
                    total = column(dfar[pl.ds(2 * j + g, 1), :])
                    den[j, part, :] += jnp.where(flag & (lane == 0), total, 0.0)

        abuf[j] = attended(j)

    def rows_copy(m, block):
        there = (ax, ay)[m % 2].at[m // 2]
        return remote(abuf.at[block], there, at_s.at[m], at_r.at[m], head=(hx, hy)[m % 2])

    def sum_copy(m):
        return remote(sbuf.at[m], rbuf.at[m], rs_s.at[m], rs_r.at[m], head=(hy, hx)[m])

    def left(a, weight=None):
        return jnp.dot(a, wo[:, :wide] if weight is None else weight[...], preferred_element_type=f32)

    def right(a, weight=None):
        return jnp.dot(a, wo[:, wide:] if weight is None else weight[...], preferred_element_type=f32)

    sent = (hd, hd, hx, hy)
    finish(hd)
    rows_copy(0, hd).start()
    rows_copy(1, hd).start()
    finish(hx)
    rows_copy(2, hx).start()
    finish(hy)
    rows_copy(3, hy).start()
    for m in range(2):
        weight_copy(m + 2, 1 - core).wait_recv()
    rows_copy(0, hd).wait_recv()
    sbuf[0] = (left(abuf[hy]) + left(ax[0], wx)).astype(bf16)
    sum_copy(0).start()
    rows_copy(1, hd).wait_recv()
    sbuf[1] = (right(abuf[hx]) + right(ay[0], wy)).astype(bf16)
    sum_copy(1).start()
    finish(h)
    hold[0] = left(abuf[h])
    hold[1] = right(abuf[h])
    rows_copy(2, hx).wait_recv()
    hold[0] += left(ax[1], wx)
    rows_copy(3, hy).wait_recv()
    hold[1] += right(ay[1], wy)
    sum_copy(0).wait_recv()
    branch_l = hold[0] + rbuf[0].astype(f32)
    sum_copy(1).wait_recv()
    branch_r = hold[1] + rbuf[1].astype(f32)
    square = jnp.sum(branch_l * branch_l, axis=-1, keepdims=True) + jnp.sum(
        branch_r * branch_r, axis=-1, keepdims=True
    )
    scale = lax.rsqrt(square / (2 * wide) + EPSILON)
    out_ref[:, :wide] = (
        tok_ref[:, :wide].astype(f32) + branch_l * scale * og_ref[:, :wide]
    ).astype(bf16)
    out_ref[:, wide:] = (
        tok_ref[:, wide:].astype(f32) + branch_r * scale * og_ref[:, wide:]
    ).astype(bf16)

    for i in range(n_seq - 1):
        ints[i].wait_send()
    for copy in gather:
        copy.wait_send()
    for m in range(4):
        rows_copy(m, sent[m]).wait_send()
        weight_copy(m, core).wait_send()
    for m in range(2):
        sum_copy(m).wait_send()
    cache_side(0, s).wait_send()
    for k in range(chips - 1):
        @pl.when((z < last) & (z >= k))
        def _():
            cache_up(k, s - 2 * k).wait_send()

        @pl.when((z > 0) & (z + k <= last))
        def _():
            cache_down(k, s + 2 * k).wait_send()

    for k in range(1, chips):
        @pl.when(z >= k)
        def _():
            cache_side(k, s - 2 * k).wait_send()

        @pl.when(z + k <= last)
        def _():
            cache_side(last + k, s + 2 * k).wait_send()

    for r in range(4):
        @pl.when(z < last)
        def _():
            kv_up(0, r).wait_send()

        @pl.when(core == 0)
        def _():
            kv_side(0, r).wait_send()

        @pl.when(z >= 1)
        def _():
            kv_side(1, r).wait_send()

        @pl.when((z >= 2) & (core == 0))
        def _():
            query_down(r).wait_send()

        @pl.when((z >= 1) & (z < last) & (core == 1))
        def _():
            far_up(r).wait_send()

        @pl.when((z >= 2) & (core == 1))
        def _():
            far_side(r).wait_send()

    @pl.when((z >= 1) & (z < last) & (core == 1))
    def _():
        total_up.wait_send()

    @pl.when((z >= 2) & (core == 1))
    def _():
        total_side.wait_send()


def whole_block(
    tokens, in_gain, out_gain, query_weight, keyval_weight, out_weight, cache_entries, segment_ids,
    cache_lengths, block_owners,
):
    n_seq = lax.axis_size("seq")
    rows, width = tokens.shape
    shard = segment_ids.shape[0]
    crow = cache_entries.shape[1]
    n_keys = 6 * shard + n_seq * crow
    angle = (10000.0 ** (-np.arange(HD // 2) * 2.0 / HD)).astype(np.float32)
    vmem, hbm = pl.BlockSpec(memory_space=pltpu.VMEM), pl.BlockSpec(memory_space=pl.ANY)
    f32, bf16, i32 = jnp.float32, jnp.bfloat16, jnp.int32
    dma = pltpu.SemaphoreType.DMA
    hops = n_seq // 2 - 1
    pairs = [dma((n,)) for n in (n_seq - 1, 6, hops, hops, 2 * hops + 1) for _ in range(2)]

    def pack(parts):
        ends = np.cumsum([-(-x.shape[0] // LANES) * LANES for x in parts]).tolist()
        starts = [0] + ends[:-1]
        return sum(jnp.pad(x, (at, ends[-1] - at - x.shape[0])) for x, at in zip(parts, starts))

    small = pack((in_gain, out_gain, jnp.asarray(angle)))
    table = pack((segment_ids, block_owners, cache_lengths))
    return pl.pallas_call(
        block_kernel,
        out_shape=jax.ShapeDtypeStruct((rows, width), bf16),
        in_specs=[vmem] + [hbm] * 6,
        out_specs=vmem,
        scratch_shapes=[
            pltpu.VMEM((n_seq, 8 * -(-(shard // LANES + 1) // 8), LANES), i32),
            pltpu.VMEM((8, LANES), i32),
            pltpu.VMEM((8, LANES), f32),
            pltpu.VMEM((1, width), f32),
            pltpu.VMEM((1, width), f32),
            pltpu.VMEM((4, rows, width), bf16),
            pltpu.VMEM((width, 2 * HD), bf16),
            pltpu.VMEM((width, 2 * HD), bf16),
            pltpu.VMEM((2 * HD, width), bf16),
            pltpu.VMEM((n_keys, 2 * HD), bf16),
            pltpu.VMEM((n_keys // LANES, LANES), i32),
            pltpu.VMEM((4, rows, LANES), i32),
            pltpu.VMEM((4, rows, LANES), f32),
            pltpu.VMEM((4, rows, LANES), f32),
            pltpu.VMEM((4, 2 * rows, HD), bf16),
            pltpu.VMEM((4, 2 * rows, HD), f32),
            pltpu.VMEM((4, 2 * rows, LANES), f32),
            pltpu.VMEM((4, 2 * rows, HD), bf16),
            pltpu.VMEM((4, rows, LANES), i32),
            pltpu.VMEM((4, 2 * rows, HD), f32),
            pltpu.VMEM((4, 2 * rows, LANES), f32),
            pltpu.VMEM((shard, 2 * HD), bf16),
            pltpu.VMEM((8, LANES), f32),
            pltpu.VMEM((8, LANES), f32),
            pltpu.VMEM((4, rows, 2 * HD), bf16),
            pltpu.VMEM((2, rows, 2 * HD), bf16),
            pltpu.VMEM((2, rows, 2 * HD), bf16),
            pltpu.VMEM((2 * HD, width // 2), bf16),
            pltpu.VMEM((2 * HD, width // 2), bf16),
            pltpu.VMEM((2, rows, width // 2), bf16),
            pltpu.VMEM((2, rows, width // 2), bf16),
            pltpu.VMEM((2, rows, width // 2), f32),
            dma((9 + shard // LANES,)),
            *pairs,
            dma((2, 4)), dma((2, 4)), dma((3, 4)), dma((3, 4)),
            dma((4,)), dma((4,)), dma((2,)), dma((2,)),
            dma((4,)), dma((4,)), dma((4,)), dma((4,)), dma((2,)), dma((2,)),
        ],
        compiler_params=pltpu.CompilerParams(
            collective_id=0, has_side_effects=True, vmem_limit_bytes=52 << 20
        ),
        cost_estimate=pl.CostEstimate(
            flops=2 * shard * (6 * HD * width + 8 * n_keys * HD // 4),
            bytes_accessed=6 * HD * 2 * width,
            transcendentals=4 * shard * n_keys,
        ),
        name="block",
    )(
        tokens, small, table, query_weight, keyval_weight, out_weight, cache_entries,
    )


def local(
    tokens,
    in_gain,
    out_gain,
    query_weight,
    keyval_weight,
    out_weight,
    cache_entries,
    segment_ids,
    cache_lengths,
    block_owners,
):
    heads_here = query_weight.shape[1] // HD
    group_size = QH // KVH
    seq_size, head_size = lax.axis_size("seq"), lax.axis_size("head")
    seq_index = lax.axis_index("seq")
    head_index = lax.axis_index("head")
    shared_head = head_index * heads_here // group_size
    stream_rows = segment_ids.shape[0]
    normed_own = rms_scale(tokens, in_gain).astype(jnp.bfloat16)
    chunks = [[lax.all_gather(normed_own, "head", axis=0, tiled=True)]]

    cache_own = lax.dynamic_index_in_dim(cache_entries, shared_head, 0, keepdims=False)
    cache_pairs = lax.all_gather(cache_own, "seq", axis=0, tiled=True)

    table = jnp.concatenate([segment_ids, block_owners])[None]
    bits = 0
    while 1 << bits < seq_size:
        step = 1 << bits
        other = lax.ppermute(table, "seq", [(s, s ^ step) for s in range(seq_size)])
        table = jnp.concatenate([table, other], axis=0)
        bits += 1
    for bit in range(bits):
        pieces = table.reshape(-1, 2, 1 << bit, table.shape[-1])
        pieces = jnp.where((seq_index >> bit) % 2 == 1, pieces[:, ::-1], pieces)
        table = pieces.reshape(seq_size, -1)
    seg_all = table[:, :stream_rows].reshape(-1)
    owners = table[:, stream_rows:].reshape(-1)

    seg_range = jnp.arange(NSEG, dtype=jnp.int32)
    earlier = (seg_all[None, :] >= 0) & (seg_all[None, :] < seg_range[:, None])
    firsts = jnp.sum(earlier.astype(jnp.int32), axis=1)
    slots_all = jnp.arange(seg_all.shape[0], dtype=jnp.int32)
    begin = seq_index * stream_rows
    q_seg = lax.dynamic_slice_in_dim(seg_all, begin, stream_rows)
    q_slot = lax.dynamic_slice_in_dim(slots_all, begin, stream_rows)
    matches = (q_seg[:, None] == seg_range[None, :]).astype(jnp.int32)
    positions = jnp.sum(matches * (cache_lengths - firsts)[None, :], axis=1) + q_slot
    angles = positions.astype(jnp.float32)[:, None] * frequencies(HD)[None, :]
    cosine, sine = jnp.cos(angles), jnp.sin(angles)

    block_index = jnp.arange(owners.shape[0], dtype=jnp.int32)
    same = (owners[:, None] == owners[None, :]) & (block_index[None, :] < block_index[:, None])
    block_rank = jnp.sum(same.astype(jnp.int32), axis=1)
    owner_match = (owners[:, None] == seg_range[None, :]).astype(jnp.int32)
    limits = jnp.sum(owner_match * cache_lengths[None, :], axis=1)
    offsets = jnp.arange(BLK, dtype=jnp.int32)
    usable = (owners[:, None] >= 0) & (
        block_rank[:, None] * BLK + offsets[None, :] < limits[:, None]
    )
    cache_seg = jnp.where(usable, owners[:, None], -2).reshape(-1)
    cache_slot = jnp.full((cache_seg.shape[0],), -1, jnp.int32)

    chunk_rows = stream_rows // len(chunks)
    pairs = []
    for at, parts in enumerate(chunks):
        rows = slice(at * chunk_rows, (at + 1) * chunk_rows)
        pairs.append(
            project(
                keyval_kernel, parts, keyval_weight, 2 * HD, shared_head,
                cosine[rows], sine[rows], (chunk_rows, 2 * HD),
            )
        )
    queries = project(
        query_kernel, sum(chunks, []), query_weight, heads_here * HD, jnp.int32(0),
        cosine, sine, (heads_here, stream_rows, HD),
    )

    hops = seq_size // 4

    def onward(array):
        return lax.ppermute(array, "seq", [(s, s + 2) for s in range(seq_size - 2)])

    def sibling(array):
        return lax.ppermute(array, "seq", [(s, s ^ 1) for s in range(seq_size)])

    key_seg = jnp.where(seg_all >= 0, seg_all, -2)

    def shard_ints(shard):
        inside = (shard >= 0) & (shard < seq_size)
        at = jnp.clip(shard, 0, seq_size - 1) * stream_rows
        seg = lax.dynamic_slice_in_dim(key_seg, at, stream_rows)
        return jnp.where(inside, seg, -2), lax.dynamic_slice_in_dim(slots_all, at, stream_rows)

    mate = seq_index + 1 - 2 * (seq_index % 2)
    travelling = [onward(pair) for pair in pairs]
    waiting, waiting_ints = [sibling(pair) for pair in pairs], [shard_ints(mate)]
    totals = attend(
        queries, q_seg, q_slot, pairs + [cache_pairs], [shard_ints(seq_index), (cache_seg, cache_slot)]
    )
    for hop in range(1, hops + 1):
        travelling, totals = lax.optimization_barrier((travelling, totals))
        following = [onward(pair) for pair in travelling] if hop < hops else []
        beside = [sibling(pair) for pair in travelling]
        parts = waiting + travelling
        ints = waiting_ints + [shard_ints(seq_index - 2 * hop)]
        waiting, waiting_ints = beside, [shard_ints(mate - 2 * hop)]
        if hop < hops:
            totals = attend(queries, q_seg, q_slot, parts, ints, totals)
        else:
            attended = attend(
                queries, q_seg, q_slot, parts + waiting, ints + waiting_ints, totals, last=True
            )
        travelling = following

    branch = lax.psum_scatter(
        jnp.dot(attended, out_weight, preferred_element_type=jnp.float32),
        "head",
        scatter_dimension=0,
        tiled=True,
    )
    return (tokens.astype(jnp.float32) + rms_scale(branch, out_gain)).astype(jnp.bfloat16)


def solution(mesh):
    in_specs = (
        P(("seq", "head"), None),
        P(),
        P(),
        P(None, "head"),
        P(),
        P("head", None),
        P(None, "seq", None),
        P("seq"),
        P(),
        P("seq"),
    )
    out_specs = P(("seq", "head"), None)
    fits = mesh.shape["seq"] == 8 and mesh.shape["head"] == 4
    body = whole_block if fits else local
    return jax.shard_map(body, mesh=mesh, in_specs=in_specs, out_specs=out_specs, check_vma=False)
```
